32 devices in a mesh: vocab: 4 (over z), expert: 8 (over y, x, core).
Axes of the slice: x: 2, y: 2, z: 4, core: 2. Of those that a mesh axis runs over, the one named last changes fastest.
Arguments:
- token_ids: int32 [1024], replicated, may hold values from 0 to 75967
- word_mask: int32 [75968], P('vocab'), may hold values 0 or 1
- embed_table: bfloat16 [75968, 4096], P('vocab', 'expert'), may hold values from -6 to 6
- attn_out: bfloat16 [1024, 4096], P('expert', 'vocab'), may hold values from -6 to 6
- in_gain: float32 [4096], replicated, may hold values from 0.25 to 1.75
- key_weight: bfloat16 [4096, 512], P(None, 'vocab'), may hold values from -0.09375 to 0.09375
- key_gain: float32 [128], replicated, may hold values from 0.25 to 1.75
- post_gain: float32 [4096], replicated, may hold values from 0.25 to 1.75
- routes: int32 [1024, 8], P('expert'), may hold values from 0 to 15, all different within a row; in each aligned block of 128 rows (0 to 127, 128 to 255, ...) at most 96 rows name the same one
- gate_ints: int32 [1024, 8], P('expert'), may hold values from 1 to 63
- w_gate: bfloat16 [32, 4096, 768], P(('expert', 'vocab')), may hold values from -0.09375 to 0.09375
- w_up: bfloat16 [32, 4096, 768], P(('expert', 'vocab')), may hold values from -0.09375 to 0.09375
- w_down: bfloat16 [32, 768, 4096], P(('expert', 'vocab')), may hold values from -0.15625 to 0.15625
Outputs:
- expert_out: bfloat16 [1024, 4096], P('expert', 'vocab')
- key_heads: bfloat16 [1024, 512], P('expert', 'vocab')
The draws below stay inside these ranges and needn't reach their ends.
Inputs may be any that keep to these rules, and one draw needn't show every extreme that they name: `routes`: each row names 8 different experts; within the 128 rows of one index of expert no expert is named by more than 96 rows, and in some such blocks one is named by exactly 96.
All inputs are finite; a program needn't handle non-finite values. No bound on the sum of `word_mask` on one device may be relied on, other than what follows from the above.
Results may differ from the reference program's by a relative error of at most 0.008.
Values may be sent and summed in bfloat16 or wider, within the bound.
A program may use at most 192 MiB of HBM per device.

```python
import math
import jax
import jax.numpy as jnp
import numpy as np
from jax import lax

D = 4096
FF = 1536
VOCAB = 75968
HD = 128
KVH = 4
TOPK = 8
TOK_DEV = 128
TOKENS = 1024
EXPERTS = 16
CAP = 96
N_EXPERT = 8


def with_ends(drawn, key, low, high):
    place = [jax.random.randint(jax.random.fold_in(key, axis), (), 0, length) for axis, length in enumerate(drawn.shape)]
    widest = drawn.shape.index(max(drawn.shape))
    next_to = place[:widest] + [(place[widest] + 1) % drawn.shape[widest]] + place[widest + 1:]
    return drawn.at[tuple(place)].set(low).at[tuple(next_to)].set(high)


def steps_of(own_key, dims, cuts, least, largest):
    loudness, own = 1.0, jax.random.fold_in(own_key, 6)
    for axis_at, parts in cuts:
        heights = jnp.exp(jax.random.uniform(jax.random.fold_in(own, axis_at), (parts,), jnp.float32, least / len(cuts), largest / len(cuts)))
        loudness = loudness * jnp.repeat(heights, dims[axis_at] // parts).reshape([-1 if axis == axis_at else 1 for axis in range(len(dims))])
    return loudness


def ranked_wide(key, extent, count, slope):
    weights = [min(1 << octave, count + 1 - (1 << octave)) * (1 << 20) // math.isqrt((1 << octave) ** slope) + 1 for octave in range((count + 1).bit_length()) if 1 << octave <= count]
    deviation = 1 + sum(weights) // (1 << 30)
    table = np.cumsum(np.array([max(1, weight // deviation) for weight in weights]))
    ticket = jax.random.randint(jax.random.fold_in(key, 1), extent, 0, int(table[len(weights) - 1]))
    start = jnp.left_shift(1, jnp.searchsorted(jnp.asarray(table, jnp.int32), ticket, side="right").astype(jnp.int32))
    rank = start - 1 + jax.random.randint(jax.random.fold_in(key, 4), extent, 0, 1 << 30) % jnp.minimum(start, count + 1 - start)
    return jax.random.permutation(jax.random.fold_in(key, 2), count)[rank].astype(jnp.int32)


def assign_block(own_key, own, number, rows, count, top, limit, skew):
    sequence = jax.random.permutation(own_key, count)
    crowded, usual = load_shares(count, rows * top, limit, skew, True), load_shares(count, rows * top, limit, skew, False)
    places = jnp.arange(count)

    def named(sizes, rotation):
        used = int((sizes > 0).sum())
        fixed = max(1, used // 4)
        passed = fixed + (places - fixed + rotation * (used - fixed)) % max(1, count - fixed)
        return jnp.zeros((count,), jnp.int32).at[sequence[jnp.where(places < fixed, places, passed)]].set(jnp.asarray(sizes, jnp.int32))

    sizes = jnp.where(number % 4 == 0, named(crowded, number // 4), named(usual, number - number // 4 - 1))
    mixed = jax.random.permutation(jax.random.fold_in(own, 3), count)
    giver, sink = mixed[0:count // 2 * 2:2], mixed[1:count // 2 * 2:2]
    room = jnp.minimum(sizes[giver] - 1, limit - sizes[sink]) // 2
    room = jnp.where((giver == sequence[0]) | (sink == sequence[0]) | (sizes[sink] == 0), 0, jnp.maximum(room, 0))
    passed = jax.random.randint(jax.random.fold_in(own, 4), (count // 2,), 0, 1 << 20) % (room + 1)
    sizes = sizes.at[giver].add(-passed).at[sink].add(passed)
    labels = jnp.searchsorted(jnp.cumsum(sizes), jnp.arange(rows * top), side="right").astype(jnp.int32)
    grid = labels.reshape(top, rows).T
    grid = grid[jax.random.permutation(jax.random.fold_in(own, 1), rows)]
    rotation = jax.random.randint(jax.random.fold_in(own, 2), (rows, 1), 0, top)
    return jnp.take_along_axis(grid, (jnp.arange(top)[None, :] + rotation) % top, axis=1)


def load_shares(amount, total, reach, slope, full):
    portions = [(1 << 20) // math.isqrt(rank ** slope) + 1 for rank in range(1, amount + 1)]
    largest = reach if full else min(reach, max(-(-total // amount), total * portions[0] // sum(portions)))
    least = 1 if total - largest >= amount - 1 else 0
    counts, rest = [largest] + [least] * (amount - 1), total - largest - least * (amount - 1)
    while rest > 0:
        candidates = [i for i in range(1, amount) if counts[i] < largest] or [i for i in range(1, amount) if counts[i] < reach]
        pool, left = sum([portions[i] for i in candidates]), rest
        for i in candidates:
            extra = min(reach - counts[i], max(1, left * portions[i] // pool), rest)
            counts[i] = counts[i] + extra
            rest = rest - extra
    return np.array(counts)


def noise(own_key, extent, deviation, reach, pieces=(), kind=jnp.bfloat16):
    loudness = steps_of(own_key, extent, pieces, -0.22, 0.18) if pieces else 1.0
    array = jax.random.normal(own_key, extent, jnp.float32) * deviation * loudness
    return jnp.minimum(jnp.maximum(array, -reach), reach).astype(kind)


def setup_inputs(seed: int = 0) -> dict:
    arg_keys = jax.random.split(jax.random.key(seed), 14)
    token_ids = with_ends(ranked_wide(arg_keys[0], (TOKENS,), VOCAB, 2), jax.random.fold_in(arg_keys[0], 3), 0, VOCAB - 1).astype(jnp.int32)
    word_mask = with_ends((jax.random.randint(arg_keys[1], (VOCAB,), 0, 4) < 3).astype(jnp.int32), jax.random.fold_in(arg_keys[1], 1), 0, 1)
    embed_table = noise(arg_keys[2], (VOCAB, D), 1.0, 6.0, ((0, 4), (1, 8)))
    attn_out = noise(arg_keys[3], (TOKENS, D), 1.0, 6.0, ((0, 8), (1, 4)))
    in_gain = jnp.clip(1.0 + 0.15 * jax.random.normal(arg_keys[4], (D,), jnp.float32), 0.25, 1.75)
    key_weight = noise(arg_keys[5], (D, KVH * HD), D ** -0.5, 0.09375, ((1, 4),))
    key_gain = jnp.clip(1.0 + 0.15 * jax.random.normal(arg_keys[6], (HD,), jnp.float32), 0.25, 1.75)
    post_gain = jnp.clip(1.0 + 0.15 * jax.random.normal(arg_keys[7], (D,), jnp.float32), 0.25, 1.75)
    routes_keys = jax.random.split(jax.random.fold_in(arg_keys[8], 1), TOKENS // TOK_DEV)
    routes_turns = jax.random.permutation(jax.random.fold_in(arg_keys[8], 3), TOKENS // TOK_DEV)
    routes = jax.vmap(lambda own, number: assign_block(jax.random.fold_in(arg_keys[8], 2), own, number, TOK_DEV, EXPERTS, TOPK, CAP, 2))(routes_keys, routes_turns).reshape((TOKENS, TOPK))
    gate_ints = with_ends(jax.random.randint(arg_keys[9], (TOKENS, TOPK), 1, 64), jax.random.fold_in(arg_keys[9], 1), 1, 63).astype(jnp.int32)
    w_gate = noise(arg_keys[10], (2 * EXPERTS, D, FF // 2), D ** -0.5, 0.09375, ((0, 32),))
    w_up = noise(arg_keys[11], (2 * EXPERTS, D, FF // 2), D ** -0.5, 0.09375, ((0, 32),))
    w_down = noise(arg_keys[12], (2 * EXPERTS, FF // 2, D), FF ** -0.5, 0.15625, ((0, 32),))
    return dict(token_ids=token_ids, word_mask=word_mask, embed_table=embed_table, attn_out=attn_out, in_gain=in_gain, key_weight=key_weight, key_gain=key_gain, post_gain=post_gain, routes=routes, gate_ints=gate_ints, w_gate=w_gate, w_up=w_up, w_down=w_down)


def rms_rows(values, scale_gain):
    inverse_rms = lax.rsqrt(lax.optimization_barrier(jnp.mean(values * values, axis=-1, keepdims=True)) + 1e-06)
    return values * inverse_rms * scale_gain

def reference(token_ids, word_mask, embed_table, attn_out, in_gain, key_weight, key_gain, post_gain, routes, gate_ints, w_gate, w_up, w_down):
    keep_row = word_mask[token_ids] == 1
    embedded = jnp.where(keep_row[:, None], embed_table[token_ids], jnp.zeros_like(embed_table[:1]))
    normed = rms_rows(embedded.astype(jnp.float32), in_gain).astype(jnp.bfloat16)
    raw_keys = jnp.dot(normed, key_weight, preferred_element_type=jnp.float32)
    head_view = raw_keys.reshape(TOKENS, KVH, HD)
    key_heads = rms_rows(head_view, key_gain).astype(jnp.bfloat16).reshape(TOKENS, KVH * HD)
    mid_stream = (embedded.astype(jnp.float32) + attn_out.astype(jnp.float32)).astype(jnp.bfloat16)
    expert_in = rms_rows(mid_stream.astype(jnp.float32), post_gain).astype(jnp.bfloat16)
    gate_share = gate_ints.astype(jnp.float32) / lax.optimization_barrier(jnp.sum(gate_ints, axis=1, keepdims=True)).astype(jnp.float32)
    blocks = routes.reshape(N_EXPERT, TOK_DEV * TOPK).astype(jnp.int32)
    onehot = (blocks[:, :, None] == jnp.arange(EXPERTS, dtype=jnp.int32)[None, None, :]).astype(jnp.int32)
    slot_rank = lax.optimization_barrier(jnp.sum((jnp.cumsum(onehot, axis=1).astype(jnp.int32) - onehot) * onehot, axis=2)).astype(jnp.int32)
    block_ids = jnp.arange(N_EXPERT, dtype=jnp.int32)[:, None]
    assign_ids = jnp.arange(TOK_DEV * TOPK, dtype=jnp.int32)[None, :]
    token_of = (block_ids * TOK_DEV + assign_ids // TOPK).astype(jnp.int32)
    slot_index = ((blocks * N_EXPERT + block_ids) * CAP + slot_rank).astype(jnp.int32)
    slot_token = jnp.full((EXPERTS * N_EXPERT * CAP,), TOKENS, jnp.int32).at[slot_index.reshape(-1)].set(token_of.reshape(-1))
    slot_gate = jnp.zeros((EXPERTS * N_EXPERT * CAP,), jnp.float32).at[slot_index.reshape(-1)].set(gate_share.reshape(-1))
    padded_in = jnp.concatenate([expert_in, jnp.zeros((1, D), expert_in.dtype)], axis=0)

    def one_expert(expert, running):
        token_list = lax.dynamic_slice_in_dim(slot_token, expert * N_EXPERT * CAP, N_EXPERT * CAP)
        gate_list = lax.dynamic_slice_in_dim(slot_gate, expert * N_EXPERT * CAP, N_EXPERT * CAP)
        row_block = padded_in[jnp.clip(token_list, 0, TOKENS)]
        summed_parts = jnp.zeros((N_EXPERT * CAP, D), jnp.float32)
        for part_idx in range(2):
            entry_idx = 2 * expert + part_idx
            gate_mat = lax.dynamic_index_in_dim(w_gate, entry_idx, 0, keepdims=False)
            up_mat = lax.dynamic_index_in_dim(w_up, entry_idx, 0, keepdims=False)
            down_mat = lax.dynamic_index_in_dim(w_down, entry_idx, 0, keepdims=False)
            gate_val = jnp.dot(row_block, gate_mat, preferred_element_type=jnp.float32)
            up_val = jnp.dot(row_block, up_mat, preferred_element_type=jnp.float32)
            hidden = (jax.nn.silu(gate_val) * up_val).astype(jnp.bfloat16)
            summed_parts = summed_parts + jnp.dot(hidden, down_mat, preferred_element_type=jnp.float32)
        part_rows = lax.optimization_barrier(summed_parts.astype(jnp.bfloat16)).astype(jnp.float32)
        return running.at[token_list].add(gate_list[:, None] * part_rows, mode='drop')
    running = lax.fori_loop(0, EXPERTS, one_expert, jnp.zeros((TOKENS, D), jnp.float32))
    return (running.astype(jnp.bfloat16), key_heads)
```

```python
import jax
import jax.numpy as jnp
from jax import lax
from jax.experimental import pallas as pl
from jax.experimental.pallas import tpu as pltpu
from jax.sharding import PartitionSpec as P

MESH = pl.DeviceIdType.MESH
GROUP = 16
CHAIN_LAG, RISE_LAG, CROSS_LAG, DIAG_LAG, SIB_LAG = 3, 1, 1, 1, 1


def rms_rows(values, scale_gain):
    inverse_rms = lax.rsqrt(jnp.mean(values * values, axis=-1, keepdims=True) + 1e-06)
    return values * inverse_rms * scale_gain


def where_am_i():
    me = lax.axis_index("expert")
    z = lax.axis_index("vocab")
    return me, z, me % 2, me // 2


def greet_all(n_vocab, n_expert, me, z):
    barrier = pltpu.get_barrier_semaphore()
    total = n_vocab * n_expert
    flat = me * n_vocab + z

    def one(d, carry):
        peer = (flat + d) % total
        pl.semaphore_signal(
            barrier, inc=1,
            device_id={"expert": peer // n_vocab, "vocab": peer % n_vocab},
            device_id_type=MESH)
        return carry

    lax.fori_loop(1, total, one, 0)
    pl.semaphore_wait(barrier, total - 1)


def front_kernel(n, ids, wm, table, attn, in_gain, kw_in, key_gain, post_gain, routes, gates,
                 wg_in, wu_in, hidden, keys,
                 tab, wg, wu, kw, part, zin, every, att, emb, kin, pick, select, xs,
                 sh_out, sh_in, share, send, recv, ksend, krecv, kfwd, ssend, srecv, asend, arecv,
                 local):
    me, z, core, c = where_am_i()
    sib, xn, yn = me + 1 - 2 * core, (c + 1 - 2 * (c % 2)) * 2 + core, (c + 2 - 4 * (c // 2)) * 2 + core
    diag = (3 - c) * 2 + core
    chunks = part.shape[0]
    width = part.shape[3]
    half = part.shape[2] // 2
    rows = table.shape[0] * GROUP
    block = chunks * GROUP
    greet_all(n, 8, me, z)

    fetch = [
        pltpu.make_async_copy(table, tab.at[pl.ds(0, rows // GROUP)], local.at[0]),
        pltpu.make_async_copy(wg_in, wg, local.at[1]),
        pltpu.make_async_copy(wu_in, wu, local.at[2]),
        pltpu.make_async_copy(kw_in, kw, local.at[3]),
    ]
    fetch[0].start()

    def remote(src, dst, s_sem, r_sem, peer):
        return pltpu.make_async_remote_copy(
            src_ref=src, dst_ref=dst, send_sem=s_sem, recv_sem=r_sem,
            device_id=peer, device_id_type=MESH)

    far = (n - 1) * core

    def attn_moves(h):
        src = attn.at[:, :, pl.ds(h * width, width)]
        return remote(src, att.at[c], asend.at[h], arecv.at[c], {"expert": 2 * z + h, "vocab": far})

    def attn_stays(h):
        src = attn.at[:, :, pl.ds(h * width, width)]
        return pltpu.make_async_copy(src, att.at[c], arecv.at[c])

    for h in range(2):
        stays = (me == 2 * z + h) & (z == far)

        @pl.when(stays)
        def _():
            attn_stays(h).start()

        @pl.when(jnp.logical_not(stays))
        def _():
            attn_moves(h).start()

    gate_of = gates[...].astype(jnp.float32)
    gate_share = gate_of / jnp.sum(gate_of, axis=1, keepdims=True)
    named = routes[...]
    lane = lax.broadcasted_iota(jnp.int32, (block, 128), 1)
    spread = jnp.zeros((block, 128), jnp.float32)
    for k in range(named.shape[1]):
        spread = spread + jnp.where(lane == named[:, k:k + 1], gate_share[:, k:k + 1], 0.0)
    sh_out[...] = spread.T[0:16, :]
    own_rows = pl.ds(pl.multiple_of(me * 16, 16), 16)
    sh_in[own_rows, :] = sh_out[...]

    def share_move(d):
        return remote(sh_out, sh_in.at[own_rows], ssend.at[d], srecv.at[me],
                      {"expert": (me + d) % 8})

    for d in range(1, 8):
        share_move(d).start()

    tab[rows // GROUP] = jnp.zeros((GROUP, width), tab.dtype)
    r_at = lax.broadcasted_iota(jnp.int32, (GROUP, 128), 0)
    for r in range(GROUP):
        pick[r] = jnp.where(r_at == r, 1.0, 0.0).astype(pick.dtype)
    m_at = lax.broadcasted_iota(jnp.int32, (GROUP, GROUP * GROUP), 0)
    n_at = lax.broadcasted_iota(jnp.int32, (GROUP, GROUP * GROUP), 1)
    select[...] = jnp.where(n_at // GROUP == m_at, 1.0, 0.0).astype(select.dtype)
    fetch[0].wait()
    for f in fetch[1:]:
        f.start()

    base = z * rows

    def lookup(k):
        def one_side(qq, carry):
            for cc in range(4):
                tiles = []
                for j in range(GROUP):
                    loc = ids[(2 * cc + qq) * block + k * GROUP + j] - base
                    safe = jnp.minimum(jnp.maximum(loc, 0), rows - 1)
                    keep = (loc == safe) & (wm[safe] == 1)
                    tile = jnp.where(keep, jnp.right_shift(safe, 4), rows // GROUP)
                    r = jnp.bitwise_and(safe, 15)
                    src = tab[tile]
                    one = pick[r]
                    tiles.append(src * jnp.concatenate([one] * (width // 128), axis=1))
                stacked = jnp.concatenate(tiles, axis=0)
                got = jnp.dot(select[...], stacked, preferred_element_type=jnp.float32)
                part[k, qq, pl.ds(cc * GROUP, GROUP), :] = got.astype(part.dtype)
            return carry

        lax.fori_loop(0, 2, one_side, 0)

    CHAIN, RISE, XS, YS, SO, D0, D1, SX, SY, SD0, SD1 = range(11)

    def chain_move(src, k, qq):
        return remote(src, zin.at[k, qq], send.at[CHAIN, k, qq], recv.at[CHAIN, k, qq],
                      {"vocab": z - 1 + 2 * qq})

    def piece(slot, k, qq, lo=0, count=None):
        count = 2 * half if count is None else count
        return every.at[slot, k, qq, pl.ds(lo, count)]

    def to_peer(kind, ref, k, qq, peer):
        return remote(ref, ref, send.at[kind, k, qq], recv.at[kind, k, qq], peer)

    def rise_move(k, qq):
        return to_peer(RISE, piece(me, k, qq), k, qq, {"vocab": z + 1 - 2 * qq})

    def spec_of(kind, k, qq):
        return {
            XS: lambda: (piece(me, k, qq), xn),
            YS: lambda: (piece(me, k, qq), yn),
            SO: lambda: (piece(me, k, qq), sib),
            D0: lambda: (piece(xn, k, qq, 0, half), yn),
            D1: lambda: (piece(yn, k, qq, half, half), xn),
            SX: lambda: (piece(xn, k, qq), sib),
            SY: lambda: (piece(yn, k, qq), sib),
            SD0: lambda: (piece(diag, k, qq, 0, half), sib),
            SD1: lambda: (piece(diag, k, qq, half, half), sib),
        }[kind]()

    def move(kind, k, qq):
        ref, peer = spec_of(kind, k, qq)
        return to_peer(kind, ref, k, qq, {"expert": peer})

    sib_of = {SO: sib, SX: xn + sib - me, SY: yn + sib - me}
    sib_diag = diag + sib - me

    def arrive(kind, ref, k, qq):
        to_peer(kind, ref, k, qq, {"expert": sib}).wait_recv()

    def spread_out(k, qq):
        for kind in (XS, YS, SO):
            move(kind, k, qq).start()

    def normed_hidden(k):
        total = jnp.zeros((4 * half, 1), jnp.float32)
        for slot in range(8):
            v = every[slot, k].reshape(4 * half, width).astype(jnp.float32)
            total = total + jnp.sum(v * v, axis=1, keepdims=True)
        inverse = lax.rsqrt(total * (1.0 / (8 * width)) + 1e-06)
        for slot in range(8):
            columns = pl.ds(slot * width, width)
            v = every[slot, k].reshape(4 * half, width).astype(jnp.float32)
            xs[:, columns] = (v * inverse * post_gain[:, columns]).astype(xs.dtype)
        gate_val = jnp.dot(xs[...], wg[...], preferred_element_type=jnp.float32)
        up_val = jnp.dot(xs[...], wu[...], preferred_element_type=jnp.float32)
        scaled = gate_val / (1.0 + jnp.exp(-gate_val)) * up_val * share[k][:, 0:1]
        hidden[k] = scaled.astype(hidden.dtype)

    def sharing():
        for d in range(1, 8):
            other = (me + d) % 8
            other_rows = pl.ds(pl.multiple_of(other * 16, 16), 16)
            remote(sh_out, sh_in.at[other_rows], ssend.at[d], srecv.at[other],
                   {"expert": other}).wait_recv()
        turned = sh_in[...].T
        mine = (me * n + z) // 2
        lane = lax.broadcasted_iota(jnp.int32, (block, 128), 1)
        for owner in range(8):
            column = jnp.sum(jnp.where(lane == owner * 16 + mine, turned, 0.0), axis=1, keepdims=True)
            column = jnp.broadcast_to(column, (block, 128))
            at = (owner % 2) * 2 * half + (owner // 2) * GROUP
            for k in range(chunks):
                share[k, pl.ds(at, GROUP), :] = column[k * GROUP:(k + 1) * GROUP, :]

    keys_at = CHAIN_LAG * (n - 1) + chunks
    settle = CHAIN_LAG * (n - 1)

    def key_out(qq, cc):
        return remote(emb.at[cc], kin.at[me], ksend.at[cc], krecv.at[me], {"expert": 2 * cc + qq})

    def key_next(slot):
        return remote(kin.at[slot], kin.at[slot], kfwd.at[slot], krecv.at[slot],
                      {"vocab": z + 1 - 2 * core})

    key_far = z + (n - 1 - 2 * z) * core

    def inside(k):
        return (k >= 0) & (k < chunks)

    def step(s, carry):
        @pl.when(s < chunks)
        def _():
            lookup(s)

        for qq in range(2):
            at = z if qq == 1 else n - 1 - z
            away = n - 1 - at
            k = s - CHAIN_LAG * at

            @pl.when(inside(k) & (at == 0))
            def _():
                chain_move(part.at[k, qq], k, qq).start()

            @pl.when(inside(k) & (at > 0) & (at < n - 1))
            def _():
                chain_move(zin.at[k, qq], k, qq).wait_recv()
                zin[k, qq] = zin[k, qq] + part[k, qq]
                chain_move(zin.at[k, qq], k, qq).start()

            @pl.when(inside(k) & (at == n - 1))
            def _():
                @pl.when(k == 0)
                def _():
                    for cc in range(4):
                        pltpu.make_async_copy(att.at[cc], att.at[cc], arecv.at[cc]).wait()

                chain_move(zin.at[k, qq], k, qq).wait_recv()
                for cc in range(4):
                    some = pl.ds(cc * GROUP, GROUP)
                    whole = zin[k, qq, some, :] + part[k, qq, some, :]
                    emb[cc, k] = whole
                    mid = whole.astype(jnp.float32) + att[cc, k].astype(jnp.float32)
                    every[me, k, qq, some, :] = mid.astype(every.dtype)
                rise_move(k, qq).start()
                spread_out(k, qq)

            k2 = s - settle - RISE_LAG * away

            @pl.when(inside(k2) & (away > 0))
            def _():
                rise_move(k2, qq).wait_recv()

                @pl.when(away < n - 1)
                def _():
                    rise_move(k2, qq).start()

                spread_out(k2, qq)

            k3 = k2 - CROSS_LAG

            @pl.when(inside(k3))
            def _():
                arrive(XS, piece(xn, k3, qq), k3, qq)
                move(D0, k3, qq).start()
                move(SX, k3, qq).start()
                arrive(YS, piece(yn, k3, qq), k3, qq)
                move(D1, k3, qq).start()
                move(SY, k3, qq).start()

            k4 = k3 - DIAG_LAG

            @pl.when(inside(k4))
            def _():
                arrive(D0, piece(diag, k4, qq, 0, half), k4, qq)
                move(SD0, k4, qq).start()
                arrive(D1, piece(diag, k4, qq, half, half), k4, qq)
                move(SD1, k4, qq).start()

            k5 = k4 - SIB_LAG

            @pl.when(inside(k5))
            def _():
                for kind, slot in sib_of.items():
                    arrive(kind, piece(slot, k5, qq), k5, qq)
                arrive(SD0, piece(sib_diag, k5, qq, 0, half), k5, qq)
                arrive(SD1, piece(sib_diag, k5, qq, half, half), k5, qq)

            @pl.when((s == keys_at) & (at == n - 1))
            def _():
                for cc in range(4):
                    stays = me == 2 * cc + qq

                    @pl.when(stays)
                    def _():
                        pltpu.make_async_copy(emb.at[cc], kin.at[me], krecv.at[me]).start()

                    @pl.when(jnp.logical_not(stays))
                    def _():
                        key_out(qq, cc).start()

        for i in range(2):
            slot = 2 * (s - keys_at - 1 - key_far) + i

            @pl.when((slot >= 0) & (slot < 8))
            def _():
                pltpu.make_async_copy(kin.at[slot], kin.at[slot], krecv.at[slot]).wait()

                @pl.when(key_far < n - 1)
                def _():
                    key_next(slot).start()

        k6 = s - settle - RISE_LAG * jnp.maximum(z, n - 1 - z) - CROSS_LAG - DIAG_LAG - SIB_LAG

        @pl.when(k6 == 0)
        def _():
            fetch[1].wait()
            fetch[2].wait()
            sharing()

        @pl.when(inside(k6))
        def _():
            normed_hidden(k6)

        return carry

    steps = max(settle + RISE_LAG * (n - 1) + CROSS_LAG + DIAG_LAG + SIB_LAG + chunks,
                keys_at + 1 + (n - 1) + 4)
    lax.fori_loop(0, steps, step, 0)

    fetch[3].wait()
    total = jnp.zeros((block, 1), jnp.float32)
    for slot in range(8):
        v = kin[slot].reshape(block, width).astype(jnp.float32)
        total = total + jnp.sum(v * v, axis=1, keepdims=True)
    inverse = lax.rsqrt(total * (1.0 / (8 * width)) + 1e-06)
    raw = jnp.zeros((block, 128), jnp.float32)
    for slot in range(8):
        columns = pl.ds(slot * width, width)
        v = kin[slot].reshape(block, width).astype(jnp.float32)
        normed = (v * inverse * in_gain[:, columns]).astype(kw.dtype)
        raw = raw + jnp.dot(normed, kw[columns, :], preferred_element_type=jnp.float32)
    keys[...] = rms_rows(raw, key_gain[...]).astype(keys.dtype)

    def drain(k, carry):
        for qq in range(2):
            at = z if qq == 1 else n - 1 - z

            @pl.when(at < n - 1)
            def _():
                chain_move(zin.at[k, qq], k, qq).wait_send()

            @pl.when(at > 0)
            def _():
                rise_move(k, qq).wait_send()

            for kind in range(XS, SD1 + 1):
                move(kind, k, qq).wait_send()
        return carry

    lax.fori_loop(0, chunks, drain, 0)
    for qq in range(2):
        at = z if qq == 1 else n - 1 - z

        @pl.when(at == n - 1)
        def _():
            for cc in range(4):
                @pl.when(me != 2 * cc + qq)
                def _():
                    key_out(qq, cc).wait_send()

    @pl.when(key_far < n - 1)
    def _():
        for slot in range(8):
            key_next(slot).wait_send()

    for d in range(1, 8):
        share_move(d).wait_send()
    for h in range(2):
        @pl.when(jnp.logical_not((me == 2 * z + h) & (z == far)))
        def _():
            attn_moves(h).wait_send()


def front(n, token_ids, word_mask, embed_table, attn_out, in_gain, key_weight, key_gain, post_gain,
          routes, gate_ints, w_gate, w_up):
    block, columns = attn_out.shape
    rows, width = embed_table.shape
    chunks = block // GROUP
    side = 4 * GROUP
    units = w_gate.shape[1]
    model = 8 * width
    kind = embed_table.dtype
    vmem, anyw, smem = (pl.BlockSpec(memory_space=m) for m in (pltpu.VMEM, pl.ANY, pltpu.SMEM))
    dma = pltpu.SemaphoreType.DMA
    return pl.pallas_call(
        lambda *refs: front_kernel(n, *refs),
        name="embed_spread_project",
        out_shape=(
            jax.ShapeDtypeStruct((chunks, 2 * side, units), kind),
            jax.ShapeDtypeStruct((block, 128), kind),
        ),
        in_specs=[smem, smem, anyw, anyw, vmem, anyw, vmem, vmem, vmem, vmem, anyw, anyw],
        out_specs=(vmem, vmem),
        scratch_shapes=[
            pltpu.VMEM((rows // GROUP + 1, GROUP, width), kind),
            pltpu.VMEM(w_gate.shape, kind),
            pltpu.VMEM(w_up.shape, kind),
            pltpu.VMEM(key_weight.shape, kind),
            pltpu.VMEM((chunks, 2, side, width), kind),
            pltpu.VMEM((chunks, 2, side, width), kind),
            pltpu.VMEM((8, chunks, 2, side, width), kind),
            pltpu.VMEM((4, chunks, GROUP, width), kind),
            pltpu.VMEM((4, chunks, GROUP, width), kind),
            pltpu.VMEM((8, chunks, GROUP, width), kind),
            pltpu.VMEM((GROUP, GROUP, 128), kind),
            pltpu.VMEM((GROUP, GROUP * GROUP), kind),
            pltpu.VMEM((2 * side, model), kind),
            pltpu.VMEM((16, block), jnp.float32),
            pltpu.VMEM((128, block), jnp.float32),
            pltpu.VMEM((chunks, 2 * side, 128), jnp.float32),
            dma((11, chunks, 2)),
            dma((11, chunks, 2)),
            dma((4,)),
            dma((8,)),
            dma((8,)),
            dma((8,)),
            dma((8,)),
            dma((2,)),
            dma((4,)),
            dma((4,)),
        ],
        compiler_params=pltpu.CompilerParams(
            collective_id=0, has_side_effects=True, vmem_limit_bytes=60 * 1024 * 1024),
    )(token_ids, word_mask, embed_table.reshape(rows // GROUP, GROUP, width), attn_out.reshape(chunks, GROUP, columns),
      in_gain.reshape(1, -1), key_weight, key_gain.reshape(1, -1), post_gain.reshape(1, -1),
      routes, gate_ints, w_gate, w_up)


def back_kernel(n, hidden, wd_in, out, wd, obuf, sib_in, total, x_in, y_in, x_last, y_last, full,
                z_in, send, recv, local):
    me, z, core, c = where_am_i()
    cx, cy, cd = c + 1 - 2 * (c % 2), c + 2 - 4 * (c // 2), 3 - c
    sib, xn, yn = me + 1 - 2 * core, cx * 2 + core, cy * 2 + core
    fetch = pltpu.make_async_copy(wd_in, wd, local.at[0])
    fetch.start()
    barrier = pltpu.get_barrier_semaphore()
    peers = [{"expert": sib}, {"expert": xn}, {"expert": yn}]
    peers += [{"vocab": (z + d) % n} for d in range(1, n)]
    for peer in peers:
        pl.semaphore_signal(barrier, inc=1, device_id=peer, device_id_type=MESH)
    pl.semaphore_wait(barrier, len(peers))
    chunks, model = obuf.shape[0], obuf.shape[3]
    middle = model // 2
    quarter = model // n
    left, right = pl.ds(0, middle), pl.ds(middle, middle)

    def remote(kind, src, dst, k, peer):
        return pltpu.make_async_remote_copy(
            src_ref=src, dst_ref=dst, send_sem=send.at[kind, k], recv_sem=recv.at[kind, k],
            device_id=peer, device_id_type=MESH)

    def sib_move(k):
        return remote(0, obuf.at[k, 1 - core], sib_in.at[k], k, {"expert": sib})

    def first_move(i, k):
        src, dst, peer = (
            lambda: (total.at[k, cd, :, left], x_in.at[k, 1], xn),
            lambda: (total.at[k, cd, :, right], y_in.at[k, 1], yn),
            lambda: (total.at[k, cx, :, left], x_in.at[k, 0], xn),
            lambda: (total.at[k, cy, :, right], y_in.at[k, 0], yn),
        )[i]()
        return remote(1 + i, src, dst, k, {"expert": peer})

    def then_y(k):
        return remote(5, total.at[k, cy, :, left], y_last.at[k], k, {"expert": yn})

    def then_x(k):
        return remote(6, total.at[k, cx, :, right], x_last.at[k], k, {"expert": xn})

    def z_moves(k):
        return [remote(7 + d, full.at[k, (z + d + 1) % n], z_in.at[k, d], k,
                       {"vocab": (z + d + 1) % n}) for d in range(n - 1)]

    def wide(value):
        return value.astype(jnp.float32)

    def inside(k):
        return (k >= 0) & (k < chunks)

    def step(s, carry):
        @pl.when(s == 0)
        def _():
            fetch.wait()

        @pl.when(s < chunks)
        def _():
            made = jnp.dot(hidden[s], wd[...], preferred_element_type=jnp.float32)
            obuf[s] = made.astype(obuf.dtype).reshape(obuf.shape[1:])
            sib_move(s).start()

        k = s - 1

        @pl.when(inside(k))
        def _():
            sib_move(k).wait_recv()
            for cc in range(4):
                some = pl.ds(cc * GROUP, GROUP)
                both = wide(obuf[k, core, some, :]) + wide(sib_in[k, some, :])
                total[k, cc] = both.astype(total.dtype)
            for i in range(4):
                first_move(i, k).start()

        k2 = s - 3

        @pl.when(inside(k2))
        def _():
            first_move(0, k2).wait_recv()
            total[k2, cy, :, left] = (wide(total[k2, cy, :, left]) + wide(x_in[k2, 1])).astype(total.dtype)
            then_y(k2).start()
            first_move(1, k2).wait_recv()
            total[k2, cx, :, right] = (wide(total[k2, cx, :, right]) + wide(y_in[k2, 1])).astype(total.dtype)
            then_x(k2).start()

        k3 = s - 4

        @pl.when(inside(k3))
        def _():
            first_move(2, k3).wait_recv()
            then_y(k3).wait_recv()
            for q in range(n // 2):
                columns = pl.ds(q * quarter, quarter)
                term = wide(total[k3, c, :, columns]) + wide(x_in[k3, 0, :, columns])
                full[k3, q] = (term + wide(y_last[k3, :, columns])).astype(full.dtype)
            first_move(3, k3).wait_recv()
            then_x(k3).wait_recv()
            for q in range(n // 2):
                columns = pl.ds(q * quarter, quarter)
                behind = pl.ds(middle + q * quarter, quarter)
                term = wide(total[k3, c, :, behind]) + wide(y_in[k3, 0, :, columns])
                full[k3, n // 2 + q] = (term + wide(x_last[k3, :, columns])).astype(full.dtype)
            for moved in z_moves(k3):
                moved.start()

        k4 = s - 5

        @pl.when(inside(k4))
        def _():
            term = wide(full[k4, z])
            for d, moved in enumerate(z_moves(k4)):
                moved.wait_recv()
                term = term + wide(z_in[k4, d])
            out[k4] = term.astype(out.dtype)

        return carry

    lax.fori_loop(0, chunks + 5, step, 0)

    def drain(k, carry):
        for moved in [sib_move(k), then_x(k), then_y(k)] + [first_move(i, k) for i in range(4)] + z_moves(k):
            moved.wait_send()
        return carry

    lax.fori_loop(0, chunks, drain, 0)


def back(n, hidden, w_down):
    chunks, both, units = hidden.shape
    model = w_down.shape[1]
    side = both // 2
    kind = w_down.dtype
    dma = pltpu.SemaphoreType.DMA
    out = pl.pallas_call(
        lambda *refs: back_kernel(n, *refs),
        name="project_down_to_owners",
        out_shape=jax.ShapeDtypeStruct((chunks, GROUP, model // n), kind),
        in_specs=[pl.BlockSpec(memory_space=pltpu.VMEM), pl.BlockSpec(memory_space=pl.ANY)],
        out_specs=pl.BlockSpec(memory_space=pltpu.VMEM),
        scratch_shapes=[
            pltpu.VMEM(w_down.shape, kind),
            pltpu.VMEM((chunks, 2, side, model), kind),
            pltpu.VMEM((chunks, side, model), kind),
            pltpu.VMEM((chunks, 4, GROUP, model), kind),
            pltpu.VMEM((chunks, 2, GROUP, model // 2), kind),
            pltpu.VMEM((chunks, 2, GROUP, model // 2), kind),
            pltpu.VMEM((chunks, GROUP, model // 2), kind),
            pltpu.VMEM((chunks, GROUP, model // 2), kind),
            pltpu.VMEM((chunks, n, GROUP, model // n), kind),
            pltpu.VMEM((chunks, n - 1, GROUP, model // n), kind),
            dma((6 + n, chunks)),
            dma((6 + n, chunks)),
            dma((1,)),
        ],
        compiler_params=pltpu.CompilerParams(
            collective_id=1, has_side_effects=True, vmem_limit_bytes=56 * 1024 * 1024),
    )(hidden, w_down)
    return out.reshape(chunks * GROUP, model // n)


def by_collectives(
    token_ids, word_mask, embed_table, attn_out, in_gain, key_weight, key_gain, post_gain,
    routes, gate_ints, w_gate, w_up, w_down,
):
    n_vocab = lax.axis_size("vocab")
    n_expert = lax.axis_size("expert")
    vocab_rows = embed_table.shape[0]
    experts_total = n_expert * n_vocab // 2
    my_vocab = lax.axis_index("vocab")
    my_expert = (lax.axis_index("expert") * n_vocab + my_vocab) // 2

    gate_share = gate_ints.astype(jnp.float32) / jnp.sum(gate_ints, axis=1, keepdims=True).astype(
        jnp.float32
    )
    onehot = routes[:, :, None] == jnp.arange(experts_total, dtype=jnp.int32)[None, None, :]
    share_of = jnp.sum(jnp.where(onehot, gate_share[:, :, None], 0.0), axis=1)
    all_shares = lax.all_gather(share_of, "expert", axis=0, tiled=True)
    my_share = lax.dynamic_slice_in_dim(all_shares, my_expert, 1, axis=1)

    own_rows = attn_out.shape[0] // n_vocab
    attn_blocks = attn_out.reshape(n_vocab, own_rows, attn_out.shape[1])
    kept = lax.dynamic_index_in_dim(attn_blocks, my_vocab, 0, keepdims=True)
    attn_parts = lax.dynamic_update_slice_in_dim(attn_blocks, kept, my_vocab, 0)
    for d in range(1, n_vocab):
        sent = lax.dynamic_index_in_dim(attn_blocks, (my_vocab + d) % n_vocab, 0, keepdims=True)
        came = lax.ppermute(sent, "vocab", [(i, (i + d) % n_vocab) for i in range(n_vocab)])
        attn_parts = lax.dynamic_update_slice_in_dim(
            attn_parts, came, (my_vocab - d + n_vocab) % n_vocab, 0
        )
    attn_rows = attn_parts.transpose(1, 0, 2).reshape(own_rows, -1)

    ids = token_ids.reshape(n_expert, n_vocab, own_rows).transpose(1, 0, 2).reshape(-1)
    local_ids = ids - my_vocab * vocab_rows
    inside = (local_ids >= 0) & (local_ids < vocab_rows)
    safe_ids = jnp.clip(local_ids, 0, vocab_rows - 1)
    keep_row = inside & (word_mask[safe_ids] == 1)
    partial_value = jnp.where(
        keep_row[:, None], embed_table[safe_ids], jnp.zeros_like(embed_table[:1])
    )
    summed = lax.psum_scatter(partial_value, "vocab", scatter_dimension=0, tiled=True)
    rows = lax.all_to_all(summed, "expert", split_axis=0, concat_axis=1, tiled=True)
    rows = rows.astype(jnp.float32)

    mid_rows = (rows + attn_rows.astype(jnp.float32)).astype(jnp.bfloat16)
    expert_in = rms_rows(mid_rows.astype(jnp.float32), post_gain).astype(jnp.bfloat16)
    normed_rows = rms_rows(rows, in_gain).astype(jnp.bfloat16)
    tokens_in = lax.all_gather(expert_in, ("expert", "vocab"), axis=0, tiled=True)
    key_rows = lax.all_gather(normed_rows, "vocab", axis=0, tiled=True)
    raw_keys = jnp.dot(key_rows, key_weight, preferred_element_type=jnp.float32)
    key_heads = rms_rows(raw_keys, key_gain).astype(jnp.bfloat16)

    gate_val = jnp.dot(tokens_in, w_gate[0], preferred_element_type=jnp.float32)
    up_val = jnp.dot(tokens_in, w_up[0], preferred_element_type=jnp.float32)
    hidden = (jax.nn.silu(gate_val) * up_val).astype(jnp.bfloat16)
    parts = jnp.dot(hidden, w_down[0], preferred_element_type=jnp.float32)
    weighted = (parts * my_share).astype(jnp.bfloat16)
    by_tokens = lax.psum_scatter(weighted, "expert", scatter_dimension=0, tiled=True)
    expert_out = lax.psum_scatter(by_tokens, "vocab", scatter_dimension=1, tiled=True)
    return (expert_out, key_heads)


def by_kernels(
    token_ids, word_mask, embed_table, attn_out, in_gain, key_weight, key_gain, post_gain,
    routes, gate_ints, w_gate, w_up, w_down,
):
    n = lax.axis_size("vocab")
    hidden, key_heads = front(
        n, token_ids, word_mask, embed_table, attn_out, in_gain, key_weight, key_gain, post_gain,
        routes, gate_ints, w_gate[0], w_up[0])
    return (back(n, hidden, w_down[0]), key_heads)


def solution(mesh):
    small = mesh.shape["expert"] == 8 and mesh.shape["vocab"] == 4
    return jax.shard_map(
        by_kernels if small else by_collectives,
        mesh=mesh,
        in_specs=(
            P(),
            P("vocab"),
            P("vocab", "expert"),
            P("expert", "vocab"),
            P(),
            P(None, "vocab"),
            P(),
            P(),
            P("expert", None),
            P("expert", None),
            P(("expert", "vocab"), None, None),
            P(("expert", "vocab"), None, None),
            P(("expert", "vocab"), None, None),
        ),
        out_specs=(P("expert", "vocab"), P("expert", "vocab")),
        check_vma=False,
    )
```

```python
import jax
import jax.numpy as jnp
from jax import lax
from jax.experimental import pallas as pl
from jax.experimental.pallas import tpu as pltpu
from jax.sharding import PartitionSpec as P

MESH = pl.DeviceIdType.MESH
GROUP = 16
CHAIN_LAG, RISE_LAG, CROSS_LAG, DIAG_LAG, SIB_LAG = 3, 1, 2, 1, 1
KEY_START, KEY_LAG = 4, 2
HALF_LAG, ADD_LAG, LAST_LAG, OUT_LAG = 1, 2, 2, 2


def rms_rows(values, scale_gain):
    inverse_rms = lax.rsqrt(jnp.mean(values * values, axis=-1, keepdims=True) + 1e-06)
    return values * inverse_rms * scale_gain


def where_am_i():
    me = lax.axis_index("expert")
    z = lax.axis_index("vocab")
    return me, z, me % 2, me // 2


def greet_all(n_vocab, n_expert, me, z):
    barrier = pltpu.get_barrier_semaphore()
    total = n_vocab * n_expert
    flat = me * n_vocab + z

    def one(d, carry):
        peer = (flat + d) % total
        pl.semaphore_signal(
            barrier, inc=1,
            device_id={"expert": peer // n_vocab, "vocab": peer % n_vocab},
            device_id_type=MESH)
        return carry

    lax.fori_loop(1, total, one, 0)
    return lambda: pl.semaphore_wait(barrier, total - 1)


def layer_kernel(n, ids, wm, table, attn, in_gain, kw_in, key_gain, post_gain, routes, gates,
                 wg_in, wu_in, wd_in, out, keys,
                 tab, wg, wu, kw, part, zin, every, att, emb, kin, pick, select, xs,
                 sh_out, sh_in, share, send, recv, ksend, krecv, kfwd, ssend, srecv, asend, arecv,
                 sib_in, total, x_in, y_in, x_last, y_last, full, z_in, bsend, brecv, local):
    me, z, core, c = where_am_i()
    cx, cy, cd = c + 1 - 2 * (c % 2), c + 2 - 4 * (c // 2), 3 - c
    sib, xn, yn, diag = me + 1 - 2 * core, cx * 2 + core, cy * 2 + core, cd * 2 + core
    chunks = part.shape[0]
    width = part.shape[3]
    half = part.shape[2] // 2
    rows = table.shape[0] * GROUP
    block = chunks * GROUP
    fetch = [
        pltpu.make_async_copy(table, tab.at[pl.ds(0, rows // GROUP)], local.at[0]),
        pltpu.make_async_copy(wg_in, wg, local.at[1]),
        pltpu.make_async_copy(wu_in, wu, local.at[2]),
        pltpu.make_async_copy(kw_in, kw, local.at[3]),
    ]
    deep = wd_in.shape[0]
    down_at = 8 * deep

    def fetch_down(j):
        return pltpu.make_async_copy(
            wd_in.at[:, :, pl.ds(j * width, width)], tab.at[pl.ds(j * deep, deep)], local.at[4 + j])

    def leaving(k):
        return pl.ds(down_at + k * 32, 32)

    fetch[0].start()
    all_here = greet_all(n, 8, me, z)

    def remote(src, dst, s_sem, r_sem, peer):
        return pltpu.make_async_remote_copy(
            src_ref=src, dst_ref=dst, send_sem=s_sem, recv_sem=r_sem,
            device_id=peer, device_id_type=MESH)

    far = (n - 1) * core

    def attn_moves(h):
        src = attn.at[:, :, pl.ds(h * width, width)]
        return remote(src, att.at[c], asend.at[h], arecv.at[c], {"expert": 2 * z + h, "vocab": far})

    def attn_stays(h):
        src = attn.at[:, :, pl.ds(h * width, width)]
        return pltpu.make_async_copy(src, att.at[c], arecv.at[c])

    gate_of = gates[...].astype(jnp.float32)
    gate_share = gate_of / jnp.sum(gate_of, axis=0, keepdims=True)
    named = routes[...]
    expert_at = lax.broadcasted_iota(jnp.int32, (16, block), 0)
    spread = jnp.zeros((16, block), jnp.float32)
    for k in range(named.shape[0]):
        spread = spread + jnp.where(expert_at == named[k:k + 1, :], gate_share[k:k + 1, :], 0.0)
    sh_out[...] = spread
    own_rows = pl.ds(pl.multiple_of(me * 16, 16), 16)
    sh_in[own_rows, :] = sh_out[...]

    def share_move(d):
        return remote(sh_out, sh_in.at[own_rows], ssend.at[d], srecv.at[me],
                      {"expert": (me + d) % 8})

    tab[rows // GROUP] = jnp.zeros((GROUP, width), tab.dtype)
    r_at = lax.broadcasted_iota(jnp.int32, (GROUP, 128), 0)
    for r in range(GROUP):
        pick[r] = jnp.where(r_at == r, 1.0, 0.0).astype(pick.dtype)
    m_at = lax.broadcasted_iota(jnp.int32, (GROUP, GROUP * GROUP), 0)
    n_at = lax.broadcasted_iota(jnp.int32, (GROUP, GROUP * GROUP), 1)
    select[...] = jnp.where(n_at // GROUP == m_at, 1.0, 0.0).astype(select.dtype)
    all_here()
    for h in range(2):
        stays = (me == 2 * z + h) & (z == far)

        @pl.when(stays)
        def _():
            attn_stays(h).start()

        @pl.when(jnp.logical_not(stays))
        def _():
            attn_moves(h).start()

    for d in range(1, 8):
        share_move(d).start()

    fetch[0].wait()
    for one in fetch[1:]:
        one.start()

    base = z * rows

    def lookup(k):
        def one_side(qq, carry):
            for cc in range(4):
                tiles = []
                for j in range(GROUP):
                    loc = ids[(2 * cc + qq) * block + k * GROUP + j] - base
                    safe = jnp.minimum(jnp.maximum(loc, 0), rows - 1)
                    keep = (loc == safe) & (wm[safe] == 1)
                    tile = jnp.where(keep, jnp.right_shift(safe, 4), rows // GROUP)
                    r = jnp.bitwise_and(safe, 15)
                    src = tab[tile]
                    one = pick[r]
                    tiles.append(src * jnp.concatenate([one] * (width // 128), axis=1))
                stacked = jnp.concatenate(tiles, axis=0)
                got = jnp.dot(select[...], stacked, preferred_element_type=jnp.float32)
                part[k, qq, pl.ds(cc * GROUP, GROUP), :] = got.astype(part.dtype)
            return carry

        lax.fori_loop(0, 2, one_side, 0)

    CHAIN, RISE, XS, YS, SO, D0, D1, SX, SY, SD0, SD1 = range(11)

    def chain_move(src, k, qq):
        return remote(src, zin.at[k, qq], send.at[CHAIN, k, qq], recv.at[CHAIN, k, qq],
                      {"vocab": z - 1 + 2 * qq})

    def piece(slot, k, qq, lo=0, count=None):
        count = 2 * half if count is None else count
        return every.at[slot, k, qq, pl.ds(lo, count)]

    def to_peer(kind, ref, k, qq, peer):
        return remote(ref, ref, send.at[kind, k, qq], recv.at[kind, k, qq], peer)

    def rise_move(k, qq):
        return to_peer(RISE, piece(me, k, qq), k, qq, {"vocab": z + 1 - 2 * qq})

    def spec_of(kind, k, qq):
        return {
            XS: lambda: (piece(me, k, qq), xn),
            YS: lambda: (piece(me, k, qq), yn),
            SO: lambda: (piece(me, k, qq), sib),
            D0: lambda: (piece(xn, k, qq, 0, half), yn),
            D1: lambda: (piece(yn, k, qq, half, half), xn),
            SX: lambda: (piece(xn, k, qq), sib),
            SY: lambda: (piece(yn, k, qq), sib),
            SD0: lambda: (piece(diag, k, qq, 0, half), sib),
            SD1: lambda: (piece(diag, k, qq, half, half), sib),
        }[kind]()

    def move(kind, k, qq):
        ref, peer = spec_of(kind, k, qq)
        return to_peer(kind, ref, k, qq, {"expert": peer})

    sib_of = {SO: sib, SX: xn + sib - me, SY: yn + sib - me}
    sib_diag = diag + sib - me

    def arrive(kind, ref, k, qq):
        to_peer(kind, ref, k, qq, {"expert": sib}).wait_recv()

    def spread_out(k, qq):
        for kind in (XS, YS, SO):
            move(kind, k, qq).start()

    def make_hidden(k):
        squares = jnp.zeros((4 * half, 1), jnp.float32)
        for slot in range(8):
            v = every[slot, k].reshape(4 * half, width).astype(jnp.float32)
            squares = squares + jnp.sum(v * v, axis=1, keepdims=True)
        inverse = lax.rsqrt(squares * (1.0 / (8 * width)) + 1e-06)
        for slot in range(8):
            columns = pl.ds(slot * width, width)
            v = every[slot, k].reshape(4 * half, width).astype(jnp.float32)
            xs[:, columns] = (v * inverse * post_gain[:, columns]).astype(xs.dtype)
        gate_val = jnp.dot(xs[...], wg[...], preferred_element_type=jnp.float32)
        up_val = jnp.dot(xs[...], wu[...], preferred_element_type=jnp.float32)
        scaled = gate_val / (1.0 + jnp.exp(-gate_val)) * up_val * share[k][:, 0:1]
        hidden = scaled.astype(xs.dtype)
        for j in range(8):
            down = tab[pl.ds(j * deep, deep)].reshape(deep * GROUP, width)
            made = jnp.dot(hidden, down, preferred_element_type=jnp.float32)
            upper, lower = made[0:2 * half], made[2 * half:4 * half]
            stay = jnp.where(core == 0, upper, lower).astype(total.dtype)
            leave = jnp.where(core == 0, lower, upper).astype(total.dtype)
            for cc in range(4):
                total[k, cc, j] = stay[cc * GROUP:(cc + 1) * GROUP]
                tab[down_at + k * 32 + j * 4 + cc] = leave[cc * GROUP:(cc + 1) * GROUP]

    def sharing():
        for d in range(1, 8):
            other = (me + d) % 8
            other_rows = pl.ds(pl.multiple_of(other * 16, 16), 16)
            remote(sh_out, sh_in.at[other_rows], ssend.at[d], srecv.at[other],
                   {"expert": other}).wait_recv()
        turned = sh_in[...].T
        mine = (me * n + z) // 2
        lane = lax.broadcasted_iota(jnp.int32, (block, 128), 1)
        for owner in range(8):
            column = jnp.sum(jnp.where(lane == owner * 16 + mine, turned, 0.0), axis=1, keepdims=True)
            column = jnp.broadcast_to(column, (block, 128))
            at = (owner % 2) * 2 * half + (owner // 2) * GROUP
            for k in range(chunks):
                share[k, pl.ds(at, GROUP), :] = column[k * GROUP:(k + 1) * GROUP, :]

    settle = CHAIN_LAG * (n - 1)
    keys_at = settle + KEY_START

    def key_out(k, qq, cc):
        return remote(emb.at[k, cc], kin.at[k, me], ksend.at[k, cc], krecv.at[k],
                      {"expert": 2 * cc + qq})

    def key_next(k):
        return remote(kin.at[k], kin.at[k], kfwd.at[k], krecv.at[k], {"vocab": z + 1 - 2 * core})

    key_far = z + (n - 1 - 2 * z) * core

    def inside(k):
        return (k >= 0) & (k < chunks)

    def make_keys():
        fetch[3].wait()
        squares = jnp.zeros((block, 1), jnp.float32)
        for slot in range(8):
            v = kin[:, slot].reshape(block, width).astype(jnp.float32)
            squares = squares + jnp.sum(v * v, axis=1, keepdims=True)
        inverse = lax.rsqrt(squares * (1.0 / (8 * width)) + 1e-06)
        raw = jnp.zeros((block, 128), jnp.float32)
        for slot in range(8):
            columns = pl.ds(slot * width, width)
            v = kin[:, slot].reshape(block, width).astype(jnp.float32)
            normed = (v * inverse * in_gain[:, columns]).astype(kw.dtype)
            raw = raw + jnp.dot(normed, kw[columns, :], preferred_element_type=jnp.float32)
        keys[...] = rms_rows(raw, key_gain[...]).astype(keys.dtype)

    def back(kind, src, dst, k, peer):
        return pltpu.make_async_remote_copy(
            src_ref=src, dst_ref=dst, send_sem=bsend.at[kind, k], recv_sem=brecv.at[kind, k],
            device_id=peer, device_id_type=MESH)

    left, right = pl.ds(0, 4), pl.ds(4, 4)

    def sib_move(k):
        return back(0, tab.at[leaving(k)], sib_in.at[k], k, {"expert": sib})

    def first_move(i, k):
        src, dst, peer = (
            lambda: (total.at[k, cd, left], x_in.at[k, 1], xn),
            lambda: (total.at[k, cd, right], y_in.at[k, 1], yn),
            lambda: (total.at[k, cx, left], x_in.at[k, 0], xn),
            lambda: (total.at[k, cy, right], y_in.at[k, 0], yn),
        )[i]()
        return back(1 + i, src, dst, k, {"expert": peer})

    def then_y(k):
        return back(5, total.at[k, cy, left], y_last.at[k], k, {"expert": yn})

    def then_x(k):
        return back(6, total.at[k, cx, right], x_last.at[k], k, {"expert": xn})

    per = 8 // n

    def z_move(d, k):
        peer = (z + d + 1) % n
        return back(7 + d, full.at[k, pl.ds(peer * per, per)], z_in.at[k, d], k, {"vocab": peer})

    def wide(value):
        return value.astype(jnp.float32)

    def add_cores(k):
        sib_move(k).wait_recv()
        for cc in range(4):
            for j in range(8):
                both = wide(total[k, cc, j]) + wide(sib_in[k, j * 4 + cc])
                total[k, cc, j] = both.astype(total.dtype)
        for i in range(4):
            first_move(i, k).start()

    def add_across(k):
        first_move(0, k).wait_recv()
        for j in range(4):
            total[k, cy, j] = (wide(total[k, cy, j]) + wide(x_in[k, 1, j])).astype(total.dtype)
        then_y(k).start()
        first_move(1, k).wait_recv()
        for j in range(4):
            total[k, cx, 4 + j] = (wide(total[k, cx, 4 + j]) + wide(y_in[k, 1, j])).astype(total.dtype)
        then_x(k).start()

    def add_last(k):
        first_move(2, k).wait_recv()
        then_y(k).wait_recv()
        for j in range(4):
            term = wide(total[k, c, j]) + wide(x_in[k, 0, j]) + wide(y_last[k, j])
            full[k, j] = term.astype(full.dtype)
        first_move(3, k).wait_recv()
        then_x(k).wait_recv()
        for j in range(4):
            term = wide(total[k, c, 4 + j]) + wide(y_in[k, 0, j]) + wide(x_last[k, j])
            full[k, 4 + j] = term.astype(full.dtype)
        for d in range(n - 1):
            z_move(d, k).start()

    def add_planes(k):
        for d in range(n - 1):
            z_move(d, k).wait_recv()
        for j in range(per):
            term = wide(full[k, z * per + j])
            for d in range(n - 1):
                term = term + wide(z_in[k, d, j])
            out[k, :, pl.ds(j * width, width)] = term.astype(out.dtype)

    def step(s, carry):
        @pl.when(s < chunks)
        def _():
            lookup(s)

        for qq in range(2):
            at = z if qq == 1 else n - 1 - z
            away = n - 1 - at
            k = s - CHAIN_LAG * at

            @pl.when(inside(k) & (at == 0))
            def _():
                chain_move(part.at[k, qq], k, qq).start()

            @pl.when(inside(k) & (at > 0) & (at < n - 1))
            def _():
                chain_move(zin.at[k, qq], k, qq).wait_recv()
                zin[k, qq] = zin[k, qq] + part[k, qq]
                chain_move(zin.at[k, qq], k, qq).start()

            @pl.when(inside(k) & (at == n - 1))
            def _():
                @pl.when(k == 0)
                def _():
                    for cc in range(4):
                        pltpu.make_async_copy(att.at[cc], att.at[cc], arecv.at[cc]).wait()

                chain_move(zin.at[k, qq], k, qq).wait_recv()
                for cc in range(4):
                    some = pl.ds(cc * GROUP, GROUP)
                    whole = zin[k, qq, some, :] + part[k, qq, some, :]
                    emb[k, cc] = whole
                    mid = whole.astype(jnp.float32) + att[cc, k].astype(jnp.float32)
                    every[me, k, qq, some, :] = mid.astype(every.dtype)
                rise_move(k, qq).start()
                spread_out(k, qq)

            k2 = s - settle - RISE_LAG * away

            @pl.when(inside(k2) & (away > 0))
            def _():
                rise_move(k2, qq).wait_recv()

                @pl.when(away < n - 1)
                def _():
                    rise_move(k2, qq).start()

                spread_out(k2, qq)

            k3 = k2 - CROSS_LAG

            @pl.when(inside(k3))
            def _():
                arrive(XS, piece(xn, k3, qq), k3, qq)
                move(D0, k3, qq).start()
                move(SX, k3, qq).start()
                arrive(YS, piece(yn, k3, qq), k3, qq)
                move(D1, k3, qq).start()
                move(SY, k3, qq).start()

            k4 = k3 - DIAG_LAG

            @pl.when(inside(k4))
            def _():
                arrive(D0, piece(diag, k4, qq, 0, half), k4, qq)
                move(SD0, k4, qq).start()
                arrive(D1, piece(diag, k4, qq, half, half), k4, qq)
                move(SD1, k4, qq).start()

            k5 = k4 - SIB_LAG

            @pl.when(inside(k5))
            def _():
                for kind, slot in sib_of.items():
                    arrive(kind, piece(slot, k5, qq), k5, qq)
                arrive(SD0, piece(sib_diag, k5, qq, 0, half), k5, qq)
                arrive(SD1, piece(sib_diag, k5, qq, half, half), k5, qq)

            k7 = s - keys_at

            @pl.when(inside(k7) & (at == n - 1))
            def _():
                for cc in range(4):
                    stays = me == 2 * cc + qq

                    @pl.when(stays)
                    def _():
                        pltpu.make_async_copy(emb.at[k7, cc], kin.at[k7, me], krecv.at[k7]).start()

                    @pl.when(jnp.logical_not(stays))
                    def _():
                        key_out(k7, qq, cc).start()

        k8 = s - keys_at - KEY_LAG * (1 + key_far)

        @pl.when(inside(k8))
        def _():
            pltpu.make_async_copy(kin.at[k8], kin.at[k8], krecv.at[k8]).wait()

            @pl.when(key_far < n - 1)
            def _():
                key_next(k8).start()

        k6 = s - settle - RISE_LAG * jnp.maximum(z, n - 1 - z) - CROSS_LAG - DIAG_LAG - SIB_LAG

        @pl.when(s == chunks)
        def _():
            for j in range(8):
                fetch_down(j).start()

        k10 = k6 - HALF_LAG
        k11 = k10 - ADD_LAG
        k12 = k11 - LAST_LAG
        k13 = k12 - OUT_LAG

        for k, stage in ((k10, add_cores), (k11, add_across), (k12, add_last), (k13, add_planes)):
            @pl.when(inside(k))
            def _():
                stage(k)

        @pl.when(k6 == 0)
        def _():
            fetch[1].wait()
            fetch[2].wait()
            for j in range(8):
                fetch_down(j).wait()
            sharing()

        @pl.when(inside(k6))
        def _():
            make_hidden(k6)
            sib_move(k6).start()

        @pl.when(s == keys_at + KEY_LAG * n + chunks - 1)
        def _():
            make_keys()

        return carry

    steps = max(settle + RISE_LAG * (n - 1) + CROSS_LAG + DIAG_LAG + SIB_LAG
                + HALF_LAG + ADD_LAG + LAST_LAG + OUT_LAG + chunks,
                keys_at + KEY_LAG * n + chunks)
    lax.fori_loop(0, steps, step, 0)

    def drain(k, carry):
        for qq in range(2):
            at = z if qq == 1 else n - 1 - z

            @pl.when(at < n - 1)
            def _():
                chain_move(zin.at[k, qq], k, qq).wait_send()

            @pl.when(at > 0)
            def _():
                rise_move(k, qq).wait_send()

            for kind in range(XS, SD1 + 1):
                move(kind, k, qq).wait_send()
        sib_move(k).wait_send()
        for i in range(4):
            first_move(i, k).wait_send()
        then_x(k).wait_send()
        then_y(k).wait_send()
        for d in range(n - 1):
            z_move(d, k).wait_send()
        return carry

    lax.fori_loop(0, chunks, drain, 0)
    for qq in range(2):
        at = z if qq == 1 else n - 1 - z

        @pl.when(at == n - 1)
        def _():
            for k in range(chunks):
                for cc in range(4):
                    @pl.when(me != 2 * cc + qq)
                    def _():
                        key_out(k, qq, cc).wait_send()

    @pl.when(key_far < n - 1)
    def _():
        for k in range(chunks):
            key_next(k).wait_send()

    for d in range(1, 8):
        share_move(d).wait_send()
    for h in range(2):
        @pl.when(jnp.logical_not((me == 2 * z + h) & (z == far)))
        def _():
            attn_moves(h).wait_send()


def layer(n, token_ids, word_mask, embed_table, attn_out, in_gain, key_weight, key_gain, post_gain,
          routes, gate_ints, w_gate, w_up, w_down):
    block, columns = attn_out.shape
    rows, width = embed_table.shape
    chunks = block // GROUP
    side = 4 * GROUP
    units = w_gate.shape[1]
    model = 8 * width
    kind = embed_table.dtype
    vmem, anyw, smem = (pl.BlockSpec(memory_space=m) for m in (pltpu.VMEM, pl.ANY, pltpu.SMEM))
    dma = pltpu.SemaphoreType.DMA
    tiles = max(rows // GROUP + 1, 8 * units // GROUP + 32 * chunks)
    out, keys = pl.pallas_call(
        lambda *refs: layer_kernel(n, *refs),
        name="embed_and_experts",
        out_shape=(
            jax.ShapeDtypeStruct((chunks, GROUP, model // n), kind),
            jax.ShapeDtypeStruct((block, 128), kind),
        ),
        in_specs=[smem, smem, anyw, anyw, vmem, anyw, vmem, vmem, vmem, vmem, anyw, anyw, anyw],
        out_specs=(vmem, vmem),
        scratch_shapes=[
            pltpu.VMEM((tiles, GROUP, width), kind),
            pltpu.VMEM(w_gate.shape, kind),
            pltpu.VMEM(w_up.shape, kind),
            pltpu.VMEM(key_weight.shape, kind),
            pltpu.VMEM((chunks, 2, side, width), kind),
            pltpu.VMEM((chunks, 2, side, width), kind),
            pltpu.VMEM((8, chunks, 2, side, width), kind),
            pltpu.VMEM((4, chunks, GROUP, width), kind),
            pltpu.VMEM((chunks, 4, GROUP, width), kind),
            pltpu.VMEM((chunks, 8, GROUP, width), kind),
            pltpu.VMEM((GROUP, GROUP, 128), kind),
            pltpu.VMEM((GROUP, GROUP * GROUP), kind),
            pltpu.VMEM((2 * side, model), kind),
            pltpu.VMEM((16, block), jnp.float32),
            pltpu.VMEM((128, block), jnp.float32),
            pltpu.VMEM((chunks, 2 * side, 128), jnp.float32),
            dma((11, chunks, 2)),
            dma((11, chunks, 2)),
            dma((chunks, 4)),
            dma((chunks,)),
            dma((chunks,)),
            dma((8,)),
            dma((8,)),
            dma((2,)),
            dma((4,)),
            pltpu.VMEM((chunks, 32, GROUP, width), kind),
            pltpu.VMEM((chunks, 4, 8, GROUP, width), kind),
            pltpu.VMEM((chunks, 2, 4, GROUP, width), kind),
            pltpu.VMEM((chunks, 2, 4, GROUP, width), kind),
            pltpu.VMEM((chunks, 4, GROUP, width), kind),
            pltpu.VMEM((chunks, 4, GROUP, width), kind),
            pltpu.VMEM((chunks, 8, GROUP, width), kind),
            pltpu.VMEM((chunks, n - 1, 8 // n, GROUP, width), kind),
            dma((6 + n, chunks)),
            dma((6 + n, chunks)),
            dma((12,)),
        ],
        compiler_params=pltpu.CompilerParams(
            collective_id=0, has_side_effects=True, vmem_limit_bytes=63 * 1024 * 1024),
    )(token_ids, word_mask, embed_table.reshape(rows // GROUP, GROUP, width), attn_out.reshape(chunks, GROUP, columns),
      in_gain.reshape(1, -1), key_weight, key_gain.reshape(1, -1), post_gain.reshape(1, -1),
      routes.T, gate_ints.T, w_gate, w_up, w_down.reshape(units // GROUP, GROUP, model))
    return out.reshape(block, model // n), keys


def by_collectives(
    token_ids, word_mask, embed_table, attn_out, in_gain, key_weight, key_gain, post_gain,
    routes, gate_ints, w_gate, w_up, w_down,
):
    n_vocab = lax.axis_size("vocab")
    n_expert = lax.axis_size("expert")
    vocab_rows = embed_table.shape[0]
    experts_total = n_expert * n_vocab // 2
    my_vocab = lax.axis_index("vocab")
    my_expert = (lax.axis_index("expert") * n_vocab + my_vocab) // 2

    gate_share = gate_ints.astype(jnp.float32) / jnp.sum(gate_ints, axis=1, keepdims=True).astype(
        jnp.float32
    )
    onehot = routes[:, :, None] == jnp.arange(experts_total, dtype=jnp.int32)[None, None, :]
    share_of = jnp.sum(jnp.where(onehot, gate_share[:, :, None], 0.0), axis=1)
    all_shares = lax.all_gather(share_of, "expert", axis=0, tiled=True)
    my_share = lax.dynamic_slice_in_dim(all_shares, my_expert, 1, axis=1)

    own_rows = attn_out.shape[0] // n_vocab
    attn_blocks = attn_out.reshape(n_vocab, own_rows, attn_out.shape[1])
    kept = lax.dynamic_index_in_dim(attn_blocks, my_vocab, 0, keepdims=True)
    attn_parts = lax.dynamic_update_slice_in_dim(attn_blocks, kept, my_vocab, 0)
    for d in range(1, n_vocab):
        sent = lax.dynamic_index_in_dim(attn_blocks, (my_vocab + d) % n_vocab, 0, keepdims=True)
        came = lax.ppermute(sent, "vocab", [(i, (i + d) % n_vocab) for i in range(n_vocab)])
        attn_parts = lax.dynamic_update_slice_in_dim(
            attn_parts, came, (my_vocab - d + n_vocab) % n_vocab, 0
        )
    attn_rows = attn_parts.transpose(1, 0, 2).reshape(own_rows, -1)

    ids = token_ids.reshape(n_expert, n_vocab, own_rows).transpose(1, 0, 2).reshape(-1)
    local_ids = ids - my_vocab * vocab_rows
    inside = (local_ids >= 0) & (local_ids < vocab_rows)
    safe_ids = jnp.clip(local_ids, 0, vocab_rows - 1)
    keep_row = inside & (word_mask[safe_ids] == 1)
    partial_value = jnp.where(
        keep_row[:, None], embed_table[safe_ids], jnp.zeros_like(embed_table[:1])
    )
    summed = lax.psum_scatter(partial_value, "vocab", scatter_dimension=0, tiled=True)
    rows = lax.all_to_all(summed, "expert", split_axis=0, concat_axis=1, tiled=True)
    rows = rows.astype(jnp.float32)

    mid_rows = (rows + attn_rows.astype(jnp.float32)).astype(jnp.bfloat16)
    expert_in = rms_rows(mid_rows.astype(jnp.float32), post_gain).astype(jnp.bfloat16)
    normed_rows = rms_rows(rows, in_gain).astype(jnp.bfloat16)
    tokens_in = lax.all_gather(expert_in, ("expert", "vocab"), axis=0, tiled=True)
    key_rows = lax.all_gather(normed_rows, "vocab", axis=0, tiled=True)
    raw_keys = jnp.dot(key_rows, key_weight, preferred_element_type=jnp.float32)
    key_heads = rms_rows(raw_keys, key_gain).astype(jnp.bfloat16)

    gate_val = jnp.dot(tokens_in, w_gate[0], preferred_element_type=jnp.float32)
    up_val = jnp.dot(tokens_in, w_up[0], preferred_element_type=jnp.float32)
    hidden = (jax.nn.silu(gate_val) * up_val).astype(jnp.bfloat16)
    parts = jnp.dot(hidden, w_down[0], preferred_element_type=jnp.float32)
    weighted = (parts * my_share).astype(jnp.bfloat16)
    by_tokens = lax.psum_scatter(weighted, "expert", scatter_dimension=0, tiled=True)
    expert_out = lax.psum_scatter(by_tokens, "vocab", scatter_dimension=1, tiled=True)
    return (expert_out, key_heads)


def by_kernels(
    token_ids, word_mask, embed_table, attn_out, in_gain, key_weight, key_gain, post_gain,
    routes, gate_ints, w_gate, w_up, w_down,
):
    return layer(
        lax.axis_size("vocab"), token_ids, word_mask, embed_table, attn_out, in_gain, key_weight,
        key_gain, post_gain, routes, gate_ints, w_gate[0], w_up[0], w_down[0])


def solution(mesh):
    small = mesh.shape["expert"] == 8 and mesh.shape["vocab"] == 4
    return jax.shard_map(
        by_kernels if small else by_collectives,
        mesh=mesh,
        in_specs=(
            P(),
            P("vocab"),
            P("vocab", "expert"),
            P("expert", "vocab"),
            P(),
            P(None, "vocab"),
            P(),
            P(),
            P("expert", None),
            P("expert", None),
            P(("expert", "vocab"), None, None),
            P(("expert", "vocab"), None, None),
            P(("expert", "vocab"), None, None),
        ),
        out_specs=(P("expert", "vocab"), P("expert", "vocab")),
        check_vma=False,
    )
```

```python
import jax
import jax.numpy as jnp
from jax import lax
from jax.experimental import pallas as pl
from jax.experimental.pallas import tpu as pltpu
from jax.sharding import PartitionSpec as P

MESH = pl.DeviceIdType.MESH
GROUP = 16
TABLE_CUTS = 4
CHAIN_LAG, RISE_LAG, CROSS_LAG, DIAG_LAG, SIB_LAG = 2, 1, 2, 2, 1
KEY_START, KEY_LAG = 4, 2
HALF_LAG, ADD_LAG, LAST_LAG, OUT_LAG = 2, 1, 2, 3


def rms_rows(values, scale_gain):
    inverse_rms = lax.rsqrt(jnp.mean(values * values, axis=-1, keepdims=True) + 1e-06)
    return values * inverse_rms * scale_gain


def where_am_i():
    me = lax.axis_index("expert")
    z = lax.axis_index("vocab")
    return me, z, me % 2, me // 2


def greet_all(n_vocab, n_expert, me, z):
    barrier = pltpu.get_barrier_semaphore()
    total = n_vocab * n_expert
    flat = me * n_vocab + z

    def one(d, carry):
        peer = (flat + d) % total
        pl.semaphore_signal(
            barrier, inc=1,
            device_id={"expert": peer // n_vocab, "vocab": peer % n_vocab},
            device_id_type=MESH)
        return carry

    lax.fori_loop(1, total, one, 0)
    return lambda: pl.semaphore_wait(barrier, total - 1)


def layer_kernel(n, ids_in, wm_in, table, attn, in_gain_in, kw_in, key_gain_in, post_gain_in, routes_in, gates_in,
                 wg_in, wu_in, wd_in, out, keys,
                 ids, in_gain, key_gain, post_gain, routes, gates, wm, tab, wg, wu, kw, part, zin, every, att, emb, kin, pick, select, xs,
                 sh_out, sh_in, share, send, recv, ksend, krecv, kfwd, ssend, srecv, asend, arecv,
                 sib_in, total, x_in, y_in, x_last, y_last, full, z_in, bsend, brecv, small, local):
    me, z, core, c = where_am_i()
    cx, cy, cd = c + 1 - 2 * (c % 2), c + 2 - 4 * (c // 2), 3 - c
    sib, xn, yn, diag = me + 1 - 2 * core, cx * 2 + core, cy * 2 + core, cd * 2 + core
    chunks = part.shape[0]
    width = part.shape[3]
    half = part.shape[2] // 2
    rows = table.shape[0] * GROUP
    block = chunks * GROUP
    share_tiles = -(-(rows // GROUP) // TABLE_CUTS)
    cuts = [(at, min(share_tiles, rows // GROUP - at)) for at in range(0, rows // GROUP, share_tiles)]
    fetch_table = [
        pltpu.make_async_copy(table.at[pl.ds(at, count)], tab.at[pl.ds(at, count)], small.at[8 + i])
        for i, (at, count) in enumerate(cuts)]
    fetch_small = [
        pltpu.make_async_copy(src, dst, small.at[i])
        for i, (src, dst) in enumerate((
            (routes_in, routes), (gates_in, gates), (ids_in, ids), (wm_in, wm),
            (post_gain_in, post_gain), (in_gain_in, in_gain), (key_gain_in, key_gain)))]
    for one in fetch_small[0:4] + fetch_table + fetch_small[4:7]:
        one.start()
    fetch = [
        None,
        pltpu.make_async_copy(wg_in, wg, local.at[1]),
        pltpu.make_async_copy(wu_in, wu, local.at[2]),
        pltpu.make_async_copy(kw_in, kw, local.at[3]),
    ]
    deep = wd_in.shape[0]
    down_at = 8 * deep

    def fetch_down(j):
        return pltpu.make_async_copy(
            wd_in.at[:, :, pl.ds(j * width, width)], tab.at[pl.ds(j * deep, deep)], local.at[4 + j])

    def leaving(k):
        return pl.ds(down_at + k * 32, 32)

    all_here = greet_all(n, 8, me, z)

    def remote(src, dst, s_sem, r_sem, peer):
        return pltpu.make_async_remote_copy(
            src_ref=src, dst_ref=dst, send_sem=s_sem, recv_sem=r_sem,
            device_id=peer, device_id_type=MESH)

    near = n // 2 - 1
    far = near + core

    def attn_moves(h):
        src = attn.at[:, :, pl.ds(h * width, width)]
        return remote(src, att.at[c], asend.at[h], arecv.at[c], {"expert": 2 * z + h, "vocab": far})

    def attn_stays(h):
        src = attn.at[:, :, pl.ds(h * width, width)]
        return pltpu.make_async_copy(src, att.at[c], arecv.at[c])

    fetch_small[0].wait()
    fetch_small[1].wait()
    gate_of = gates[...].astype(jnp.float32)
    gate_share = gate_of / jnp.sum(gate_of, axis=0, keepdims=True)
    named = routes[...]
    expert_at = lax.broadcasted_iota(jnp.int32, (16, block), 0)
    spread = jnp.zeros((16, block), jnp.float32)
    for k in range(named.shape[0]):
        spread = spread + jnp.where(expert_at == named[k:k + 1, :], gate_share[k:k + 1, :], 0.0)
    sh_out[...] = spread
    own_rows = pl.ds(pl.multiple_of(me * 16, 16), 16)
    sh_in[own_rows, :] = sh_out[...]

    def share_move(d):
        return remote(sh_out, sh_in.at[own_rows], ssend.at[d], srecv.at[me],
                      {"expert": (me + d) % 8})

    tab[rows // GROUP] = jnp.zeros((GROUP, width), tab.dtype)
    r_at = lax.broadcasted_iota(jnp.int32, (GROUP, 128), 0)
    for r in range(GROUP):
        pick[r] = jnp.where(r_at == r, 1.0, 0.0).astype(pick.dtype)
    m_at = lax.broadcasted_iota(jnp.int32, (GROUP, GROUP * GROUP), 0)
    n_at = lax.broadcasted_iota(jnp.int32, (GROUP, GROUP * GROUP), 1)
    select[...] = jnp.where(n_at // GROUP == m_at, 1.0, 0.0).astype(select.dtype)
    all_here()
    for h in range(2):
        stays = (me == 2 * z + h) & (z == far)

        @pl.when(stays)
        def _():
            attn_stays(h).start()

        @pl.when(jnp.logical_not(stays))
        def _():
            attn_moves(h).start()

    for d in range(1, 8):
        share_move(d).start()

    for one in fetch_small[2:7] + fetch_table:
        one.wait()
    for one in fetch[1:]:
        one.start()

    base = z * rows

    def lookup(k):
        def one_side(qq, carry):
            for cc in range(4):
                tiles = []
                for j in range(GROUP):
                    loc = ids[(2 * cc + qq) * block + k * GROUP + j] - base
                    safe = jnp.minimum(jnp.maximum(loc, 0), rows - 1)
                    keep = (loc == safe) & (wm[safe] == 1)
                    tile = jnp.where(keep, jnp.right_shift(safe, 4), rows // GROUP)
                    r = jnp.bitwise_and(safe, 15)
                    src = tab[tile]
                    one = pick[r]
                    tiles.append(src * jnp.concatenate([one] * (width // 128), axis=1))
                stacked = jnp.concatenate(tiles, axis=0)
                got = jnp.dot(select[...], stacked, preferred_element_type=jnp.float32)
                part[k, qq, pl.ds(cc * GROUP, GROUP), :] = got.astype(part.dtype)
            return carry

        lax.fori_loop(0, 2, one_side, 0)

    CHAIN, RISE, XS, YS, SO, D0, D1, SX, SY, SD0, SD1 = 0, 2, 4, 5, 6, 7, 8, 9, 10, 11, 12

    def chain_move(src, k, qq, up):
        return remote(src, zin.at[up, k, qq], send.at[CHAIN + up, k, qq], recv.at[CHAIN + up, k, qq],
                      {"vocab": z - 1 + 2 * up})

    def chain_in(k, qq, up):
        chain_move(zin.at[up, k, qq], k, qq, up).wait_recv()

    def piece(slot, k, qq, lo=0, count=None):
        count = 2 * half if count is None else count
        return every.at[slot, k, qq, pl.ds(lo, count)]

    def to_peer(kind, ref, k, qq, peer):
        return remote(ref, ref, send.at[kind, k, qq], recv.at[kind, k, qq], peer)

    def rise_move(k, qq, up):
        return to_peer(RISE + up, piece(me, k, qq), k, qq, {"vocab": z - 1 + 2 * up})

    def spec_of(kind, k, qq):
        return {
            XS: lambda: (piece(me, k, qq), xn),
            YS: lambda: (piece(me, k, qq), yn),
            SO: lambda: (piece(me, k, qq), sib),
            D0: lambda: (piece(xn, k, qq, 0, half), yn),
            D1: lambda: (piece(yn, k, qq, half, half), xn),
            SX: lambda: (piece(xn, k, qq), sib),
            SY: lambda: (piece(yn, k, qq), sib),
            SD0: lambda: (piece(diag, k, qq, 0, half), sib),
            SD1: lambda: (piece(diag, k, qq, half, half), sib),
        }[kind]()

    def move(kind, k, qq):
        ref, peer = spec_of(kind, k, qq)
        return to_peer(kind, ref, k, qq, {"expert": peer})

    sib_of = {SO: sib, SX: xn + sib - me, SY: yn + sib - me}
    sib_diag = diag + sib - me

    def arrive(kind, ref, k, qq):
        to_peer(kind, ref, k, qq, {"expert": sib}).wait_recv()

    def spread_out(k, qq):
        for kind in (XS, YS, SO):
            move(kind, k, qq).start()

    def make_hidden(k):
        squares = jnp.zeros((4 * half, 1), jnp.float32)
        for slot in range(8):
            v = every[slot, k].reshape(4 * half, width).astype(jnp.float32)
            squares = squares + jnp.sum(v * v, axis=1, keepdims=True)
        inverse = lax.rsqrt(squares * (1.0 / (8 * width)) + 1e-06)
        for slot in range(8):
            columns = pl.ds(slot * width, width)
            v = every[slot, k].reshape(4 * half, width).astype(jnp.float32)
            xs[:, columns] = (v * inverse * post_gain[:, columns]).astype(xs.dtype)
        gate_val = jnp.dot(xs[...], wg[...], preferred_element_type=jnp.float32)
        up_val = jnp.dot(xs[...], wu[...], preferred_element_type=jnp.float32)
        scaled = gate_val / (1.0 + jnp.exp(-gate_val)) * up_val * share[k][:, 0:1]
        hidden = scaled.astype(xs.dtype)
        for j in range(8):
            down = tab[pl.ds(j * deep, deep)].reshape(deep * GROUP, width)
            made = jnp.dot(hidden, down, preferred_element_type=jnp.float32)
            upper, lower = made[0:2 * half], made[2 * half:4 * half]
            stay = jnp.where(core == 0, upper, lower).astype(total.dtype)
            leave = jnp.where(core == 0, lower, upper).astype(total.dtype)
            for cc in range(4):
                total[k, cc, j] = stay[cc * GROUP:(cc + 1) * GROUP]
                tab[down_at + k * 32 + j * 4 + cc] = leave[cc * GROUP:(cc + 1) * GROUP]

    def sharing():
        for d in range(1, 8):
            other = (me + d) % 8
            other_rows = pl.ds(pl.multiple_of(other * 16, 16), 16)
            remote(sh_out, sh_in.at[other_rows], ssend.at[d], srecv.at[other],
                   {"expert": other}).wait_recv()
        turned = sh_in[...].T
        mine = (me * n + z) // 2
        lane = lax.broadcasted_iota(jnp.int32, (block, 128), 1)
        for owner in range(8):
            column = jnp.sum(jnp.where(lane == owner * 16 + mine, turned, 0.0), axis=1, keepdims=True)
            column = jnp.broadcast_to(column, (block, 128))
            at = (owner % 2) * 2 * half + (owner // 2) * GROUP
            for k in range(chunks):
                share[k, pl.ds(at, GROUP), :] = column[k * GROUP:(k + 1) * GROUP, :]

    settle = CHAIN_LAG * (n // 2)
    long = n // 2
    keys_at = settle + KEY_START

    def key_out(k, qq, cc):
        return remote(emb.at[k, cc], kin.at[k, me], ksend.at[k, cc], krecv.at[k],
                      {"expert": 2 * cc + qq})

    def key_next(k, up):
        return remote(kin.at[k], kin.at[k], kfwd.at[k, up], krecv.at[k], {"vocab": z - 1 + 2 * up})

    def away_of(qq):
        offset = z - near - qq
        return jnp.maximum(offset, -offset)

    key_far = away_of(core)

    def outward(qq, run):
        for up in range(2):
            beyond = (z >= near + qq) & (z < n - 1) if up else (z <= near + qq) & (z > 0)

            @pl.when(beyond)
            def _():
                run(up)

    def inside(k):
        return (k >= 0) & (k < chunks)

    def make_keys():
        fetch[3].wait()
        squares = jnp.zeros((block, 1), jnp.float32)
        for slot in range(8):
            v = kin[:, slot].reshape(block, width).astype(jnp.float32)
            squares = squares + jnp.sum(v * v, axis=1, keepdims=True)
        inverse = lax.rsqrt(squares * (1.0 / (8 * width)) + 1e-06)
        raw = jnp.zeros((block, 128), jnp.float32)
        for slot in range(8):
            columns = pl.ds(slot * width, width)
            v = kin[:, slot].reshape(block, width).astype(jnp.float32)
            normed = (v * inverse * in_gain[:, columns]).astype(kw.dtype)
            raw = raw + jnp.dot(normed, kw[columns, :], preferred_element_type=jnp.float32)
        keys[...] = rms_rows(raw, key_gain[...]).astype(keys.dtype)

    def back(kind, src, dst, k, peer):
        return pltpu.make_async_remote_copy(
            src_ref=src, dst_ref=dst, send_sem=bsend.at[kind, k], recv_sem=brecv.at[kind, k],
            device_id=peer, device_id_type=MESH)

    left, right = pl.ds(0, 4), pl.ds(4, 4)

    def sib_move(k):
        return back(0, tab.at[leaving(k)], sib_in.at[k], k, {"expert": sib})

    def first_move(i, k):
        src, dst, peer = (
            lambda: (total.at[k, cd, left], x_in.at[k, 1], xn),
            lambda: (total.at[k, cd, right], y_in.at[k, 1], yn),
            lambda: (total.at[k, cx, left], x_in.at[k, 0], xn),
            lambda: (total.at[k, cy, right], y_in.at[k, 0], yn),
        )[i]()
        return back(1 + i, src, dst, k, {"expert": peer})

    def then_y(k):
        return back(5, total.at[k, cy, left], y_last.at[k], k, {"expert": yn})

    def then_x(k):
        return back(6, total.at[k, cx, right], x_last.at[k], k, {"expert": xn})

    per = 8 // n

    def z_move(d, k):
        peer = (z + d + 1) % n
        return back(7 + d, full.at[k, pl.ds(peer * per, per)], z_in.at[k, d], k, {"vocab": peer})

    def wide(value):
        return value.astype(jnp.float32)

    def add_cores(k):
        sib_move(k).wait_recv()
        for cc in range(4):
            for j in range(8):
                both = wide(total[k, cc, j]) + wide(sib_in[k, j * 4 + cc])
                total[k, cc, j] = both.astype(total.dtype)
        for i in range(4):
            first_move(i, k).start()

    def add_across(k):
        first_move(0, k).wait_recv()
        for j in range(4):
            total[k, cy, j] = (wide(total[k, cy, j]) + wide(x_in[k, 1, j])).astype(total.dtype)
        then_y(k).start()
        first_move(1, k).wait_recv()
        for j in range(4):
            total[k, cx, 4 + j] = (wide(total[k, cx, 4 + j]) + wide(y_in[k, 1, j])).astype(total.dtype)
        then_x(k).start()

    def add_last(k):
        first_move(2, k).wait_recv()
        then_y(k).wait_recv()
        for j in range(4):
            term = wide(total[k, c, j]) + wide(x_in[k, 0, j]) + wide(y_last[k, j])
            full[k, j] = term.astype(full.dtype)
        first_move(3, k).wait_recv()
        then_x(k).wait_recv()
        for j in range(4):
            term = wide(total[k, c, 4 + j]) + wide(y_in[k, 0, j]) + wide(x_last[k, j])
            full[k, 4 + j] = term.astype(full.dtype)
        for d in range(n - 1):
            z_move(d, k).start()

    def add_planes(k):
        for d in range(n - 1):
            z_move(d, k).wait_recv()
        for j in range(per):
            term = wide(full[k, z * per + j])
            for d in range(n - 1):
                term = term + wide(z_in[k, d, j])
            out[k, :, pl.ds(j * width, width)] = term.astype(out.dtype)

    def step(s, carry):
        @pl.when(s < chunks)
        def _():
            lookup(s)

        for qq in range(2):
            away = away_of(qq)
            ends = (z == 0) | (z == n - 1)
            relay = (away == 1) & jnp.logical_not(ends)

            for up in range(2):
                @pl.when((s < chunks) & (z == (0 if up else n - 1)))
                def _():
                    chain_move(part.at[s, qq], s, qq, up).start()

            k = s - CHAIN_LAG

            @pl.when(inside(k) & relay)
            def _():
                chain_in(k, qq, qq)
                zin[qq, k, qq] = zin[qq, k, qq] + part[k, qq]
                chain_move(zin.at[qq, k, qq], k, qq, qq).start()

            k1 = s - settle

            @pl.when(inside(k1) & (away == 0))
            def _():
                @pl.when(k1 == 0)
                def _():
                    for cc in range(4):
                        pltpu.make_async_copy(att.at[cc], att.at[cc], arecv.at[cc]).wait()

                chain_in(k1, qq, 1 - qq)
                chain_in(k1, qq, qq)
                for cc in range(4):
                    some = pl.ds(cc * GROUP, GROUP)
                    whole = zin[0, k1, qq, some, :] + zin[1, k1, qq, some, :] + part[k1, qq, some, :]
                    emb[k1, cc] = whole
                    mid = whole.astype(jnp.float32) + att[cc, k1].astype(jnp.float32)
                    every[me, k1, qq, some, :] = mid.astype(every.dtype)
                outward(qq, lambda up: rise_move(k1, qq, up).start())
                spread_out(k1, qq)

            k2 = s - settle - RISE_LAG * away

            @pl.when(inside(k2) & (away > 0))
            def _():
                for up in range(2):
                    @pl.when((z > near + qq) if up else (z < near + qq))
                    def _():
                        rise_move(k2, qq, up).wait_recv()

                outward(qq, lambda up: rise_move(k2, qq, up).start())
                spread_out(k2, qq)

            k3 = k2 - CROSS_LAG

            @pl.when(inside(k3))
            def _():
                arrive(XS, piece(xn, k3, qq), k3, qq)
                move(D0, k3, qq).start()
                move(SX, k3, qq).start()
                arrive(YS, piece(yn, k3, qq), k3, qq)
                move(D1, k3, qq).start()
                move(SY, k3, qq).start()

            k4 = k3 - DIAG_LAG

            @pl.when(inside(k4))
            def _():
                arrive(D0, piece(diag, k4, qq, 0, half), k4, qq)
                move(SD0, k4, qq).start()
                arrive(D1, piece(diag, k4, qq, half, half), k4, qq)
                move(SD1, k4, qq).start()

            k5 = k4 - SIB_LAG

            @pl.when(inside(k5))
            def _():
                for kind, slot in sib_of.items():
                    arrive(kind, piece(slot, k5, qq), k5, qq)
                arrive(SD0, piece(sib_diag, k5, qq, 0, half), k5, qq)
                arrive(SD1, piece(sib_diag, k5, qq, half, half), k5, qq)

            k7 = s - keys_at

            @pl.when(inside(k7) & (away == 0))
            def _():
                for cc in range(4):
                    stays = me == 2 * cc + qq

                    @pl.when(stays)
                    def _():
                        pltpu.make_async_copy(emb.at[k7, cc], kin.at[k7, me], krecv.at[k7]).start()

                    @pl.when(jnp.logical_not(stays))
                    def _():
                        key_out(k7, qq, cc).start()

        k8 = s - keys_at - KEY_LAG * (1 + key_far)

        @pl.when(inside(k8))
        def _():
            pltpu.make_async_copy(kin.at[k8], kin.at[k8], krecv.at[k8]).wait()

            outward(core, lambda up: key_next(k8, up).start())

        k6 = s - settle - RISE_LAG * jnp.maximum(away_of(0), away_of(1)) - CROSS_LAG - DIAG_LAG - SIB_LAG

        @pl.when(s == chunks)
        def _():
            for j in range(8):
                fetch_down(j).start()

        k10 = k6 - HALF_LAG
        k11 = k10 - ADD_LAG
        k12 = k11 - LAST_LAG
        k13 = k12 - OUT_LAG

        for k, stage in ((k10, add_cores), (k11, add_across), (k12, add_last), (k13, add_planes)):
            @pl.when(inside(k))
            def _():
                stage(k)

        @pl.when(k6 == 0)
        def _():
            fetch[1].wait()
            fetch[2].wait()
            for j in range(8):
                fetch_down(j).wait()
            sharing()

        @pl.when(inside(k6))
        def _():
            make_hidden(k6)
            sib_move(k6).start()

        @pl.when(s == keys_at + KEY_LAG * (1 + long) + chunks - 1)
        def _():
            make_keys()

        return carry

    steps = max(settle + RISE_LAG * long + CROSS_LAG + DIAG_LAG + SIB_LAG
                + HALF_LAG + ADD_LAG + LAST_LAG + OUT_LAG + chunks,
                keys_at + KEY_LAG * (1 + long) + chunks)
    lax.fori_loop(0, steps, step, 0)

    def drain(k, carry):
        for qq in range(2):
            for up in range(2):
                @pl.when(z == (0 if up else n - 1))
                def _():
                    chain_move(part.at[k, qq], k, qq, up).wait_send()

            @pl.when((z == near + 1 - qq))
            def _():
                chain_move(part.at[k, qq], k, qq, qq).wait_send()

            outward(qq, lambda up: rise_move(k, qq, up).wait_send())

            for kind in range(XS, SD1 + 1):
                move(kind, k, qq).wait_send()
        sib_move(k).wait_send()
        for i in range(4):
            first_move(i, k).wait_send()
        then_x(k).wait_send()
        then_y(k).wait_send()
        for d in range(n - 1):
            z_move(d, k).wait_send()
        return carry

    lax.fori_loop(0, chunks, drain, 0)
    for qq in range(2):
        @pl.when(away_of(qq) == 0)
        def _():
            for k in range(chunks):
                for cc in range(4):
                    @pl.when(me != 2 * cc + qq)
                    def _():
                        key_out(k, qq, cc).wait_send()

    for k in range(chunks):
        outward(core, lambda up: key_next(k, up).wait_send())

    for d in range(1, 8):
        share_move(d).wait_send()
    for h in range(2):
        @pl.when(jnp.logical_not((me == 2 * z + h) & (z == far)))
        def _():
            attn_moves(h).wait_send()


def layer(n, token_ids, word_mask, embed_table, attn_out, in_gain, key_weight, key_gain, post_gain,
          routes, gate_ints, w_gate, w_up, w_down):
    block, columns = attn_out.shape
    rows, width = embed_table.shape
    chunks = block // GROUP
    side = 4 * GROUP
    units = w_gate.shape[1]
    model = 8 * width
    kind = embed_table.dtype
    vmem, anyw = (pl.BlockSpec(memory_space=m) for m in (pltpu.VMEM, pl.ANY))
    dma = pltpu.SemaphoreType.DMA
    tiles = max(rows // GROUP + 1, 8 * units // GROUP + 32 * chunks)
    out, keys = pl.pallas_call(
        lambda *refs: layer_kernel(n, *refs),
        name="embed_and_experts",
        out_shape=(
            jax.ShapeDtypeStruct((chunks, GROUP, model // n), kind),
            jax.ShapeDtypeStruct((block, 128), kind),
        ),
        in_specs=[anyw] * 13,
        out_specs=(vmem, vmem),
        scratch_shapes=[
            pltpu.SMEM(token_ids.shape, token_ids.dtype),
            pltpu.VMEM((1, model), jnp.float32),
            pltpu.VMEM((1, 128), jnp.float32),
            pltpu.VMEM((1, model), jnp.float32),
            pltpu.VMEM((8, block), routes.dtype),
            pltpu.VMEM((8, block), gate_ints.dtype),
            pltpu.SMEM(word_mask.shape, word_mask.dtype),
            pltpu.VMEM((tiles, GROUP, width), kind),
            pltpu.VMEM(w_gate.shape, kind),
            pltpu.VMEM(w_up.shape, kind),
            pltpu.VMEM(key_weight.shape, kind),
            pltpu.VMEM((chunks, 2, side, width), kind),
            pltpu.VMEM((2, chunks, 2, side, width), kind),
            pltpu.VMEM((8, chunks, 2, side, width), kind),
            pltpu.VMEM((4, chunks, GROUP, width), kind),
            pltpu.VMEM((chunks, 4, GROUP, width), kind),
            pltpu.VMEM((chunks, 8, GROUP, width), kind),
            pltpu.VMEM((GROUP, GROUP, 128), kind),
            pltpu.VMEM((GROUP, GROUP * GROUP), kind),
            pltpu.VMEM((2 * side, model), kind),
            pltpu.VMEM((16, block), jnp.float32),
            pltpu.VMEM((128, block), jnp.float32),
            pltpu.VMEM((chunks, 2 * side, 128), jnp.float32),
            dma((13, chunks, 2)),
            dma((13, chunks, 2)),
            dma((chunks, 4)),
            dma((chunks,)),
            dma((chunks, 2)),
            dma((8,)),
            dma((8,)),
            dma((2,)),
            dma((4,)),
            pltpu.VMEM((chunks, 32, GROUP, width), kind),
            pltpu.VMEM((chunks, 4, 8, GROUP, width), kind),
            pltpu.VMEM((chunks, 2, 4, GROUP, width), kind),
            pltpu.VMEM((chunks, 2, 4, GROUP, width), kind),
            pltpu.VMEM((chunks, 4, GROUP, width), kind),
            pltpu.VMEM((chunks, 4, GROUP, width), kind),
            pltpu.VMEM((chunks, 8, GROUP, width), kind),
            pltpu.VMEM((chunks, n - 1, 8 // n, GROUP, width), kind),
            dma((6 + n, chunks)),
            dma((6 + n, chunks)),
            dma((8 + TABLE_CUTS,)),
            dma((13,)),
        ],
        compiler_params=pltpu.CompilerParams(
            collective_id=0, has_side_effects=True, vmem_limit_bytes=63 * 1024 * 1024),
    )(token_ids, word_mask, embed_table.reshape(rows // GROUP, GROUP, width), attn_out.reshape(chunks, GROUP, columns),
      in_gain.reshape(1, -1), key_weight, key_gain.reshape(1, -1), post_gain.reshape(1, -1),
      routes.T, gate_ints.T, w_gate, w_up, w_down.reshape(units // GROUP, GROUP, model))
    return out.reshape(block, model // n), keys


def by_collectives(
    token_ids, word_mask, embed_table, attn_out, in_gain, key_weight, key_gain, post_gain,
    routes, gate_ints, w_gate, w_up, w_down,
):
    n_vocab = lax.axis_size("vocab")
    n_expert = lax.axis_size("expert")
    vocab_rows = embed_table.shape[0]
    experts_total = n_expert * n_vocab // 2
    my_vocab = lax.axis_index("vocab")
    my_expert = (lax.axis_index("expert") * n_vocab + my_vocab) // 2

    gate_share = gate_ints.astype(jnp.float32) / jnp.sum(gate_ints, axis=1, keepdims=True).astype(
        jnp.float32
    )
    onehot = routes[:, :, None] == jnp.arange(experts_total, dtype=jnp.int32)[None, None, :]
    share_of = jnp.sum(jnp.where(onehot, gate_share[:, :, None], 0.0), axis=1)
    all_shares = lax.all_gather(share_of, "expert", axis=0, tiled=True)
    my_share = lax.dynamic_slice_in_dim(all_shares, my_expert, 1, axis=1)

    own_rows = attn_out.shape[0] // n_vocab
    attn_blocks = attn_out.reshape(n_vocab, own_rows, attn_out.shape[1])
    kept = lax.dynamic_index_in_dim(attn_blocks, my_vocab, 0, keepdims=True)
    attn_parts = lax.dynamic_update_slice_in_dim(attn_blocks, kept, my_vocab, 0)
    for d in range(1, n_vocab):
        sent = lax.dynamic_index_in_dim(attn_blocks, (my_vocab + d) % n_vocab, 0, keepdims=True)
        came = lax.ppermute(sent, "vocab", [(i, (i + d) % n_vocab) for i in range(n_vocab)])
        attn_parts = lax.dynamic_update_slice_in_dim(
            attn_parts, came, (my_vocab - d + n_vocab) % n_vocab, 0
        )
    attn_rows = attn_parts.transpose(1, 0, 2).reshape(own_rows, -1)

    ids = token_ids.reshape(n_expert, n_vocab, own_rows).transpose(1, 0, 2).reshape(-1)
    local_ids = ids - my_vocab * vocab_rows
    inside = (local_ids >= 0) & (local_ids < vocab_rows)
    safe_ids = jnp.clip(local_ids, 0, vocab_rows - 1)
    keep_row = inside & (word_mask[safe_ids] == 1)
    partial_value = jnp.where(
        keep_row[:, None], embed_table[safe_ids], jnp.zeros_like(embed_table[:1])
    )
    summed = lax.psum_scatter(partial_value, "vocab", scatter_dimension=0, tiled=True)
    rows = lax.all_to_all(summed, "expert", split_axis=0, concat_axis=1, tiled=True)
    rows = rows.astype(jnp.float32)

    mid_rows = (rows + attn_rows.astype(jnp.float32)).astype(jnp.bfloat16)
    expert_in = rms_rows(mid_rows.astype(jnp.float32), post_gain).astype(jnp.bfloat16)
    normed_rows = rms_rows(rows, in_gain).astype(jnp.bfloat16)
    tokens_in = lax.all_gather(expert_in, ("expert", "vocab"), axis=0, tiled=True)
    key_rows = lax.all_gather(normed_rows, "vocab", axis=0, tiled=True)
    raw_keys = jnp.dot(key_rows, key_weight, preferred_element_type=jnp.float32)
    key_heads = rms_rows(raw_keys, key_gain).astype(jnp.bfloat16)

    gate_val = jnp.dot(tokens_in, w_gate[0], preferred_element_type=jnp.float32)
    up_val = jnp.dot(tokens_in, w_up[0], preferred_element_type=jnp.float32)
    hidden = (jax.nn.silu(gate_val) * up_val).astype(jnp.bfloat16)
    parts = jnp.dot(hidden, w_down[0], preferred_element_type=jnp.float32)
    weighted = (parts * my_share).astype(jnp.bfloat16)
    by_tokens = lax.psum_scatter(weighted, "expert", scatter_dimension=0, tiled=True)
    expert_out = lax.psum_scatter(by_tokens, "vocab", scatter_dimension=1, tiled=True)
    return (expert_out, key_heads)


def by_kernels(
    token_ids, word_mask, embed_table, attn_out, in_gain, key_weight, key_gain, post_gain,
    routes, gate_ints, w_gate, w_up, w_down,
):
    return layer(
        lax.axis_size("vocab"), token_ids, word_mask, embed_table, attn_out, in_gain, key_weight,
        key_gain, post_gain, routes, gate_ints, w_gate[0], w_up[0], w_down[0])


def solution(mesh):
    small = mesh.shape["expert"] == 8 and mesh.shape["vocab"] == 4
    return jax.shard_map(
        by_kernels if small else by_collectives,
        mesh=mesh,
        in_specs=(
            P(),
            P("vocab"),
            P("vocab", "expert"),
            P("expert", "vocab"),
            P(),
            P(None, "vocab"),
            P(),
            P(),
            P("expert", None),
            P("expert", None),
            P(("expert", "vocab"), None, None),
            P(("expert", "vocab"), None, None),
            P(("expert", "vocab"), None, None),
        ),
        out_specs=(P("expert", "vocab"), P("expert", "vocab")),
        check_vma=False,
    )
```

```python
import jax
import jax.numpy as jnp
from jax import lax
from jax.experimental import pallas as pl
from jax.experimental.pallas import tpu as pltpu
from jax.sharding import PartitionSpec as P

MESH = pl.DeviceIdType.MESH
GROUP = 16
TABLE_CUTS = 4
CHAIN_LAG, RISE_LAG, CROSS_LAG, DIAG_LAG, SIB_LAG = 2, 1, 2, 2, 1
KEY_START, KEY_LAG = 4, 2
HALF_LAG, ADD_LAG, LAST_LAG, OUT_LAG = 2, 1, 2, 3


def rms_rows(values, scale_gain):
    inverse_rms = lax.rsqrt(jnp.mean(values * values, axis=-1, keepdims=True) + 1e-06)
    return values * inverse_rms * scale_gain


def where_am_i():
    me = lax.axis_index("expert")
    z = lax.axis_index("vocab")
    return me, z, me % 2, me // 2


def greet_all(n_vocab, n_expert, me, z):
    barrier = pltpu.get_barrier_semaphore()
    total = n_vocab * n_expert
    flat = me * n_vocab + z

    def one(d, carry):
        peer = (flat + d) % total
        pl.semaphore_signal(
            barrier, inc=1,
            device_id={"expert": peer // n_vocab, "vocab": peer % n_vocab},
            device_id_type=MESH)
        return carry

    lax.fori_loop(1, total, one, 0)
    return lambda: pl.semaphore_wait(barrier, total - 1)


def layer_kernel(n, ids_in, wm_in, table, attn, in_gain_in, kw_in, key_gain_in, post_gain_in, routes_in, gates_in,
                 wg_in, wu_in, wd_in, out, keys,
                 ids, in_gain, key_gain, post_gain, routes, gates, wm, tab, wg, wu, kw, part, zin, every, att, emb, kin, pick, select, xs,
                 sh_out, sh_in, share, send, recv, ksend, krecv, kfwd, ssend, srecv, asend, arecv,
                 sib_in, total, x_in, y_in, x_last, y_last, full, z_in, bsend, brecv, small, local):
    me, z, core, c = where_am_i()
    cx, cy, cd = c + 1 - 2 * (c % 2), c + 2 - 4 * (c // 2), 3 - c
    sib, xn, yn, diag = me + 1 - 2 * core, cx * 2 + core, cy * 2 + core, cd * 2 + core
    chunks = part.shape[0]
    width = part.shape[3]
    half = part.shape[2] // 2
    rows = table.shape[0] * GROUP
    block = chunks * GROUP
    share_tiles = -(-(rows // GROUP) // TABLE_CUTS)
    cuts = [(at, min(share_tiles, rows // GROUP - at)) for at in range(0, rows // GROUP, share_tiles)]
    fetch_table = [
        pltpu.make_async_copy(table.at[pl.ds(at, count)], tab.at[pl.ds(at, count)], small.at[8 + i])
        for i, (at, count) in enumerate(cuts)]
    fetch_small = [
        pltpu.make_async_copy(src, dst, small.at[i])
        for i, (src, dst) in enumerate((
            (routes_in, routes), (gates_in, gates), (ids_in, ids), (wm_in, wm),
            (post_gain_in, post_gain), (in_gain_in, in_gain), (key_gain_in, key_gain)))]
    for one in fetch_small[0:4] + fetch_table + fetch_small[4:7]:
        one.start()
    fetch = [
        None,
        pltpu.make_async_copy(wg_in, wg, local.at[1]),
        pltpu.make_async_copy(wu_in, wu, local.at[2]),
        pltpu.make_async_copy(kw_in, kw, local.at[3]),
    ]
    deep = wd_in.shape[0]
    down_at = 8 * deep

    def fetch_down(j):
        return pltpu.make_async_copy(
            wd_in.at[:, :, pl.ds(j * width, width)], tab.at[pl.ds(j * deep, deep)], local.at[4 + j])

    def leaving(k):
        return pl.ds(down_at + k * 32, 32)

    all_here = greet_all(n, 8, me, z)

    def remote(src, dst, s_sem, r_sem, peer):
        return pltpu.make_async_remote_copy(
            src_ref=src, dst_ref=dst, send_sem=s_sem, recv_sem=r_sem,
            device_id=peer, device_id_type=MESH)

    near = n // 2 - 1
    far = near + core

    def attn_moves(h):
        src = attn.at[:, :, pl.ds(h * width, width)]
        return remote(src, att.at[c], asend.at[h], arecv.at[c], {"expert": 2 * z + h, "vocab": far})

    def attn_stays(h):
        src = attn.at[:, :, pl.ds(h * width, width)]
        return pltpu.make_async_copy(src, att.at[c], arecv.at[c])

    fetch_small[0].wait()
    fetch_small[1].wait()
    gate_of = gates[...].astype(jnp.float32)
    gate_share = gate_of / jnp.sum(gate_of, axis=0, keepdims=True)
    named = routes[...]
    expert_at = lax.broadcasted_iota(jnp.int32, (16, block), 0)
    spread = jnp.zeros((16, block), jnp.float32)
    for k in range(named.shape[0]):
        spread = spread + jnp.where(expert_at == named[k:k + 1, :], gate_share[k:k + 1, :], 0.0)
    sh_out[...] = spread
    own_rows = pl.ds(pl.multiple_of(me * 16, 16), 16)
    sh_in[own_rows, :] = sh_out[...]

    def share_move(d):
        return remote(sh_out, sh_in.at[own_rows], ssend.at[d], srecv.at[me],
                      {"expert": (me + d) % 8})

    tab[rows // GROUP] = jnp.zeros((GROUP, width), tab.dtype)
    r_at = lax.broadcasted_iota(jnp.int32, (GROUP, 128), 0)
    for r in range(GROUP):
        pick[r] = jnp.where(r_at == r, 1.0, 0.0).astype(pick.dtype)
    m_at = lax.broadcasted_iota(jnp.int32, (GROUP, GROUP * GROUP), 0)
    n_at = lax.broadcasted_iota(jnp.int32, (GROUP, GROUP * GROUP), 1)
    select[...] = jnp.where(n_at // GROUP == m_at, 1.0, 0.0).astype(select.dtype)
    all_here()
    for h in range(2):
        stays = (me == 2 * z + h) & (z == far)

        @pl.when(stays)
        def _():
            attn_stays(h).start()

        @pl.when(jnp.logical_not(stays))
        def _():
            attn_moves(h).start()

    for d in range(1, 8):
        share_move(d).start()

    for one in fetch_small[2:7] + fetch_table:
        one.wait()
    for one in fetch[1:]:
        one.start()

    base = z * rows

    def lookup(k):
        def one_side(qq, carry):
            for cc in range(4):
                tiles = []
                for j in range(GROUP):
                    loc = ids[(2 * cc + qq) * block + k * GROUP + j] - base
                    safe = jnp.minimum(jnp.maximum(loc, 0), rows - 1)
                    keep = (loc == safe) & (wm[safe] == 1)
                    tile = jnp.where(keep, jnp.right_shift(safe, 4), rows // GROUP)
                    r = jnp.bitwise_and(safe, 15)
                    src = tab[tile]
                    one = pick[r]
                    tiles.append(src * jnp.concatenate([one] * (width // 128), axis=1))
                stacked = jnp.concatenate(tiles, axis=0)
                got = jnp.dot(select[...], stacked, preferred_element_type=jnp.float32)
                part[k, qq, pl.ds(cc * GROUP, GROUP), :] = got.astype(part.dtype)
            return carry

        lax.fori_loop(0, 2, one_side, 0)

    CHAIN, RISE, XS, YS, SO, D0, D1, SX, SY, SD0, SD1 = 0, 2, 4, 5, 6, 7, 8, 9, 10, 11, 12

    def chain_move(src, k, qq, up):
        return remote(src, zin.at[up, k, qq], send.at[CHAIN + up, k, qq], recv.at[CHAIN + up, k, qq],
                      {"vocab": z - 1 + 2 * up})

    def chain_in(k, qq, up):
        chain_move(zin.at[up, k, qq], k, qq, up).wait_recv()

    def piece(slot, k, qq, lo=0, count=None):
        count = 2 * half if count is None else count
        return every.at[slot, k, qq, pl.ds(lo, count)]

    def to_peer(kind, ref, k, qq, peer):
        return remote(ref, ref, send.at[kind, k, qq], recv.at[kind, k, qq], peer)

    def rise_move(k, qq, up):
        return to_peer(RISE + up, piece(me, k, qq), k, qq, {"vocab": z - 1 + 2 * up})

    def spec_of(kind, k, qq):
        return {
            XS: lambda: (piece(me, k, qq), xn),
            YS: lambda: (piece(me, k, qq), yn),
            SO: lambda: (piece(me, k, qq), sib),
            D0: lambda: (piece(xn, k, qq, 0, half), yn),
            D1: lambda: (piece(yn, k, qq, half, half), xn),
            SX: lambda: (piece(xn, k, qq), sib),
            SY: lambda: (piece(yn, k, qq), sib),
            SD0: lambda: (piece(diag, k, qq, 0, half), sib),
            SD1: lambda: (piece(diag, k, qq, half, half), sib),
        }[kind]()

    def move(kind, k, qq):
        ref, peer = spec_of(kind, k, qq)
        return to_peer(kind, ref, k, qq, {"expert": peer})

    sib_of = {SO: sib, SX: xn + sib - me, SY: yn + sib - me}
    sib_diag = diag + sib - me

    def arrive(kind, ref, k, qq):
        to_peer(kind, ref, k, qq, {"expert": sib}).wait_recv()

    def spread_out(k, qq):
        for kind in (XS, YS, SO):
            move(kind, k, qq).start()

    def make_hidden(k):
        squares = jnp.zeros((4 * half, 1), jnp.float32)
        for slot in range(8):
            v = every[slot, k].reshape(4 * half, width).astype(jnp.float32)
            squares = squares + jnp.sum(v * v, axis=1, keepdims=True)
        inverse = lax.rsqrt(squares * (1.0 / (8 * width)) + 1e-06)
        for slot in range(8):
            columns = pl.ds(slot * width, width)
            v = every[slot, k].reshape(4 * half, width).astype(jnp.float32)
            xs[:, columns] = (v * inverse * post_gain[:, columns]).astype(xs.dtype)
        gate_val = jnp.dot(xs[...], wg[...], preferred_element_type=jnp.float32)
        up_val = jnp.dot(xs[...], wu[...], preferred_element_type=jnp.float32)
        scaled = gate_val / (1.0 + jnp.exp(-gate_val)) * up_val * share[k][:, 0:1]
        hidden = scaled.astype(xs.dtype)
        for j in range(8):
            down = tab[pl.ds(j * deep, deep)].reshape(deep * GROUP, width)
            made = jnp.dot(hidden, down, preferred_element_type=jnp.float32)
            upper, lower = made[0:2 * half], made[2 * half:4 * half]
            stay = jnp.where(core == 0, upper, lower).astype(total.dtype)
            leave = jnp.where(core == 0, lower, upper).astype(total.dtype)
            for cc in range(4):
                total[k, cc, j] = stay[cc * GROUP:(cc + 1) * GROUP]
                tab[down_at + k * 32 + j * 4 + cc] = leave[cc * GROUP:(cc + 1) * GROUP]

    def sharing():
        for d in range(1, 8):
            other = (me + d) % 8
            other_rows = pl.ds(pl.multiple_of(other * 16, 16), 16)
            remote(sh_out, sh_in.at[other_rows], ssend.at[d], srecv.at[other],
                   {"expert": other}).wait_recv()
        turned = sh_in[...].T
        mine = (me * n + z) // 2
        lane = lax.broadcasted_iota(jnp.int32, (block, 128), 1)
        for owner in range(8):
            column = jnp.sum(jnp.where(lane == owner * 16 + mine, turned, 0.0), axis=1, keepdims=True)
            column = jnp.broadcast_to(column, (block, 128))
            at = (owner % 2) * 2 * half + (owner // 2) * GROUP
            for k in range(chunks):
                share[k, pl.ds(at, GROUP), :] = column[k * GROUP:(k + 1) * GROUP, :]

    settle = CHAIN_LAG * (n // 2)
    long = n // 2
    keys_at = settle + KEY_START

    def key_out(k, qq, cc):
        return remote(emb.at[k, cc], kin.at[k, me], ksend.at[k, cc], krecv.at[k],
                      {"expert": 2 * cc + qq})

    def key_next(k, up):
        return remote(kin.at[k], kin.at[k], kfwd.at[k, up], krecv.at[k], {"vocab": z - 1 + 2 * up})

    def away_of(qq):
        offset = z - near - qq
        return jnp.maximum(offset, -offset)

    key_far = away_of(core)

    def outward(qq, run):
        for up in range(2):
            beyond = (z >= near + qq) & (z < n - 1) if up else (z <= near + qq) & (z > 0)

            @pl.when(beyond)
            def _():
                run(up)

    def inside(k):
        return (k >= 0) & (k < chunks)

    def make_keys():
        fetch[3].wait()
        squares = jnp.zeros((block, 1), jnp.float32)
        for slot in range(8):
            v = kin[:, slot].reshape(block, width).astype(jnp.float32)
            squares = squares + jnp.sum(v * v, axis=1, keepdims=True)
        inverse = lax.rsqrt(squares * (1.0 / (8 * width)) + 1e-06)
        raw = jnp.zeros((block, 128), jnp.float32)
        for slot in range(8):
            columns = pl.ds(slot * width, width)
            v = kin[:, slot].reshape(block, width).astype(jnp.float32)
            normed = (v * inverse * in_gain[:, columns]).astype(kw.dtype)
            raw = raw + jnp.dot(normed, kw[columns, :], preferred_element_type=jnp.float32)
        keys[...] = rms_rows(raw, key_gain[...]).astype(keys.dtype)

    def back(kind, src, dst, k, peer):
        return pltpu.make_async_remote_copy(
            src_ref=src, dst_ref=dst, send_sem=bsend.at[kind, k], recv_sem=brecv.at[kind, k],
            device_id=peer, device_id_type=MESH)

    left, right = pl.ds(0, 4), pl.ds(4, 4)

    def sib_move(k):
        return back(0, tab.at[leaving(k)], sib_in.at[k], k, {"expert": sib})

    def first_move(i, k):
        src, dst, peer = (
            lambda: (total.at[k, cd, left], x_in.at[k, 1], xn),
            lambda: (total.at[k, cd, right], y_in.at[k, 1], yn),
            lambda: (total.at[k, cx, left], x_in.at[k, 0], xn),
            lambda: (total.at[k, cy, right], y_in.at[k, 0], yn),
        )[i]()
        return back(1 + i, src, dst, k, {"expert": peer})

    def then_y(k):
        return back(5, total.at[k, cy, left], y_last.at[k], k, {"expert": yn})

    def then_x(k):
        return back(6, total.at[k, cx, right], x_last.at[k], k, {"expert": xn})

    per = 8 // n

    def z_move(d, k):
        peer = (z + d + 1) % n
        return back(7 + d, full.at[k, pl.ds(peer * per, per)], z_in.at[k, d], k, {"vocab": peer})

    def wide(value):
        return value.astype(jnp.float32)

    def add_cores(k):
        sib_move(k).wait_recv()
        for cc in range(4):
            for j in range(8):
                both = wide(total[k, cc, j]) + wide(sib_in[k, j * 4 + cc])
                total[k, cc, j] = both.astype(total.dtype)
        for i in range(4):
            first_move(i, k).start()

    def add_across(k):
        first_move(0, k).wait_recv()
        for j in range(4):
            total[k, cy, j] = (wide(total[k, cy, j]) + wide(x_in[k, 1, j])).astype(total.dtype)
        then_y(k).start()
        first_move(1, k).wait_recv()
        for j in range(4):
            total[k, cx, 4 + j] = (wide(total[k, cx, 4 + j]) + wide(y_in[k, 1, j])).astype(total.dtype)
        then_x(k).start()

    def add_last(k):
        first_move(2, k).wait_recv()
        then_y(k).wait_recv()
        for j in range(4):
            term = wide(total[k, c, j]) + wide(x_in[k, 0, j]) + wide(y_last[k, j])
            full[k, j] = term.astype(full.dtype)
        first_move(3, k).wait_recv()
        then_x(k).wait_recv()
        for j in range(4):
            term = wide(total[k, c, 4 + j]) + wide(y_in[k, 0, j]) + wide(x_last[k, j])
            full[k, 4 + j] = term.astype(full.dtype)
        for d in range(n - 1):
            z_move(d, k).start()

    def add_planes(k):
        for d in range(n - 1):
            z_move(d, k).wait_recv()
        for j in range(per):
            term = wide(full[k, z * per + j])
            for d in range(n - 1):
                term = term + wide(z_in[k, d, j])
            out[k, :, pl.ds(j * width, width)] = term.astype(out.dtype)

    def drain_front(k):
        for qq in range(2):
            for up in range(2):
                @pl.when(z == (0 if up else n - 1))
                def _():
                    chain_move(part.at[k, qq], k, qq, up).wait_send()

            @pl.when(z == near + 1 - qq)
            def _():
                chain_move(part.at[k, qq], k, qq, qq).wait_send()

            outward(qq, lambda up: rise_move(k, qq, up).wait_send())
            for kind in range(XS, SD1 + 1):
                move(kind, k, qq).wait_send()

            @pl.when(away_of(qq) == 0)
            def _():
                for cc in range(4):
                    @pl.when(me != 2 * cc + qq)
                    def _():
                        key_out(k, qq, cc).wait_send()

    def drain_early():
        for d in range(1, 8):
            share_move(d).wait_send()
        for h in range(2):
            @pl.when(jnp.logical_not((me == 2 * z + h) & (z == far)))
            def _():
                attn_moves(h).wait_send()

    def drain_back(k):
        outward(core, lambda up: key_next(k, up).wait_send())
        sib_move(k).wait_send()
        for i in range(4):
            first_move(i, k).wait_send()
        then_x(k).wait_send()
        then_y(k).wait_send()
        for d in range(n - 1):
            z_move(d, k).wait_send()

    def step(s, carry):
        @pl.when(s < chunks)
        def _():
            lookup(s)

        for qq in range(2):
            away = away_of(qq)
            ends = (z == 0) | (z == n - 1)
            relay = (away == 1) & jnp.logical_not(ends)

            for up in range(2):
                @pl.when((s < chunks) & (z == (0 if up else n - 1)))
                def _():
                    chain_move(part.at[s, qq], s, qq, up).start()

            k = s - CHAIN_LAG

            @pl.when(inside(k) & relay)
            def _():
                chain_in(k, qq, qq)
                zin[qq, k, qq] = zin[qq, k, qq] + part[k, qq]
                chain_move(zin.at[qq, k, qq], k, qq, qq).start()

            k1 = s - settle

            @pl.when(inside(k1) & (away == 0))
            def _():
                @pl.when(k1 == 0)
                def _():
                    for cc in range(4):
                        pltpu.make_async_copy(att.at[cc], att.at[cc], arecv.at[cc]).wait()

                chain_in(k1, qq, 1 - qq)
                chain_in(k1, qq, qq)
                for cc in range(4):
                    some = pl.ds(cc * GROUP, GROUP)
                    whole = zin[0, k1, qq, some, :] + zin[1, k1, qq, some, :] + part[k1, qq, some, :]
                    emb[k1, cc] = whole
                    mid = whole.astype(jnp.float32) + att[cc, k1].astype(jnp.float32)
                    every[me, k1, qq, some, :] = mid.astype(every.dtype)
                outward(qq, lambda up: rise_move(k1, qq, up).start())
                spread_out(k1, qq)

            k2 = s - settle - RISE_LAG * away

            @pl.when(inside(k2) & (away > 0))
            def _():
                for up in range(2):
                    @pl.when((z > near + qq) if up else (z < near + qq))
                    def _():
                        rise_move(k2, qq, up).wait_recv()

                outward(qq, lambda up: rise_move(k2, qq, up).start())
                spread_out(k2, qq)

            k3 = k2 - CROSS_LAG

            @pl.when(inside(k3))
            def _():
                arrive(XS, piece(xn, k3, qq), k3, qq)
                move(D0, k3, qq).start()
                move(SX, k3, qq).start()
                arrive(YS, piece(yn, k3, qq), k3, qq)
                move(D1, k3, qq).start()
                move(SY, k3, qq).start()

            k4 = k3 - DIAG_LAG

            @pl.when(inside(k4))
            def _():
                arrive(D0, piece(diag, k4, qq, 0, half), k4, qq)
                move(SD0, k4, qq).start()
                arrive(D1, piece(diag, k4, qq, half, half), k4, qq)
                move(SD1, k4, qq).start()

            k5 = k4 - SIB_LAG

            @pl.when(inside(k5))
            def _():
                for kind, slot in sib_of.items():
                    arrive(kind, piece(slot, k5, qq), k5, qq)
                arrive(SD0, piece(sib_diag, k5, qq, 0, half), k5, qq)
                arrive(SD1, piece(sib_diag, k5, qq, half, half), k5, qq)

            k7 = s - keys_at

            @pl.when(inside(k7) & (away == 0))
            def _():
                for cc in range(4):
                    stays = me == 2 * cc + qq

                    @pl.when(stays)
                    def _():
                        pltpu.make_async_copy(emb.at[k7, cc], kin.at[k7, me], krecv.at[k7]).start()

                    @pl.when(jnp.logical_not(stays))
                    def _():
                        key_out(k7, qq, cc).start()

        k8 = s - keys_at - KEY_LAG * (1 + key_far)

        @pl.when(inside(k8))
        def _():
            pltpu.make_async_copy(kin.at[k8], kin.at[k8], krecv.at[k8]).wait()

            outward(core, lambda up: key_next(k8, up).start())

        k6 = s - settle - RISE_LAG * jnp.maximum(away_of(0), away_of(1)) - CROSS_LAG - DIAG_LAG - SIB_LAG

        @pl.when(s == chunks)
        def _():
            for j in range(8):
                fetch_down(j).start()

        k10 = k6 - HALF_LAG
        k11 = k10 - ADD_LAG
        k12 = k11 - LAST_LAG
        k13 = k12 - OUT_LAG

        for k, stage in ((k10, add_cores), (k11, add_across), (k12, add_last), (k13, add_planes),
                         (k12, drain_front), (k13 - 1, drain_back)):
            @pl.when(inside(k))
            def _():
                stage(k)

        @pl.when(k6 == 0)
        def _():
            fetch[1].wait()
            fetch[2].wait()
            for j in range(8):
                fetch_down(j).wait()
            sharing()

        @pl.when(inside(k6))
        def _():
            make_hidden(k6)
            sib_move(k6).start()

        @pl.when(s == keys_at + KEY_LAG * (1 + long) + chunks - 1)
        def _():
            make_keys()
            drain_early()

        return carry

    steps = max(settle + RISE_LAG * long + CROSS_LAG + DIAG_LAG + SIB_LAG
                + HALF_LAG + ADD_LAG + LAST_LAG + OUT_LAG + chunks + 1,
                keys_at + KEY_LAG * (1 + long) + chunks)
    lax.fori_loop(0, steps, step, 0)


def hand_over(out, keys):
    def kernel(out_in, keys_in, out_ref, keys_ref):
        out_ref[...] = out_in[...]
        keys_ref[...] = keys_in[...]

    vmem = pl.BlockSpec(memory_space=pltpu.VMEM)
    return pl.pallas_call(
        kernel,
        name="hand_over",
        out_shape=tuple(jax.ShapeDtypeStruct(r.shape, r.dtype) for r in (out, keys)),
        in_specs=[vmem, vmem],
        out_specs=(vmem, vmem),
    )(out, keys)


def layer(n, token_ids, word_mask, embed_table, attn_out, in_gain, key_weight, key_gain, post_gain,
          routes, gate_ints, w_gate, w_up, w_down):
    block, columns = attn_out.shape
    rows, width = embed_table.shape
    chunks = block // GROUP
    side = 4 * GROUP
    units = w_gate.shape[1]
    model = 8 * width
    kind = embed_table.dtype
    vmem, anyw = (pl.BlockSpec(memory_space=m) for m in (pltpu.VMEM, pl.ANY))
    dma = pltpu.SemaphoreType.DMA
    tiles = max(rows // GROUP + 1, 8 * units // GROUP + 32 * chunks)
    out, keys = pl.pallas_call(
        lambda *refs: layer_kernel(n, *refs),
        name="embed_and_experts",
        out_shape=(
            jax.ShapeDtypeStruct((chunks, GROUP, model // n), kind),
            jax.ShapeDtypeStruct((block, 128), kind),
        ),
        in_specs=[anyw] * 13,
        out_specs=(vmem, vmem),
        scratch_shapes=[
            pltpu.SMEM(token_ids.shape, token_ids.dtype),
            pltpu.VMEM((1, model), jnp.float32),
            pltpu.VMEM((1, 128), jnp.float32),
            pltpu.VMEM((1, model), jnp.float32),
            pltpu.VMEM((8, block), routes.dtype),
            pltpu.VMEM((8, block), gate_ints.dtype),
            pltpu.SMEM(word_mask.shape, word_mask.dtype),
            pltpu.VMEM((tiles, GROUP, width), kind),
            pltpu.VMEM(w_gate.shape, kind),
            pltpu.VMEM(w_up.shape, kind),
            pltpu.VMEM(key_weight.shape, kind),
            pltpu.VMEM((chunks, 2, side, width), kind),
            pltpu.VMEM((2, chunks, 2, side, width), kind),
            pltpu.VMEM((8, chunks, 2, side, width), kind),
            pltpu.VMEM((4, chunks, GROUP, width), kind),
            pltpu.VMEM((chunks, 4, GROUP, width), kind),
            pltpu.VMEM((chunks, 8, GROUP, width), kind),
            pltpu.VMEM((GROUP, GROUP, 128), kind),
            pltpu.VMEM((GROUP, GROUP * GROUP), kind),
            pltpu.VMEM((2 * side, model), kind),
            pltpu.VMEM((16, block), jnp.float32),
            pltpu.VMEM((128, block), jnp.float32),
            pltpu.VMEM((chunks, 2 * side, 128), jnp.float32),
            dma((13, chunks, 2)),
            dma((13, chunks, 2)),
            dma((chunks, 4)),
            dma((chunks,)),
            dma((chunks, 2)),
            dma((8,)),
            dma((8,)),
            dma((2,)),
            dma((4,)),
            pltpu.VMEM((chunks, 32, GROUP, width), kind),
            pltpu.VMEM((chunks, 4, 8, GROUP, width), kind),
            pltpu.VMEM((chunks, 2, 4, GROUP, width), kind),
            pltpu.VMEM((chunks, 2, 4, GROUP, width), kind),
            pltpu.VMEM((chunks, 4, GROUP, width), kind),
            pltpu.VMEM((chunks, 4, GROUP, width), kind),
            pltpu.VMEM((chunks, 8, GROUP, width), kind),
            pltpu.VMEM((chunks, n - 1, 8 // n, GROUP, width), kind),
            dma((6 + n, chunks)),
            dma((6 + n, chunks)),
            dma((8 + TABLE_CUTS,)),
            dma((13,)),
        ],
        compiler_params=pltpu.CompilerParams(
            collective_id=0, has_side_effects=True, vmem_limit_bytes=63 * 1024 * 1024),
    )(token_ids, word_mask, embed_table.reshape(rows // GROUP, GROUP, width), attn_out.reshape(chunks, GROUP, columns),
      in_gain.reshape(1, -1), key_weight, key_gain.reshape(1, -1), post_gain.reshape(1, -1),
      routes.T, gate_ints.T, w_gate, w_up, w_down.reshape(units // GROUP, GROUP, model))
    return hand_over(out.reshape(block, model // n), keys)


def by_collectives(
    token_ids, word_mask, embed_table, attn_out, in_gain, key_weight, key_gain, post_gain,
    routes, gate_ints, w_gate, w_up, w_down,
):
    n_vocab = lax.axis_size("vocab")
    n_expert = lax.axis_size("expert")
    vocab_rows = embed_table.shape[0]
    experts_total = n_expert * n_vocab // 2
    my_vocab = lax.axis_index("vocab")
    my_expert = (lax.axis_index("expert") * n_vocab + my_vocab) // 2

    gate_share = gate_ints.astype(jnp.float32) / jnp.sum(gate_ints, axis=1, keepdims=True).astype(
        jnp.float32
    )
    onehot = routes[:, :, None] == jnp.arange(experts_total, dtype=jnp.int32)[None, None, :]
    share_of = jnp.sum(jnp.where(onehot, gate_share[:, :, None], 0.0), axis=1)
    all_shares = lax.all_gather(share_of, "expert", axis=0, tiled=True)
    my_share = lax.dynamic_slice_in_dim(all_shares, my_expert, 1, axis=1)

    own_rows = attn_out.shape[0] // n_vocab
    attn_blocks = attn_out.reshape(n_vocab, own_rows, attn_out.shape[1])
    kept = lax.dynamic_index_in_dim(attn_blocks, my_vocab, 0, keepdims=True)
    attn_parts = lax.dynamic_update_slice_in_dim(attn_blocks, kept, my_vocab, 0)
    for d in range(1, n_vocab):
        sent = lax.dynamic_index_in_dim(attn_blocks, (my_vocab + d) % n_vocab, 0, keepdims=True)
        came = lax.ppermute(sent, "vocab", [(i, (i + d) % n_vocab) for i in range(n_vocab)])
        attn_parts = lax.dynamic_update_slice_in_dim(
            attn_parts, came, (my_vocab - d + n_vocab) % n_vocab, 0
        )
    attn_rows = attn_parts.transpose(1, 0, 2).reshape(own_rows, -1)

    ids = token_ids.reshape(n_expert, n_vocab, own_rows).transpose(1, 0, 2).reshape(-1)
    local_ids = ids - my_vocab * vocab_rows
    inside = (local_ids >= 0) & (local_ids < vocab_rows)
    safe_ids = jnp.clip(local_ids, 0, vocab_rows - 1)
    keep_row = inside & (word_mask[safe_ids] == 1)
    partial_value = jnp.where(
        keep_row[:, None], embed_table[safe_ids], jnp.zeros_like(embed_table[:1])
    )
    summed = lax.psum_scatter(partial_value, "vocab", scatter_dimension=0, tiled=True)
    rows = lax.all_to_all(summed, "expert", split_axis=0, concat_axis=1, tiled=True)
    rows = rows.astype(jnp.float32)

    mid_rows = (rows + attn_rows.astype(jnp.float32)).astype(jnp.bfloat16)
    expert_in = rms_rows(mid_rows.astype(jnp.float32), post_gain).astype(jnp.bfloat16)
    normed_rows = rms_rows(rows, in_gain).astype(jnp.bfloat16)
    tokens_in = lax.all_gather(expert_in, ("expert", "vocab"), axis=0, tiled=True)
    key_rows = lax.all_gather(normed_rows, "vocab", axis=0, tiled=True)
    raw_keys = jnp.dot(key_rows, key_weight, preferred_element_type=jnp.float32)
    key_heads = rms_rows(raw_keys, key_gain).astype(jnp.bfloat16)

    gate_val = jnp.dot(tokens_in, w_gate[0], preferred_element_type=jnp.float32)
    up_val = jnp.dot(tokens_in, w_up[0], preferred_element_type=jnp.float32)
    hidden = (jax.nn.silu(gate_val) * up_val).astype(jnp.bfloat16)
    parts = jnp.dot(hidden, w_down[0], preferred_element_type=jnp.float32)
    weighted = (parts * my_share).astype(jnp.bfloat16)
    by_tokens = lax.psum_scatter(weighted, "expert", scatter_dimension=0, tiled=True)
    expert_out = lax.psum_scatter(by_tokens, "vocab", scatter_dimension=1, tiled=True)
    return (expert_out, key_heads)


def by_kernels(
    token_ids, word_mask, embed_table, attn_out, in_gain, key_weight, key_gain, post_gain,
    routes, gate_ints, w_gate, w_up, w_down,
):
    return layer(
        lax.axis_size("vocab"), token_ids, word_mask, embed_table, attn_out, in_gain, key_weight,
        key_gain, post_gain, routes, gate_ints, w_gate[0], w_up[0], w_down[0])


def solution(mesh):
    small = mesh.shape["expert"] == 8 and mesh.shape["vocab"] == 4
    return jax.shard_map(
        by_kernels if small else by_collectives,
        mesh=mesh,
        in_specs=(
            P(),
            P("vocab"),
            P("vocab", "expert"),
            P("expert", "vocab"),
            P(),
            P(None, "vocab"),
            P(),
            P(),
            P("expert", None),
            P("expert", None),
            P(("expert", "vocab"), None, None),
            P(("expert", "vocab"), None, None),
            P(("expert", "vocab"), None, None),
        ),
        out_specs=(P("expert", "vocab"), P("expert", "vocab")),
        check_vma=False,
    )
```

```python
import jax
import jax.numpy as jnp
from jax import lax
from jax.experimental import pallas as pl
from jax.experimental.pallas import tpu as pltpu
from jax.sharding import PartitionSpec as P

MESH = pl.DeviceIdType.MESH
GROUP = 16
TABLE_CUTS = 4
CHAIN_LAG, RISE_LAG, CROSS_LAG, DIAG_LAG, SIB_LAG = 2, 1, 2, 2, 1
KEY_START, KEY_LAG = 4, 2
HALF_LAG, ADD_LAG, LAST_LAG, OUT_LAG = 2, 1, 2, 2


def rms_rows(values, scale_gain):
    inverse_rms = lax.rsqrt(jnp.mean(values * values, axis=-1, keepdims=True) + 1e-06)
    return values * inverse_rms * scale_gain


def where_am_i():
    me = lax.axis_index("expert")
    z = lax.axis_index("vocab")
    return me, z, me % 2, me // 2


def greet_all(n_vocab, n_expert, me, z):
    barrier = pltpu.get_barrier_semaphore()
    total = n_vocab * n_expert
    flat = me * n_vocab + z

    def one(d, carry):
        peer = (flat + d) % total
        pl.semaphore_signal(
            barrier, inc=1,
            device_id={"expert": peer // n_vocab, "vocab": peer % n_vocab},
            device_id_type=MESH)
        return carry

    lax.fori_loop(1, total, one, 0)
    return lambda: pl.semaphore_wait(barrier, total - 1)


def layer_kernel(n, ids_in, wm_in, table, attn, in_gain_in, kw_in, key_gain_in, post_gain_in, routes_in, gates_in,
                 wg_in, wu_in, wd_in, out, keys,
                 ids, in_gain, key_gain, post_gain, routes, gates, wm, tab, wg, wu, kw, part, zin, every, att, emb, kin, pick, select, xs,
                 sh_out, sh_in, share, send, recv, ksend, krecv, kfwd, ssend, srecv, asend, arecv,
                 sib_in, total, x_in, y_in, x_last, y_last, full, z_in, bsend, brecv, small, local):
    me, z, core, c = where_am_i()
    cx, cy, cd = c + 1 - 2 * (c % 2), c + 2 - 4 * (c // 2), 3 - c
    sib, xn, yn, diag = me + 1 - 2 * core, cx * 2 + core, cy * 2 + core, cd * 2 + core
    chunks = part.shape[0]
    width = part.shape[3]
    half = part.shape[2] // 2
    rows = table.shape[0] * GROUP
    block = chunks * GROUP
    share_tiles = -(-(rows // GROUP) // TABLE_CUTS)
    cuts = [(at, min(share_tiles, rows // GROUP - at)) for at in range(0, rows // GROUP, share_tiles)]
    fetch_table = [
        pltpu.make_async_copy(table.at[pl.ds(at, count)], tab.at[pl.ds(at, count)], small.at[8 + i])
        for i, (at, count) in enumerate(cuts)]
    fetch_small = [
        pltpu.make_async_copy(src, dst, small.at[i])
        for i, (src, dst) in enumerate((
            (routes_in, routes), (gates_in, gates), (ids_in, ids), (wm_in, wm),
            (post_gain_in, post_gain), (in_gain_in, in_gain), (key_gain_in, key_gain)))]
    for one in fetch_small[0:4] + fetch_table + fetch_small[4:7]:
        one.start()
    fetch = [
        None,
        pltpu.make_async_copy(wg_in, wg, local.at[1]),
        pltpu.make_async_copy(wu_in, wu, local.at[2]),
        pltpu.make_async_copy(kw_in, kw, local.at[3]),
    ]
    deep = wd_in.shape[0]
    down_at = 8 * deep

    def fetch_down(j):
        return pltpu.make_async_copy(
            wd_in.at[:, :, pl.ds(j * width, width)], tab.at[pl.ds(j * deep, deep)], local.at[4 + j])

    def leaving(k):
        return pl.ds(down_at + k * 32, 32)

    all_here = greet_all(n, 8, me, z)

    def remote(src, dst, s_sem, r_sem, peer):
        return pltpu.make_async_remote_copy(
            src_ref=src, dst_ref=dst, send_sem=s_sem, recv_sem=r_sem,
            device_id=peer, device_id_type=MESH)

    near = n // 2 - 1
    far = near + core

    def attn_moves(h):
        src = attn.at[:, :, pl.ds(h * width, width)]
        return remote(src, att.at[c], asend.at[h], arecv.at[c], {"expert": 2 * z + h, "vocab": far})

    def attn_stays(h):
        src = attn.at[:, :, pl.ds(h * width, width)]
        return pltpu.make_async_copy(src, att.at[c], arecv.at[c])

    fetch_small[0].wait()
    fetch_small[1].wait()
    gate_of = gates[...].astype(jnp.float32)
    gate_share = gate_of / jnp.sum(gate_of, axis=0, keepdims=True)
    named = routes[...]
    expert_at = lax.broadcasted_iota(jnp.int32, (16, block), 0)
    spread = jnp.zeros((16, block), jnp.float32)
    for k in range(named.shape[0]):
        spread = spread + jnp.where(expert_at == named[k:k + 1, :], gate_share[k:k + 1, :], 0.0)
    sh_out[...] = spread
    own_rows = pl.ds(pl.multiple_of(me * 16, 16), 16)
    sh_in[own_rows, :] = sh_out[...]

    def share_move(d):
        return remote(sh_out, sh_in.at[own_rows], ssend.at[d], srecv.at[me],
                      {"expert": (me + d) % 8})

    tab[rows // GROUP] = jnp.zeros((GROUP, width), tab.dtype)
    r_at = lax.broadcasted_iota(jnp.int32, (GROUP, 128), 0)
    for r in range(GROUP):
        pick[r] = jnp.where(r_at == r, 1.0, 0.0).astype(pick.dtype)
    m_at = lax.broadcasted_iota(jnp.int32, (GROUP, GROUP * GROUP), 0)
    n_at = lax.broadcasted_iota(jnp.int32, (GROUP, GROUP * GROUP), 1)
    select[...] = jnp.where(n_at // GROUP == m_at, 1.0, 0.0).astype(select.dtype)
    all_here()
    for h in range(2):
        stays = (me == 2 * z + h) & (z == far)

        @pl.when(stays)
        def _():
            attn_stays(h).start()

        @pl.when(jnp.logical_not(stays))
        def _():
            attn_moves(h).start()

    for d in range(1, 8):
        share_move(d).start()

    for one in fetch_small[2:7] + fetch_table:
        one.wait()
    for one in fetch[1:]:
        one.start()

    base = z * rows

    def lookup(k):
        def one_side(qq, carry):
            for cc in range(4):
                tiles = []
                for j in range(GROUP):
                    loc = ids[(2 * cc + qq) * block + k * GROUP + j] - base
                    safe = jnp.minimum(jnp.maximum(loc, 0), rows - 1)
                    keep = (loc == safe) & (wm[safe] == 1)
                    tile = jnp.where(keep, jnp.right_shift(safe, 4), rows // GROUP)
                    r = jnp.bitwise_and(safe, 15)
                    src = tab[tile]
                    one = pick[r]
                    tiles.append(src * jnp.concatenate([one] * (width // 128), axis=1))
                stacked = jnp.concatenate(tiles, axis=0)
                got = jnp.dot(select[...], stacked, preferred_element_type=jnp.float32)
                part[k, qq, pl.ds(cc * GROUP, GROUP), :] = got.astype(part.dtype)
            return carry

        lax.fori_loop(0, 2, one_side, 0)

    CHAIN, RISE, XS, YS, SO, D0, D1, SX, SY, SD0, SD1 = 0, 2, 4, 5, 6, 7, 8, 9, 10, 11, 12

    def chain_move(src, k, qq, up):
        return remote(src, zin.at[up, k, qq], send.at[CHAIN + up, k, qq], recv.at[CHAIN + up, k, qq],
                      {"vocab": z - 1 + 2 * up})

    def chain_in(k, qq, up):
        chain_move(zin.at[up, k, qq], k, qq, up).wait_recv()

    def piece(slot, k, qq, lo=0, count=None):
        count = 2 * half if count is None else count
        return every.at[slot, k, qq, pl.ds(lo, count)]

    def to_peer(kind, ref, k, qq, peer):
        return remote(ref, ref, send.at[kind, k, qq], recv.at[kind, k, qq], peer)

    def rise_move(k, qq, up):
        return to_peer(RISE + up, piece(me, k, qq), k, qq, {"vocab": z - 1 + 2 * up})

    def spec_of(kind, k, qq):
        return {
            XS: lambda: (piece(me, k, qq), xn),
            YS: lambda: (piece(me, k, qq), yn),
            SO: lambda: (piece(me, k, qq), sib),
            D0: lambda: (piece(xn, k, qq, 0, half), yn),
            D1: lambda: (piece(yn, k, qq, half, half), xn),
            SX: lambda: (piece(xn, k, qq), sib),
            SY: lambda: (piece(yn, k, qq), sib),
            SD0: lambda: (piece(diag, k, qq, 0, half), sib),
            SD1: lambda: (piece(diag, k, qq, half, half), sib),
        }[kind]()

    def move(kind, k, qq):
        ref, peer = spec_of(kind, k, qq)
        return to_peer(kind, ref, k, qq, {"expert": peer})

    sib_of = {SO: sib, SX: xn + sib - me, SY: yn + sib - me}
    sib_diag = diag + sib - me

    def arrive(kind, ref, k, qq):
        to_peer(kind, ref, k, qq, {"expert": sib}).wait_recv()

    def spread_out(k, qq):
        for kind in (XS, YS, SO):
            move(kind, k, qq).start()

    def make_hidden(k):
        squares = jnp.zeros((4 * half, 1), jnp.float32)
        for slot in range(8):
            v = every[slot, k].reshape(4 * half, width).astype(jnp.float32)
            squares = squares + jnp.sum(v * v, axis=1, keepdims=True)
        inverse = lax.rsqrt(squares * (1.0 / (8 * width)) + 1e-06)
        for slot in range(8):
            columns = pl.ds(slot * width, width)
            v = every[slot, k].reshape(4 * half, width).astype(jnp.float32)
            xs[:, columns] = (v * inverse * post_gain[:, columns]).astype(xs.dtype)
        gate_val = jnp.dot(xs[...], wg[...], preferred_element_type=jnp.float32)
        up_val = jnp.dot(xs[...], wu[...], preferred_element_type=jnp.float32)
        scaled = gate_val / (1.0 + jnp.exp(-gate_val)) * up_val * share[k][:, 0:1]
        hidden = scaled.astype(xs.dtype)
        for j in range(8):
            down = tab[pl.ds(j * deep, deep)].reshape(deep * GROUP, width)
            made = jnp.dot(hidden, down, preferred_element_type=jnp.float32)
            upper, lower = made[0:2 * half], made[2 * half:4 * half]
            stay = jnp.where(core == 0, upper, lower).astype(total.dtype)
            leave = jnp.where(core == 0, lower, upper).astype(total.dtype)
            for cc in range(4):
                total[k, cc, j] = stay[cc * GROUP:(cc + 1) * GROUP]
                tab[down_at + k * 32 + j * 4 + cc] = leave[cc * GROUP:(cc + 1) * GROUP]

    def sharing():
        for d in range(1, 8):
            other = (me + d) % 8
            other_rows = pl.ds(pl.multiple_of(other * 16, 16), 16)
            remote(sh_out, sh_in.at[other_rows], ssend.at[d], srecv.at[other],
                   {"expert": other}).wait_recv()
        turned = sh_in[...].T
        mine = (me * n + z) // 2
        lane = lax.broadcasted_iota(jnp.int32, (block, 128), 1)
        for owner in range(8):
            column = jnp.sum(jnp.where(lane == owner * 16 + mine, turned, 0.0), axis=1, keepdims=True)
            column = jnp.broadcast_to(column, (block, 128))
            at = (owner % 2) * 2 * half + (owner // 2) * GROUP
            for k in range(chunks):
                share[k, pl.ds(at, GROUP), :] = column[k * GROUP:(k + 1) * GROUP, :]

    settle = CHAIN_LAG * (n // 2)
    long = n // 2
    keys_at = settle + KEY_START

    def key_out(k, qq, cc):
        return remote(emb.at[k, cc], kin.at[k, me], ksend.at[k, cc], krecv.at[k],
                      {"expert": 2 * cc + qq})

    def key_next(k, up):
        return remote(kin.at[k], kin.at[k], kfwd.at[k, up], krecv.at[k], {"vocab": z - 1 + 2 * up})

    def away_of(qq):
        offset = z - near - qq
        return jnp.maximum(offset, -offset)

    key_far = away_of(core)

    def outward(qq, run):
        for up in range(2):
            beyond = (z >= near + qq) & (z < n - 1) if up else (z <= near + qq) & (z > 0)

            @pl.when(beyond)
            def _():
                run(up)

    def inside(k):
        return (k >= 0) & (k < chunks)

    def make_keys():
        fetch[3].wait()
        squares = jnp.zeros((block, 1), jnp.float32)
        for slot in range(8):
            v = kin[:, slot].reshape(block, width).astype(jnp.float32)
            squares = squares + jnp.sum(v * v, axis=1, keepdims=True)
        inverse = lax.rsqrt(squares * (1.0 / (8 * width)) + 1e-06)
        raw = jnp.zeros((block, 128), jnp.float32)
        for slot in range(8):
            columns = pl.ds(slot * width, width)
            v = kin[:, slot].reshape(block, width).astype(jnp.float32)
            normed = (v * inverse * in_gain[:, columns]).astype(kw.dtype)
            raw = raw + jnp.dot(normed, kw[columns, :], preferred_element_type=jnp.float32)
        keys[...] = rms_rows(raw, key_gain[...]).astype(keys.dtype)

    def back(kind, src, dst, k, peer):
        return pltpu.make_async_remote_copy(
            src_ref=src, dst_ref=dst, send_sem=bsend.at[kind, k], recv_sem=brecv.at[kind, k],
            device_id=peer, device_id_type=MESH)

    left, right = pl.ds(0, 4), pl.ds(4, 4)

    def sib_move(k):
        return back(0, tab.at[leaving(k)], sib_in.at[k], k, {"expert": sib})

    def first_move(i, k):
        src, dst, peer = (
            lambda: (total.at[k, cd, left], x_in.at[k, 1], xn),
            lambda: (total.at[k, cd, right], y_in.at[k, 1], yn),
            lambda: (total.at[k, cx, left], x_in.at[k, 0], xn),
            lambda: (total.at[k, cy, right], y_in.at[k, 0], yn),
        )[i]()
        return back(1 + i, src, dst, k, {"expert": peer})

    def then_y(k):
        return back(5, total.at[k, cy, left], y_last.at[k], k, {"expert": yn})

    def then_x(k):
        return back(6, total.at[k, cx, right], x_last.at[k], k, {"expert": xn})

    per = 8 // n

    def z_move(d, k):
        peer = (z + d + 1) % n
        return back(7 + d, full.at[k, pl.ds(peer * per, per)], z_in.at[k, d], k, {"vocab": peer})

    def wide(value):
        return value.astype(jnp.float32)

    def add_cores(k):
        sib_move(k).wait_recv()
        for cc in range(4):
            for j in range(8):
                both = wide(total[k, cc, j]) + wide(sib_in[k, j * 4 + cc])
                total[k, cc, j] = both.astype(total.dtype)
        for i in range(4):
            first_move(i, k).start()

    def add_across(k):
        first_move(0, k).wait_recv()
        for j in range(4):
            total[k, cy, j] = (wide(total[k, cy, j]) + wide(x_in[k, 1, j])).astype(total.dtype)
        then_y(k).start()
        first_move(1, k).wait_recv()
        for j in range(4):
            total[k, cx, 4 + j] = (wide(total[k, cx, 4 + j]) + wide(y_in[k, 1, j])).astype(total.dtype)
        then_x(k).start()

    def add_last(k):
        first_move(2, k).wait_recv()
        then_y(k).wait_recv()
        for j in range(4):
            term = wide(total[k, c, j]) + wide(x_in[k, 0, j]) + wide(y_last[k, j])
            full[k, j] = term.astype(full.dtype)
        first_move(3, k).wait_recv()
        then_x(k).wait_recv()
        for j in range(4):
            term = wide(total[k, c, 4 + j]) + wide(y_in[k, 0, j]) + wide(x_last[k, j])
            full[k, 4 + j] = term.astype(full.dtype)
        for d in range(n - 1):
            z_move(d, k).start()

    def add_planes(k):
        for d in range(n - 1):
            z_move(d, k).wait_recv()
        for j in range(per):
            term = wide(full[k, z * per + j])
            for d in range(n - 1):
                term = term + wide(z_in[k, d, j])
            out[k, :, pl.ds(j * width, width)] = term.astype(out.dtype)

    def drain_front(k):
        for qq in range(2):
            for up in range(2):
                @pl.when(z == (0 if up else n - 1))
                def _():
                    chain_move(part.at[k, qq], k, qq, up).wait_send()

            @pl.when(z == near + 1 - qq)
            def _():
                chain_move(part.at[k, qq], k, qq, qq).wait_send()

            outward(qq, lambda up: rise_move(k, qq, up).wait_send())
            for kind in range(XS, SD1 + 1):
                move(kind, k, qq).wait_send()

            @pl.when(away_of(qq) == 0)
            def _():
                for cc in range(4):
                    @pl.when(me != 2 * cc + qq)
                    def _():
                        key_out(k, qq, cc).wait_send()

    def drain_early():
        for d in range(1, 8):
            share_move(d).wait_send()
        for h in range(2):
            @pl.when(jnp.logical_not((me == 2 * z + h) & (z == far)))
            def _():
                attn_moves(h).wait_send()

    def drain_back(k):
        outward(core, lambda up: key_next(k, up).wait_send())
        sib_move(k).wait_send()
        for i in range(4):
            first_move(i, k).wait_send()
        then_x(k).wait_send()
        then_y(k).wait_send()
        for d in range(n - 1):
            z_move(d, k).wait_send()

    def step(s, carry):
        @pl.when(s < chunks)
        def _():
            lookup(s)

        for qq in range(2):
            away = away_of(qq)
            ends = (z == 0) | (z == n - 1)
            relay = (away == 1) & jnp.logical_not(ends)

            for up in range(2):
                @pl.when((s < chunks) & (z == (0 if up else n - 1)))
                def _():
                    chain_move(part.at[s, qq], s, qq, up).start()

            k = s - CHAIN_LAG

            @pl.when(inside(k) & relay)
            def _():
                chain_in(k, qq, qq)
                zin[qq, k, qq] = zin[qq, k, qq] + part[k, qq]
                chain_move(zin.at[qq, k, qq], k, qq, qq).start()

            k1 = s - settle

            @pl.when(inside(k1) & (away == 0))
            def _():
                @pl.when(k1 == 0)
                def _():
                    for cc in range(4):
                        pltpu.make_async_copy(att.at[cc], att.at[cc], arecv.at[cc]).wait()

                chain_in(k1, qq, 1 - qq)
                chain_in(k1, qq, qq)
                for cc in range(4):
                    some = pl.ds(cc * GROUP, GROUP)
                    whole = zin[0, k1, qq, some, :] + zin[1, k1, qq, some, :] + part[k1, qq, some, :]
                    emb[k1, cc] = whole
                    mid = whole.astype(jnp.float32) + att[cc, k1].astype(jnp.float32)
                    every[me, k1, qq, some, :] = mid.astype(every.dtype)
                outward(qq, lambda up: rise_move(k1, qq, up).start())
                spread_out(k1, qq)

        for qq in range(2):
            away = away_of(qq)
            k2 = s - settle - RISE_LAG * away

            @pl.when(inside(k2) & (away > 0))
            def _():
                for up in range(2):
                    @pl.when((z > near + qq) if up else (z < near + qq))
                    def _():
                        rise_move(k2, qq, up).wait_recv()

                outward(qq, lambda up: rise_move(k2, qq, up).start())
                spread_out(k2, qq)

        for qq in range(2):
            away = away_of(qq)
            k2 = s - settle - RISE_LAG * away
            k3 = k2 - CROSS_LAG

            @pl.when(inside(k3))
            def _():
                arrive(XS, piece(xn, k3, qq), k3, qq)
                move(D0, k3, qq).start()
                move(SX, k3, qq).start()
                arrive(YS, piece(yn, k3, qq), k3, qq)
                move(D1, k3, qq).start()
                move(SY, k3, qq).start()

        for qq in range(2):
            away = away_of(qq)
            k2 = s - settle - RISE_LAG * away
            k3 = k2 - CROSS_LAG
            k4 = k3 - DIAG_LAG

            @pl.when(inside(k4))
            def _():
                arrive(D0, piece(diag, k4, qq, 0, half), k4, qq)
                move(SD0, k4, qq).start()
                arrive(D1, piece(diag, k4, qq, half, half), k4, qq)
                move(SD1, k4, qq).start()

        for qq in range(2):
            away = away_of(qq)
            k2 = s - settle - RISE_LAG * away
            k3 = k2 - CROSS_LAG
            k4 = k3 - DIAG_LAG
            k5 = k4 - SIB_LAG

            @pl.when(inside(k5))
            def _():
                for kind, slot in sib_of.items():
                    arrive(kind, piece(slot, k5, qq), k5, qq)
                arrive(SD0, piece(sib_diag, k5, qq, 0, half), k5, qq)
                arrive(SD1, piece(sib_diag, k5, qq, half, half), k5, qq)

        for qq in range(2):
            away = away_of(qq)
            k7 = s - keys_at

            @pl.when(inside(k7) & (away == 0))
            def _():
                for cc in range(4):
                    stays = me == 2 * cc + qq

                    @pl.when(stays)
                    def _():
                        pltpu.make_async_copy(emb.at[k7, cc], kin.at[k7, me], krecv.at[k7]).start()

                    @pl.when(jnp.logical_not(stays))
                    def _():
                        key_out(k7, qq, cc).start()

        k8 = s - keys_at - KEY_LAG * (1 + key_far)

        @pl.when(inside(k8))
        def _():
            pltpu.make_async_copy(kin.at[k8], kin.at[k8], krecv.at[k8]).wait()

            outward(core, lambda up: key_next(k8, up).start())

        k6 = s - settle - RISE_LAG * jnp.maximum(away_of(0), away_of(1)) - CROSS_LAG - DIAG_LAG - SIB_LAG

        @pl.when(s == chunks)
        def _():
            for j in range(8):
                fetch_down(j).start()

        k10 = k6 - HALF_LAG
        k11 = k10 - ADD_LAG
        k12 = k11 - LAST_LAG
        k13 = k12 - OUT_LAG

        for k, stage in ((k10, add_cores), (k11, add_across), (k12, add_last), (k13, add_planes),
                         (k12, drain_front), (k13 - 1, drain_back)):
            @pl.when(inside(k))
            def _():
                stage(k)

        @pl.when(k6 == 0)
        def _():
            fetch[1].wait()
            fetch[2].wait()
            for j in range(8):
                fetch_down(j).wait()
            sharing()

        @pl.when(inside(k6))
        def _():
            make_hidden(k6)
            sib_move(k6).start()

        @pl.when(s == keys_at + KEY_LAG * (1 + long) + chunks - 1)
        def _():
            make_keys()
            drain_early()

        return carry

    steps = max(settle + RISE_LAG * long + CROSS_LAG + DIAG_LAG + SIB_LAG
                + HALF_LAG + ADD_LAG + LAST_LAG + OUT_LAG + chunks + 1,
                keys_at + KEY_LAG * (1 + long) + chunks)
    lax.fori_loop(0, steps, step, 0)


def hand_over(out, keys):
    def kernel(out_in, keys_in, out_ref, keys_ref):
        out_ref[...] = out_in[...]
        keys_ref[...] = keys_in[...]

    vmem = pl.BlockSpec(memory_space=pltpu.VMEM)
    return pl.pallas_call(
        kernel,
        name="hand_over",
        out_shape=tuple(jax.ShapeDtypeStruct(r.shape, r.dtype) for r in (out, keys)),
        in_specs=[vmem, vmem],
        out_specs=(vmem, vmem),
    )(out, keys)


def layer(n, token_ids, word_mask, embed_table, attn_out, in_gain, key_weight, key_gain, post_gain,
          routes, gate_ints, w_gate, w_up, w_down):
    block, columns = attn_out.shape
    rows, width = embed_table.shape
    chunks = block // GROUP
    side = 4 * GROUP
    units = w_gate.shape[1]
    model = 8 * width
    kind = embed_table.dtype
    vmem, anyw = (pl.BlockSpec(memory_space=m) for m in (pltpu.VMEM, pl.ANY))
    dma = pltpu.SemaphoreType.DMA
    tiles = max(rows // GROUP + 1, 8 * units // GROUP + 32 * chunks)
    out, keys = pl.pallas_call(
        lambda *refs: layer_kernel(n, *refs),
        name="embed_and_experts",
        out_shape=(
            jax.ShapeDtypeStruct((chunks, GROUP, model // n), kind),
            jax.ShapeDtypeStruct((block, 128), kind),
        ),
        in_specs=[anyw] * 13,
        out_specs=(vmem, vmem),
        scratch_shapes=[
            pltpu.SMEM(token_ids.shape, token_ids.dtype),
            pltpu.VMEM((1, model), jnp.float32),
            pltpu.VMEM((1, 128), jnp.float32),
            pltpu.VMEM((1, model), jnp.float32),
            pltpu.VMEM((8, block), routes.dtype),
            pltpu.VMEM((8, block), gate_ints.dtype),
            pltpu.SMEM(word_mask.shape, word_mask.dtype),
            pltpu.VMEM((tiles, GROUP, width), kind),
            pltpu.VMEM(w_gate.shape, kind),
            pltpu.VMEM(w_up.shape, kind),
            pltpu.VMEM(key_weight.shape, kind),
            pltpu.VMEM((chunks, 2, side, width), kind),
            pltpu.VMEM((2, chunks, 2, side, width), kind),
            pltpu.VMEM((8, chunks, 2, side, width), kind),
            pltpu.VMEM((4, chunks, GROUP, width), kind),
            pltpu.VMEM((chunks, 4, GROUP, width), kind),
            pltpu.VMEM((chunks, 8, GROUP, width), kind),
            pltpu.VMEM((GROUP, GROUP, 128), kind),
            pltpu.VMEM((GROUP, GROUP * GROUP), kind),
            pltpu.VMEM((2 * side, model), kind),
            pltpu.VMEM((16, block), jnp.float32),
            pltpu.VMEM((128, block), jnp.float32),
            pltpu.VMEM((chunks, 2 * side, 128), jnp.float32),
            dma((13, chunks, 2)),
            dma((13, chunks, 2)),
            dma((chunks, 4)),
            dma((chunks,)),
            dma((chunks, 2)),
            dma((8,)),
            dma((8,)),
            dma((2,)),
            dma((4,)),
            pltpu.VMEM((chunks, 32, GROUP, width), kind),
            pltpu.VMEM((chunks, 4, 8, GROUP, width), kind),
            pltpu.VMEM((chunks, 2, 4, GROUP, width), kind),
            pltpu.VMEM((chunks, 2, 4, GROUP, width), kind),
            pltpu.VMEM((chunks, 4, GROUP, width), kind),
            pltpu.VMEM((chunks, 4, GROUP, width), kind),
            pltpu.VMEM((chunks, 8, GROUP, width), kind),
            pltpu.VMEM((chunks, n - 1, 8 // n, GROUP, width), kind),
            dma((6 + n, chunks)),
            dma((6 + n, chunks)),
            dma((8 + TABLE_CUTS,)),
            dma((13,)),
        ],
        compiler_params=pltpu.CompilerParams(
            collective_id=0, has_side_effects=True, vmem_limit_bytes=63 * 1024 * 1024),
    )(token_ids, word_mask, embed_table.reshape(rows // GROUP, GROUP, width), attn_out.reshape(chunks, GROUP, columns),
      in_gain.reshape(1, -1), key_weight, key_gain.reshape(1, -1), post_gain.reshape(1, -1),
      routes.T, gate_ints.T, w_gate, w_up, w_down.reshape(units // GROUP, GROUP, model))
    return hand_over(out.reshape(block, model // n), keys)


def by_collectives(
    token_ids, word_mask, embed_table, attn_out, in_gain, key_weight, key_gain, post_gain,
    routes, gate_ints, w_gate, w_up, w_down,
):
    n_vocab = lax.axis_size("vocab")
    n_expert = lax.axis_size("expert")
    vocab_rows = embed_table.shape[0]
    experts_total = n_expert * n_vocab // 2
    my_vocab = lax.axis_index("vocab")
    my_expert = (lax.axis_index("expert") * n_vocab + my_vocab) // 2

    gate_share = gate_ints.astype(jnp.float32) / jnp.sum(gate_ints, axis=1, keepdims=True).astype(
        jnp.float32
    )
    onehot = routes[:, :, None] == jnp.arange(experts_total, dtype=jnp.int32)[None, None, :]
    share_of = jnp.sum(jnp.where(onehot, gate_share[:, :, None], 0.0), axis=1)
    all_shares = lax.all_gather(share_of, "expert", axis=0, tiled=True)
    my_share = lax.dynamic_slice_in_dim(all_shares, my_expert, 1, axis=1)

    own_rows = attn_out.shape[0] // n_vocab
    attn_blocks = attn_out.reshape(n_vocab, own_rows, attn_out.shape[1])
    kept = lax.dynamic_index_in_dim(attn_blocks, my_vocab, 0, keepdims=True)
    attn_parts = lax.dynamic_update_slice_in_dim(attn_blocks, kept, my_vocab, 0)
    for d in range(1, n_vocab):
        sent = lax.dynamic_index_in_dim(attn_blocks, (my_vocab + d) % n_vocab, 0, keepdims=True)
        came = lax.ppermute(sent, "vocab", [(i, (i + d) % n_vocab) for i in range(n_vocab)])
        attn_parts = lax.dynamic_update_slice_in_dim(
            attn_parts, came, (my_vocab - d + n_vocab) % n_vocab, 0
        )
    attn_rows = attn_parts.transpose(1, 0, 2).reshape(own_rows, -1)

    ids = token_ids.reshape(n_expert, n_vocab, own_rows).transpose(1, 0, 2).reshape(-1)
    local_ids = ids - my_vocab * vocab_rows
    inside = (local_ids >= 0) & (local_ids < vocab_rows)
    safe_ids = jnp.clip(local_ids, 0, vocab_rows - 1)
    keep_row = inside & (word_mask[safe_ids] == 1)
    partial_value = jnp.where(
        keep_row[:, None], embed_table[safe_ids], jnp.zeros_like(embed_table[:1])
    )
    summed = lax.psum_scatter(partial_value, "vocab", scatter_dimension=0, tiled=True)
    rows = lax.all_to_all(summed, "expert", split_axis=0, concat_axis=1, tiled=True)
    rows = rows.astype(jnp.float32)

    mid_rows = (rows + attn_rows.astype(jnp.float32)).astype(jnp.bfloat16)
    expert_in = rms_rows(mid_rows.astype(jnp.float32), post_gain).astype(jnp.bfloat16)
    normed_rows = rms_rows(rows, in_gain).astype(jnp.bfloat16)
    tokens_in = lax.all_gather(expert_in, ("expert", "vocab"), axis=0, tiled=True)
    key_rows = lax.all_gather(normed_rows, "vocab", axis=0, tiled=True)
    raw_keys = jnp.dot(key_rows, key_weight, preferred_element_type=jnp.float32)
    key_heads = rms_rows(raw_keys, key_gain).astype(jnp.bfloat16)

    gate_val = jnp.dot(tokens_in, w_gate[0], preferred_element_type=jnp.float32)
    up_val = jnp.dot(tokens_in, w_up[0], preferred_element_type=jnp.float32)
    hidden = (jax.nn.silu(gate_val) * up_val).astype(jnp.bfloat16)
    parts = jnp.dot(hidden, w_down[0], preferred_element_type=jnp.float32)
    weighted = (parts * my_share).astype(jnp.bfloat16)
    by_tokens = lax.psum_scatter(weighted, "expert", scatter_dimension=0, tiled=True)
    expert_out = lax.psum_scatter(by_tokens, "vocab", scatter_dimension=1, tiled=True)
    return (expert_out, key_heads)


def by_kernels(
    token_ids, word_mask, embed_table, attn_out, in_gain, key_weight, key_gain, post_gain,
    routes, gate_ints, w_gate, w_up, w_down,
):
    return layer(
        lax.axis_size("vocab"), token_ids, word_mask, embed_table, attn_out, in_gain, key_weight,
        key_gain, post_gain, routes, gate_ints, w_gate[0], w_up[0], w_down[0])


def solution(mesh):
    small = mesh.shape["expert"] == 8 and mesh.shape["vocab"] == 4
    return jax.shard_map(
        by_kernels if small else by_collectives,
        mesh=mesh,
        in_specs=(
            P(),
            P("vocab"),
            P("vocab", "expert"),
            P("expert", "vocab"),
            P(),
            P(None, "vocab"),
            P(),
            P(),
            P("expert", None),
            P("expert", None),
            P(("expert", "vocab"), None, None),
            P(("expert", "vocab"), None, None),
            P(("expert", "vocab"), None, None),
        ),
        out_specs=(P("expert", "vocab"), P("expert", "vocab")),
        check_vma=False,
    )
```

```python
import jax
import jax.numpy as jnp
from jax import lax
from jax.experimental import pallas as pl
from jax.experimental.pallas import tpu as pltpu
from jax.sharding import PartitionSpec as P

MESH = pl.DeviceIdType.MESH
GROUP = 16
TABLE_CUTS = 4
CHAIN_LAG, RISE_LAG, CROSS_LAG, DIAG_LAG, SIB_LAG = 2, 1, 2, 2, 1
KEY_START, KEY_LAG = 4, 2
HALF_LAG, ADD_LAG, LAST_LAG, OUT_LAG = 2, 1, 2, 2


def rms_rows(values, scale_gain):
    inverse_rms = lax.rsqrt(jnp.mean(values * values, axis=-1, keepdims=True) + 1e-06)
    return values * inverse_rms * scale_gain


def where_am_i():
    me = lax.axis_index("expert")
    z = lax.axis_index("vocab")
    return me, z, me % 2, me // 2


def greet_all(n_vocab, n_expert, me, z):
    barrier = pltpu.get_barrier_semaphore()
    total = n_vocab * n_expert
    flat = me * n_vocab + z

    def one(d, carry):
        peer = (flat + d) % total
        pl.semaphore_signal(
            barrier, inc=1,
            device_id={"expert": peer // n_vocab, "vocab": peer % n_vocab},
            device_id_type=MESH)
        return carry

    lax.fori_loop(1, total, one, 0)
    return lambda: pl.semaphore_wait(barrier, total - 1)


def layer_kernel(n, ids_in, wm_in, table, attn, in_gain_in, kw_in, key_gain_in, post_gain_in, routes_in, gates_in,
                 wg_in, wu_in, wd_in, out, keys,
                 ids, in_gain, key_gain, post_gain, routes, gates, wm, tab, wg, wu, kw, part, zin, every, att, emb, kin, pick, select, xs,
                 sh_out, sh_in, share, send, recv, ksend, krecv, kfwd, ssend, srecv, asend, arecv,
                 sib_in, total, x_in, y_in, x_last, y_last, full, z_in, bsend, brecv, small, local):
    me, z, core, c = where_am_i()
    cx, cy, cd = c + 1 - 2 * (c % 2), c + 2 - 4 * (c // 2), 3 - c
    sib, xn, yn, diag = me + 1 - 2 * core, cx * 2 + core, cy * 2 + core, cd * 2 + core
    chunks = part.shape[0]
    width = part.shape[3]
    half = part.shape[2] // 2
    rows = table.shape[0] * GROUP
    block = chunks * GROUP
    share_tiles = -(-(rows // GROUP) // TABLE_CUTS)
    cuts = [(at, min(share_tiles, rows // GROUP - at)) for at in range(0, rows // GROUP, share_tiles)]
    fetch_table = [
        pltpu.make_async_copy(table.at[pl.ds(at, count)], tab.at[pl.ds(at, count)], small.at[8 + i])
        for i, (at, count) in enumerate(cuts)]
    fetch_small = [
        pltpu.make_async_copy(src, dst, small.at[i])
        for i, (src, dst) in enumerate((
            (routes_in, routes), (gates_in, gates), (ids_in, ids), (wm_in, wm),
            (post_gain_in, post_gain), (in_gain_in, in_gain), (key_gain_in, key_gain)))]
    for one in fetch_small[0:4] + fetch_table + fetch_small[4:7]:
        one.start()
    fetch = [
        None,
        pltpu.make_async_copy(wg_in, wg, local.at[1]),
        pltpu.make_async_copy(wu_in, wu, local.at[2]),
        pltpu.make_async_copy(kw_in, kw, local.at[3]),
    ]
    deep = wd_in.shape[0]
    down_at = 8 * deep

    def fetch_down(j):
        return pltpu.make_async_copy(
            wd_in.at[:, :, pl.ds(j * width, width)], tab.at[pl.ds(j * deep, deep)], local.at[4 + j])

    def leaving(k):
        return pl.ds(down_at + k * 32, 32)

    all_here = greet_all(n, 8, me, z)

    def remote(src, dst, s_sem, r_sem, peer):
        return pltpu.make_async_remote_copy(
            src_ref=src, dst_ref=dst, send_sem=s_sem, recv_sem=r_sem,
            device_id=peer, device_id_type=MESH)

    near = n // 2 - 1
    far = near + core

    def attn_moves(h):
        src = attn.at[:, :, pl.ds(h * width, width)]
        return remote(src, att.at[c], asend.at[h], arecv.at[c], {"expert": 2 * z + h, "vocab": far})

    def attn_stays(h):
        src = attn.at[:, :, pl.ds(h * width, width)]
        return pltpu.make_async_copy(src, att.at[c], arecv.at[c])

    fetch_small[0].wait()
    fetch_small[1].wait()
    gate_of = gates[...].astype(jnp.float32)
    gate_share = gate_of / jnp.sum(gate_of, axis=0, keepdims=True)
    named = routes[...]
    expert_at = lax.broadcasted_iota(jnp.int32, (16, block), 0)
    spread = jnp.zeros((16, block), jnp.float32)
    for k in range(named.shape[0]):
        spread = spread + jnp.where(expert_at == named[k:k + 1, :], gate_share[k:k + 1, :], 0.0)
    sh_out[...] = spread
    own_rows = pl.ds(pl.multiple_of(me * 16, 16), 16)
    sh_in[own_rows, :] = sh_out[...]

    def share_move(d):
        return remote(sh_out, sh_in.at[own_rows], ssend.at[d], srecv.at[me],
                      {"expert": (me + d) % 8})

    tab[rows // GROUP] = jnp.zeros((GROUP, width), tab.dtype)
    r_at = lax.broadcasted_iota(jnp.int32, (GROUP, 128), 0)
    for r in range(GROUP):
        pick[r] = jnp.where(r_at == r, 1.0, 0.0).astype(pick.dtype)
    m_at = lax.broadcasted_iota(jnp.int32, (GROUP, GROUP * GROUP), 0)
    n_at = lax.broadcasted_iota(jnp.int32, (GROUP, GROUP * GROUP), 1)
    select[...] = jnp.where(n_at // GROUP == m_at, 1.0, 0.0).astype(select.dtype)
    all_here()
    for h in range(2):
        stays = (me == 2 * z + h) & (z == far)

        @pl.when(stays)
        def _():
            attn_stays(h).start()

        @pl.when(jnp.logical_not(stays))
        def _():
            attn_moves(h).start()

    for d in range(1, 8):
        share_move(d).start()

    for one in fetch_small[2:7] + fetch_table:
        one.wait()
    for one in fetch[1:]:
        one.start()

    base = z * rows

    def lookup(k):
        def one_side(qq, carry):
            for cc in range(4):
                tiles = []
                for j in range(GROUP):
                    loc = ids[(2 * cc + qq) * block + k * GROUP + j] - base
                    safe = jnp.minimum(jnp.maximum(loc, 0), rows - 1)
                    keep = (loc == safe) & (wm[safe] == 1)
                    tile = jnp.where(keep, jnp.right_shift(safe, 4), rows // GROUP)
                    r = jnp.bitwise_and(safe, 15)
                    src = tab[tile]
                    one = pick[r]
                    tiles.append(src * jnp.concatenate([one] * (width // 128), axis=1))
                stacked = jnp.concatenate(tiles, axis=0)
                got = jnp.dot(select[...], stacked, preferred_element_type=jnp.float32)
                part[k, qq, pl.ds(cc * GROUP, GROUP), :] = got.astype(part.dtype)
            return carry

        lax.fori_loop(0, 2, one_side, 0)

    CHAIN, RISE, XS, YS, SO, D0, D1, SX, SY, SD0, SD1 = 0, 2, 4, 5, 6, 7, 8, 9, 10, 11, 12

    def chain_move(src, k, qq, up):
        return remote(src, zin.at[up, k, qq], send.at[CHAIN + up, k, qq], recv.at[CHAIN + up, k, qq],
                      {"vocab": z - 1 + 2 * up})

    def chain_in(k, qq, up):
        chain_move(zin.at[up, k, qq], k, qq, up).wait_recv()

    def piece(slot, k, qq, lo=0, count=None):
        count = 2 * half if count is None else count
        return every.at[slot, k, qq, pl.ds(lo, count)]

    def to_peer(kind, ref, k, qq, peer):
        return remote(ref, ref, send.at[kind, k, qq], recv.at[kind, k, qq], peer)

    def rise_move(k, qq, up):
        return to_peer(RISE + up, piece(me, k, qq), k, qq, {"vocab": z - 1 + 2 * up})

    def spec_of(kind, k, qq):
        return {
            XS: lambda: (piece(me, k, qq), xn),
            YS: lambda: (piece(me, k, qq), yn),
            SO: lambda: (piece(me, k, qq), sib),
            D0: lambda: (piece(xn, k, qq, 0, half), yn),
            D1: lambda: (piece(yn, k, qq, half, half), xn),
            SX: lambda: (piece(xn, k, qq), sib),
            SY: lambda: (piece(yn, k, qq), sib),
            SD0: lambda: (piece(diag, k, qq, 0, half), sib),
            SD1: lambda: (piece(diag, k, qq, half, half), sib),
        }[kind]()

    def move(kind, k, qq):
        ref, peer = spec_of(kind, k, qq)
        return to_peer(kind, ref, k, qq, {"expert": peer})

    sib_of = {SO: sib, SX: xn + sib - me, SY: yn + sib - me}
    sib_diag = diag + sib - me

    def arrive(kind, ref, k, qq):
        to_peer(kind, ref, k, qq, {"expert": sib}).wait_recv()

    def spread_out(k, qq):
        for kind in (XS, YS, SO):
            move(kind, k, qq).start()

    def make_hidden(k):
        squares = jnp.zeros((4 * half, 1), jnp.float32)
        for slot in range(8):
            v = every[slot, k].reshape(4 * half, width).astype(jnp.float32)
            squares = squares + jnp.sum(v * v, axis=1, keepdims=True)
        inverse = lax.rsqrt(squares * (1.0 / (8 * width)) + 1e-06)
        for slot in range(8):
            columns = pl.ds(slot * width, width)
            v = every[slot, k].reshape(4 * half, width).astype(jnp.float32)
            xs[:, columns] = (v * inverse * post_gain[:, columns]).astype(xs.dtype)
        gate_val = jnp.dot(xs[...], wg[...], preferred_element_type=jnp.float32)
        up_val = jnp.dot(xs[...], wu[...], preferred_element_type=jnp.float32)
        scaled = gate_val / (1.0 + jnp.exp(-gate_val)) * up_val * share[k][:, 0:1]
        hidden = scaled.astype(xs.dtype)
        for j in range(8):
            down = tab[pl.ds(j * deep, deep)].reshape(deep * GROUP, width)
            made = jnp.dot(hidden, down, preferred_element_type=jnp.float32)
            upper, lower = made[0:2 * half], made[2 * half:4 * half]
            stay = jnp.where(core == 0, upper, lower).astype(total.dtype)
            leave = jnp.where(core == 0, lower, upper).astype(total.dtype)
            for cc in range(4):
                total[k, cc, j] = stay[cc * GROUP:(cc + 1) * GROUP]
                tab[down_at + k * 32 + j * 4 + cc] = leave[cc * GROUP:(cc + 1) * GROUP]

    def sharing():
        for d in range(1, 8):
            other = (me + d) % 8
            other_rows = pl.ds(pl.multiple_of(other * 16, 16), 16)
            remote(sh_out, sh_in.at[other_rows], ssend.at[d], srecv.at[other],
                   {"expert": other}).wait_recv()
        turned = sh_in[...].T
        mine = (me * n + z) // 2
        lane = lax.broadcasted_iota(jnp.int32, (block, 128), 1)
        for owner in range(8):
            column = jnp.sum(jnp.where(lane == owner * 16 + mine, turned, 0.0), axis=1, keepdims=True)
            column = jnp.broadcast_to(column, (block, 128))
            at = (owner % 2) * 2 * half + (owner // 2) * GROUP
            for k in range(chunks):
                share[k, pl.ds(at, GROUP), :] = column[k * GROUP:(k + 1) * GROUP, :]

    settle = CHAIN_LAG * (n // 2)
    long = n // 2
    keys_at = settle + KEY_START

    def key_out(k, qq, cc):
        return remote(emb.at[k, cc], kin.at[k, me], ksend.at[k, cc], krecv.at[k],
                      {"expert": 2 * cc + qq})

    def key_next(k, up):
        return remote(kin.at[k], kin.at[k], kfwd.at[k, up], krecv.at[k], {"vocab": z - 1 + 2 * up})

    def away_of(qq):
        offset = z - near - qq
        return jnp.maximum(offset, -offset)

    key_far = away_of(core)

    def outward(qq, run):
        for up in range(2):
            beyond = (z >= near + qq) & (z < n - 1) if up else (z <= near + qq) & (z > 0)

            @pl.when(beyond)
            def _():
                run(up)

    def inside(k):
        return (k >= 0) & (k < chunks)

    def make_keys():
        fetch[3].wait()
        squares = jnp.zeros((block, 1), jnp.float32)
        for slot in range(8):
            v = kin[:, slot].reshape(block, width).astype(jnp.float32)
            squares = squares + jnp.sum(v * v, axis=1, keepdims=True)
        inverse = lax.rsqrt(squares * (1.0 / (8 * width)) + 1e-06)
        raw = jnp.zeros((block, 128), jnp.float32)
        for slot in range(8):
            columns = pl.ds(slot * width, width)
            v = kin[:, slot].reshape(block, width).astype(jnp.float32)
            normed = (v * inverse * in_gain[:, columns]).astype(kw.dtype)
            raw = raw + jnp.dot(normed, kw[columns, :], preferred_element_type=jnp.float32)
        keys[...] = rms_rows(raw, key_gain[...]).astype(keys.dtype)

    def back(kind, src, dst, k, peer):
        return pltpu.make_async_remote_copy(
            src_ref=src, dst_ref=dst, send_sem=bsend.at[kind, k], recv_sem=brecv.at[kind, k],
            device_id=peer, device_id_type=MESH)

    left, right = pl.ds(0, 4), pl.ds(4, 4)

    def sib_move(k):
        return back(0, tab.at[leaving(k)], sib_in.at[k], k, {"expert": sib})

    def first_move(i, k):
        src, dst, peer = (
            lambda: (total.at[k, cd, left], x_in.at[k, 1], xn),
            lambda: (total.at[k, cd, right], y_in.at[k, 1], yn),
            lambda: (total.at[k, cx, left], x_in.at[k, 0], xn),
            lambda: (total.at[k, cy, right], y_in.at[k, 0], yn),
        )[i]()
        return back(1 + i, src, dst, k, {"expert": peer})

    def then_y(k):
        return back(5, total.at[k, cy, left], y_last.at[k], k, {"expert": yn})

    def then_x(k):
        return back(6, total.at[k, cx, right], x_last.at[k], k, {"expert": xn})

    per = 8 // n

    def z_move(d, k):
        peer = (z + d + 1) % n
        return back(7 + d, full.at[k, pl.ds(peer * per, per)], z_in.at[k, d], k, {"vocab": peer})

    def wide(value):
        return value.astype(jnp.float32)

    def add_cores(k):
        sib_move(k).wait_recv()
        for cc in range(4):
            for j in range(8):
                total[k, cc, j] = total[k, cc, j] + sib_in[k, j * 4 + cc]
        for i in range(4):
            first_move(i, k).start()

    def add_across(k):
        first_move(0, k).wait_recv()
        for j in range(4):
            total[k, cy, j] = total[k, cy, j] + x_in[k, 1, j]
        then_y(k).start()
        first_move(1, k).wait_recv()
        for j in range(4):
            total[k, cx, 4 + j] = total[k, cx, 4 + j] + y_in[k, 1, j]
        then_x(k).start()

    def add_last(k):
        first_move(2, k).wait_recv()
        then_y(k).wait_recv()
        for j in range(4):
            term = wide(total[k, c, j]) + wide(x_in[k, 0, j]) + wide(y_last[k, j])
            full[k, j] = term.astype(full.dtype)
        first_move(3, k).wait_recv()
        then_x(k).wait_recv()
        for j in range(4):
            term = wide(total[k, c, 4 + j]) + wide(y_in[k, 0, j]) + wide(x_last[k, j])
            full[k, 4 + j] = term.astype(full.dtype)
        for d in range(n - 1):
            z_move(d, k).start()

    def add_planes(k):
        for d in range(n - 1):
            z_move(d, k).wait_recv()
        for j in range(per):
            term = wide(full[k, z * per + j])
            for d in range(n - 1):
                term = term + wide(z_in[k, d, j])
            out[k, :, pl.ds(j * width, width)] = term.astype(out.dtype)

    def drain_front(k):
        for qq in range(2):
            for up in range(2):
                @pl.when(z == (0 if up else n - 1))
                def _():
                    chain_move(part.at[k, qq], k, qq, up).wait_send()

            @pl.when(z == near + 1 - qq)
            def _():
                chain_move(part.at[k, qq], k, qq, qq).wait_send()

            outward(qq, lambda up: rise_move(k, qq, up).wait_send())
            for kind in range(XS, SD1 + 1):
                move(kind, k, qq).wait_send()

            @pl.when(away_of(qq) == 0)
            def _():
                for cc in range(4):
                    @pl.when(me != 2 * cc + qq)
                    def _():
                        key_out(k, qq, cc).wait_send()

    def drain_early():
        for d in range(1, 8):
            share_move(d).wait_send()
        for h in range(2):
            @pl.when(jnp.logical_not((me == 2 * z + h) & (z == far)))
            def _():
                attn_moves(h).wait_send()

    def drain_back(k):
        outward(core, lambda up: key_next(k, up).wait_send())
        sib_move(k).wait_send()
        for i in range(4):
            first_move(i, k).wait_send()
        then_x(k).wait_send()
        then_y(k).wait_send()
        for d in range(n - 1):
            z_move(d, k).wait_send()

    def step(s, carry):
        @pl.when(s < chunks)
        def _():
            lookup(s)

        for qq in range(2):
            away = away_of(qq)
            ends = (z == 0) | (z == n - 1)
            relay = (away == 1) & jnp.logical_not(ends)

            for up in range(2):
                @pl.when((s < chunks) & (z == (0 if up else n - 1)))
                def _():
                    chain_move(part.at[s, qq], s, qq, up).start()

            k = s - CHAIN_LAG

            @pl.when(inside(k) & relay)
            def _():
                chain_in(k, qq, qq)
                zin[qq, k, qq] = zin[qq, k, qq] + part[k, qq]
                chain_move(zin.at[qq, k, qq], k, qq, qq).start()

            k1 = s - settle

            @pl.when(inside(k1) & (away == 0))
            def _():
                @pl.when(k1 == 0)
                def _():
                    for cc in range(4):
                        pltpu.make_async_copy(att.at[cc], att.at[cc], arecv.at[cc]).wait()

                chain_in(k1, qq, 1 - qq)
                chain_in(k1, qq, qq)
                for cc in range(4):
                    some = pl.ds(cc * GROUP, GROUP)
                    whole = zin[0, k1, qq, some, :] + zin[1, k1, qq, some, :] + part[k1, qq, some, :]
                    emb[k1, cc] = whole
                    mid = whole.astype(jnp.float32) + att[cc, k1].astype(jnp.float32)
                    every[me, k1, qq, some, :] = mid.astype(every.dtype)
                outward(qq, lambda up: rise_move(k1, qq, up).start())
                spread_out(k1, qq)

        for qq in range(2):
            away = away_of(qq)
            k2 = s - settle - RISE_LAG * away

            @pl.when(inside(k2) & (away > 0))
            def _():
                for up in range(2):
                    @pl.when((z > near + qq) if up else (z < near + qq))
                    def _():
                        rise_move(k2, qq, up).wait_recv()

                outward(qq, lambda up: rise_move(k2, qq, up).start())
                spread_out(k2, qq)

        for qq in range(2):
            away = away_of(qq)
            k2 = s - settle - RISE_LAG * away
            k3 = k2 - CROSS_LAG

            @pl.when(inside(k3))
            def _():
                arrive(XS, piece(xn, k3, qq), k3, qq)
                move(D0, k3, qq).start()
                move(SX, k3, qq).start()
                arrive(YS, piece(yn, k3, qq), k3, qq)
                move(D1, k3, qq).start()
                move(SY, k3, qq).start()

        for qq in range(2):
            away = away_of(qq)
            k2 = s - settle - RISE_LAG * away
            k3 = k2 - CROSS_LAG
            k4 = k3 - DIAG_LAG

            @pl.when(inside(k4))
            def _():
                arrive(D0, piece(diag, k4, qq, 0, half), k4, qq)
                move(SD0, k4, qq).start()
                arrive(D1, piece(diag, k4, qq, half, half), k4, qq)
                move(SD1, k4, qq).start()

        for qq in range(2):
            away = away_of(qq)
            k2 = s - settle - RISE_LAG * away
            k3 = k2 - CROSS_LAG
            k4 = k3 - DIAG_LAG
            k5 = k4 - SIB_LAG

            @pl.when(inside(k5))
            def _():
                for kind, slot in sib_of.items():
                    arrive(kind, piece(slot, k5, qq), k5, qq)
                arrive(SD0, piece(sib_diag, k5, qq, 0, half), k5, qq)
                arrive(SD1, piece(sib_diag, k5, qq, half, half), k5, qq)

        for qq in range(2):
            away = away_of(qq)
            k7 = s - keys_at

            @pl.when(inside(k7) & (away == 0))
            def _():
                for cc in range(4):
                    stays = me == 2 * cc + qq

                    @pl.when(stays)
                    def _():
                        pltpu.make_async_copy(emb.at[k7, cc], kin.at[k7, me], krecv.at[k7]).start()

                    @pl.when(jnp.logical_not(stays))
                    def _():
                        key_out(k7, qq, cc).start()

        k8 = s - keys_at - KEY_LAG * (1 + key_far)

        @pl.when(inside(k8))
        def _():
            pltpu.make_async_copy(kin.at[k8], kin.at[k8], krecv.at[k8]).wait()

            outward(core, lambda up: key_next(k8, up).start())

        k6 = s - settle - RISE_LAG * jnp.maximum(away_of(0), away_of(1)) - CROSS_LAG - DIAG_LAG - SIB_LAG

        @pl.when(s == chunks)
        def _():
            for j in range(8):
                fetch_down(j).start()

        k10 = k6 - HALF_LAG
        k11 = k10 - ADD_LAG
        k12 = k11 - LAST_LAG
        k13 = k12 - OUT_LAG

        for k, stage in ((k10, add_cores), (k11, add_across), (k12, add_last), (k13, add_planes),
                         (k12, drain_front), (k13 - 1, drain_back)):
            @pl.when(inside(k))
            def _():
                stage(k)

        @pl.when(k6 == 0)
        def _():
            fetch[1].wait()
            fetch[2].wait()
            for j in range(8):
                fetch_down(j).wait()
            sharing()

        @pl.when(inside(k6))
        def _():
            make_hidden(k6)
            sib_move(k6).start()

        @pl.when(s == keys_at + KEY_LAG * (1 + long) + chunks - 1)
        def _():
            make_keys()
            drain_early()

        return carry

    steps = max(settle + RISE_LAG * long + CROSS_LAG + DIAG_LAG + SIB_LAG
                + HALF_LAG + ADD_LAG + LAST_LAG + OUT_LAG + chunks + 1,
                keys_at + KEY_LAG * (1 + long) + chunks)
    lax.fori_loop(0, steps, step, 0)


def hand_over(out, keys):
    def kernel(out_in, keys_in, out_ref, keys_ref):
        out_ref[...] = out_in[...]
        keys_ref[...] = keys_in[...]

    vmem = pl.BlockSpec(memory_space=pltpu.VMEM)
    return pl.pallas_call(
        kernel,
        name="hand_over",
        out_shape=tuple(jax.ShapeDtypeStruct(r.shape, r.dtype) for r in (out, keys)),
        in_specs=[vmem, vmem],
        out_specs=(vmem, vmem),
    )(out, keys)


def layer(n, token_ids, word_mask, embed_table, attn_out, in_gain, key_weight, key_gain, post_gain,
          routes, gate_ints, w_gate, w_up, w_down):
    block, columns = attn_out.shape
    rows, width = embed_table.shape
    chunks = block // GROUP
    side = 4 * GROUP
    units = w_gate.shape[1]
    model = 8 * width
    kind = embed_table.dtype
    vmem, anyw = (pl.BlockSpec(memory_space=m) for m in (pltpu.VMEM, pl.ANY))
    dma = pltpu.SemaphoreType.DMA
    tiles = max(rows // GROUP + 1, 8 * units // GROUP + 32 * chunks)
    out, keys = pl.pallas_call(
        lambda *refs: layer_kernel(n, *refs),
        name="embed_and_experts",
        out_shape=(
            jax.ShapeDtypeStruct((chunks, GROUP, model // n), kind),
            jax.ShapeDtypeStruct((block, 128), kind),
        ),
        in_specs=[anyw] * 13,
        out_specs=(vmem, vmem),
        scratch_shapes=[
            pltpu.SMEM(token_ids.shape, token_ids.dtype),
            pltpu.VMEM((1, model), jnp.float32),
            pltpu.VMEM((1, 128), jnp.float32),
            pltpu.VMEM((1, model), jnp.float32),
            pltpu.VMEM((8, block), routes.dtype),
            pltpu.VMEM((8, block), gate_ints.dtype),
            pltpu.SMEM(word_mask.shape, word_mask.dtype),
            pltpu.VMEM((tiles, GROUP, width), kind),
            pltpu.VMEM(w_gate.shape, kind),
            pltpu.VMEM(w_up.shape, kind),
            pltpu.VMEM(key_weight.shape, kind),
            pltpu.VMEM((chunks, 2, side, width), kind),
            pltpu.VMEM((2, chunks, 2, side, width), kind),
            pltpu.VMEM((8, chunks, 2, side, width), kind),
            pltpu.VMEM((4, chunks, GROUP, width), kind),
            pltpu.VMEM((chunks, 4, GROUP, width), kind),
            pltpu.VMEM((chunks, 8, GROUP, width), kind),
            pltpu.VMEM((GROUP, GROUP, 128), kind),
            pltpu.VMEM((GROUP, GROUP * GROUP), kind),
            pltpu.VMEM((2 * side, model), kind),
            pltpu.VMEM((16, block), jnp.float32),
            pltpu.VMEM((128, block), jnp.float32),
            pltpu.VMEM((chunks, 2 * side, 128), jnp.float32),
            dma((13, chunks, 2)),
            dma((13, chunks, 2)),
            dma((chunks, 4)),
            dma((chunks,)),
            dma((chunks, 2)),
            dma((8,)),
            dma((8,)),
            dma((2,)),
            dma((4,)),
            pltpu.VMEM((chunks, 32, GROUP, width), kind),
            pltpu.VMEM((chunks, 4, 8, GROUP, width), kind),
            pltpu.VMEM((chunks, 2, 4, GROUP, width), kind),
            pltpu.VMEM((chunks, 2, 4, GROUP, width), kind),
            pltpu.VMEM((chunks, 4, GROUP, width), kind),
            pltpu.VMEM((chunks, 4, GROUP, width), kind),
            pltpu.VMEM((chunks, 8, GROUP, width), kind),
            pltpu.VMEM((chunks, n - 1, 8 // n, GROUP, width), kind),
            dma((6 + n, chunks)),
            dma((6 + n, chunks)),
            dma((8 + TABLE_CUTS,)),
            dma((13,)),
        ],
        compiler_params=pltpu.CompilerParams(
            collective_id=0, has_side_effects=True, vmem_limit_bytes=63 * 1024 * 1024),
    )(token_ids, word_mask, embed_table.reshape(rows // GROUP, GROUP, width), attn_out.reshape(chunks, GROUP, columns),
      in_gain.reshape(1, -1), key_weight, key_gain.reshape(1, -1), post_gain.reshape(1, -1),
      routes.T, gate_ints.T, w_gate, w_up, w_down.reshape(units // GROUP, GROUP, model))
    return hand_over(out.reshape(block, model // n), keys)


def by_collectives(
    token_ids, word_mask, embed_table, attn_out, in_gain, key_weight, key_gain, post_gain,
    routes, gate_ints, w_gate, w_up, w_down,
):
    n_vocab = lax.axis_size("vocab")
    n_expert = lax.axis_size("expert")
    vocab_rows = embed_table.shape[0]
    experts_total = n_expert * n_vocab // 2
    my_vocab = lax.axis_index("vocab")
    my_expert = (lax.axis_index("expert") * n_vocab + my_vocab) // 2

    gate_share = gate_ints.astype(jnp.float32) / jnp.sum(gate_ints, axis=1, keepdims=True).astype(
        jnp.float32
    )
    onehot = routes[:, :, None] == jnp.arange(experts_total, dtype=jnp.int32)[None, None, :]
    share_of = jnp.sum(jnp.where(onehot, gate_share[:, :, None], 0.0), axis=1)
    all_shares = lax.all_gather(share_of, "expert", axis=0, tiled=True)
    my_share = lax.dynamic_slice_in_dim(all_shares, my_expert, 1, axis=1)

    own_rows = attn_out.shape[0] // n_vocab
    attn_blocks = attn_out.reshape(n_vocab, own_rows, attn_out.shape[1])
    kept = lax.dynamic_index_in_dim(attn_blocks, my_vocab, 0, keepdims=True)
    attn_parts = lax.dynamic_update_slice_in_dim(attn_blocks, kept, my_vocab, 0)
    for d in range(1, n_vocab):
        sent = lax.dynamic_index_in_dim(attn_blocks, (my_vocab + d) % n_vocab, 0, keepdims=True)
        came = lax.ppermute(sent, "vocab", [(i, (i + d) % n_vocab) for i in range(n_vocab)])
        attn_parts = lax.dynamic_update_slice_in_dim(
            attn_parts, came, (my_vocab - d + n_vocab) % n_vocab, 0
        )
    attn_rows = attn_parts.transpose(1, 0, 2).reshape(own_rows, -1)

    ids = token_ids.reshape(n_expert, n_vocab, own_rows).transpose(1, 0, 2).reshape(-1)
    local_ids = ids - my_vocab * vocab_rows
    inside = (local_ids >= 0) & (local_ids < vocab_rows)
    safe_ids = jnp.clip(local_ids, 0, vocab_rows - 1)
    keep_row = inside & (word_mask[safe_ids] == 1)
    partial_value = jnp.where(
        keep_row[:, None], embed_table[safe_ids], jnp.zeros_like(embed_table[:1])
    )
    summed = lax.psum_scatter(partial_value, "vocab", scatter_dimension=0, tiled=True)
    rows = lax.all_to_all(summed, "expert", split_axis=0, concat_axis=1, tiled=True)
    rows = rows.astype(jnp.float32)

    mid_rows = (rows + attn_rows.astype(jnp.float32)).astype(jnp.bfloat16)
    expert_in = rms_rows(mid_rows.astype(jnp.float32), post_gain).astype(jnp.bfloat16)
    normed_rows = rms_rows(rows, in_gain).astype(jnp.bfloat16)
    tokens_in = lax.all_gather(expert_in, ("expert", "vocab"), axis=0, tiled=True)
    key_rows = lax.all_gather(normed_rows, "vocab", axis=0, tiled=True)
    raw_keys = jnp.dot(key_rows, key_weight, preferred_element_type=jnp.float32)
    key_heads = rms_rows(raw_keys, key_gain).astype(jnp.bfloat16)

    gate_val = jnp.dot(tokens_in, w_gate[0], preferred_element_type=jnp.float32)
    up_val = jnp.dot(tokens_in, w_up[0], preferred_element_type=jnp.float32)
    hidden = (jax.nn.silu(gate_val) * up_val).astype(jnp.bfloat16)
    parts = jnp.dot(hidden, w_down[0], preferred_element_type=jnp.float32)
    weighted = (parts * my_share).astype(jnp.bfloat16)
    by_tokens = lax.psum_scatter(weighted, "expert", scatter_dimension=0, tiled=True)
    expert_out = lax.psum_scatter(by_tokens, "vocab", scatter_dimension=1, tiled=True)
    return (expert_out, key_heads)


def by_kernels(
    token_ids, word_mask, embed_table, attn_out, in_gain, key_weight, key_gain, post_gain,
    routes, gate_ints, w_gate, w_up, w_down,
):
    return layer(
        lax.axis_size("vocab"), token_ids, word_mask, embed_table, attn_out, in_gain, key_weight,
        key_gain, post_gain, routes, gate_ints, w_gate[0], w_up[0], w_down[0])


def solution(mesh):
    small = mesh.shape["expert"] == 8 and mesh.shape["vocab"] == 4
    return jax.shard_map(
        by_kernels if small else by_collectives,
        mesh=mesh,
        in_specs=(
            P(),
            P("vocab"),
            P("vocab", "expert"),
            P("expert", "vocab"),
            P(),
            P(None, "vocab"),
            P(),
            P(),
            P("expert", None),
            P("expert", None),
            P(("expert", "vocab"), None, None),
            P(("expert", "vocab"), None, None),
            P(("expert", "vocab"), None, None),
        ),
        out_specs=(P("expert", "vocab"), P("expert", "vocab")),
        check_vma=False,
    )
```
